32 devices in a mesh: dp: 2 (over x), fsdp: 16 (over z, y, core).
Axes of the slice: x: 2, y: 2, z: 4, core: 2. Of those that a mesh axis runs over, the one named last changes fastest.
Arguments:
- inputs: bfloat16 [32, 788, 768], P(('dp', 'fsdp')), may hold values from -6 to 6
- cotangent: bfloat16 [32, 788, 768], P(('dp', 'fsdp')), may hold values from -6 to 6
- segment_ids: int32 [32, 788], P(('dp', 'fsdp')), may hold values from 0 to 3, as said below
- keep_rows: int32 [32, 788], P(('dp', 'fsdp')), may hold values from 0 to 1, as said below
- index_map: int32 [197, 197], replicated, may hold values from 0 to 731
- ln1_gain: bfloat16 [768], P(('dp', 'fsdp')), may hold values from 0.5 to 1.5
- ln1_bias: bfloat16 [768], P(('dp', 'fsdp')), may hold values from -3 to 3
- qkv_weight: bfloat16 [768, 2304], P(('dp', 'fsdp')), may hold values from -0.21875 to 0.21875
- qv_bias: bfloat16 [2, 768], P(None, ('dp', 'fsdp')), may hold values from -3 to 3
- out_weight: bfloat16 [768, 768], P(None, ('dp', 'fsdp')), may hold values from -1.75 to 1.75
- out_bias: bfloat16 [768], P(('dp', 'fsdp')), may hold values from -2 to 2
- gamma_attn: bfloat16 [768], P(('dp', 'fsdp')), may hold values from 0.5 to 2
- rel_table: bfloat16 [12, 736], P(None, ('dp', 'fsdp')), may hold values from -4 to 4
- ln2_gain: bfloat16 [768], P(('dp', 'fsdp')), may hold values from 0.5 to 1.5
- ln2_bias: bfloat16 [768], P(('dp', 'fsdp')), may hold values from -3 to 3
- fc1_weight: bfloat16 [768, 3072], P(('dp', 'fsdp')), may hold values from -0.21875 to 0.21875
- fc1_bias: bfloat16 [3072], P(('dp', 'fsdp')), may hold values from -3 to 3
- fc2_weight: bfloat16 [3072, 768], P(None, ('dp', 'fsdp')), may hold values from -0.109375 to 0.109375
- fc2_bias: bfloat16 [768], P(('dp', 'fsdp')), may hold values from -2 to 2
- gamma_mlp: bfloat16 [768], P(('dp', 'fsdp')), may hold values from 0.5 to 2
Outputs:
- output: bfloat16 [32, 788, 768], P(('dp', 'fsdp'))
- input_grad: bfloat16 [32, 788, 768], P(('dp', 'fsdp'))
- grad_ln1_gain: float32 [768], P(('dp', 'fsdp'))
- grad_ln1_bias: float32 [768], P(('dp', 'fsdp'))
- grad_qkv_weight: float32 [768, 2304], P(('dp', 'fsdp'))
- grad_qv_bias: float32 [2, 768], P(None, ('dp', 'fsdp'))
- grad_out_weight: float32 [768, 768], P(None, ('dp', 'fsdp'))
- output_bias_gradient: float32 [768], P(('dp', 'fsdp'))
- grad_gamma_attn: float32 [768], P(('dp', 'fsdp'))
- grad_rel_table: float32 [12, 736], P(None, ('dp', 'fsdp'))
- grad_ln2_gain: float32 [768], P(('dp', 'fsdp'))
- grad_ln2_bias: float32 [768], P(('dp', 'fsdp'))
- grad_fc1_weight: float32 [768, 3072], P(('dp', 'fsdp'))
- grad_fc1_bias: float32 [3072], P(('dp', 'fsdp'))
- grad_fc2_weight: float32 [3072, 768], P(None, ('dp', 'fsdp'))
- grad_fc2_bias: float32 [768], P(('dp', 'fsdp'))
- grad_gamma_mlp: float32 [768], P(('dp', 'fsdp'))
The draws below stay inside these ranges and needn't reach their ends.
Inputs may be any that keep to these rules, and one draw needn't show every extreme that they name: `segment_ids`: each sequence is either 4 runs of 197 rows with segment numbers 0 to 3 in order, or 3 such runs numbered 0 to 2 that follow a run of padding rows and precede another (197 padding rows in all, either run possibly empty); padding rows have segment number 4 - 1. `keep_rows`: 0 exactly on the padding rows described for segment_ids.
All inputs are finite; a program needn't handle non-finite values.
Results may differ from the reference program's by a relative error of at most 0.011.
Values may be sent and summed in bfloat16 or wider, within the bound.
No kernel may reach another device: no remote copies, remote signals or barrier semaphores. Data moves between devices by JAX's collectives and lax.ppermute only.
A program may use at most 128 MiB of HBM per device.

```python
import math
import jax
import jax.numpy as jnp
from jax import lax

D = 768
HEADS = 12
FF = 3072
IMG_TOK = 197
IMGS = 4
REL = 732
SEQ_LEN = 788
SEQS = 32
REL_PAD = 736


def image_layout(key):
    layout_key = jax.random.fold_in(key, 7)
    count_key, offset_key = jax.random.split(layout_key)
    three_images = jax.random.randint(count_key, (SEQS,), 0, 4) == 0
    front_pad = jax.random.randint(offset_key, (SEQS,), 0, IMG_TOK + 1)
    row_ids = jnp.arange(SEQ_LEN, dtype=jnp.int32)
    shifted = row_ids[None, :] - front_pad[:, None]
    inside = (shifted >= 0) & (shifted < (IMGS - 1) * IMG_TOK)
    short_labels = jnp.where(inside, shifted // IMG_TOK, IMGS - 1)
    full_labels = jnp.broadcast_to(row_ids // IMG_TOK, (SEQS, SEQ_LEN))
    segments = jnp.where(three_images[:, None], short_labels, full_labels).astype(jnp.int32)
    kept_flags = jnp.where(three_images[:, None], inside, True).astype(jnp.int32)
    return (segments, kept_flags)


def draw_segment_ids(key, part):
    return image_layout(key)[0]


def draw_keep_rows(key, part):
    return image_layout(key)[1]


def place_ends(values, stream_key, least, largest):
    longest = values.shape.index(max(values.shape))
    spots = []
    for shift in (0, 1):
        where = [jax.random.randint(jax.random.fold_in(stream_key, axis), (), 0, length) for axis, length in enumerate(values.shape)]
        where[longest] = (where[longest] + shift) % values.shape[longest]
        spots.append(tuple(where))
    return values.at[spots[0]].set(least).at[spots[1]].set(largest)


def spiked(drawn, stream_key, source, target, parts, factor):
    owner, partner = [(jnp.arange(drawn.shape[axis_at]) // (drawn.shape[axis_at] // parts)).reshape([-1 if axis == axis_at else 1 for axis in range(drawn.ndim)]) for axis_at in (source, target)]
    chosen = jax.random.permutation(stream_key, parts)[partner]
    strong = (owner == chosen) | (owner == (partner + parts // 2) % parts)
    return jnp.where(strong, factor * drawn, drawn)


def levels(key, extent, cuts, smallest, high):
    level = 1.0
    for position, shards_of in cuts:
        steps = jax.random.uniform(jax.random.fold_in(jax.random.fold_in(key, 6), position), (shards_of,), jnp.float32, smallest / len(cuts), high / len(cuts))
        level = level * jnp.repeat(jnp.exp(steps), extent[position] // shards_of).reshape((-1,) + (1,) * (len(extent) - 1 - position))
    return level


def noise(stream_key, extent, width, limit, cuts=(), kind=jnp.bfloat16):
    values = width * jax.random.normal(stream_key, extent, jnp.float32)
    if cuts:
        values = values * levels(stream_key, extent, cuts, -0.22, 0.18)
    return jnp.clip(values, -limit, limit).astype(kind)


def gaussian_with(rng, shape, width, most, cuts, heavy, kind=jnp.bfloat16):
    array = width * jax.random.normal(rng, shape, jnp.float32)
    if cuts:
        array = array * levels(rng, shape, cuts, -0.22, 0.18)
    return jnp.clip(spiked(array, jax.random.fold_in(rng, 3), *heavy), -most, most).astype(kind)


def setup_inputs(seed: int = 0) -> dict:
    key_list = jax.random.split(jax.random.key(seed), 21)
    inputs = noise(key_list[0], (SEQS, SEQ_LEN, D), 1.0, 6.0, ((0, 32),))
    cotangent = gaussian_with(key_list[1], (SEQS, SEQ_LEN, D), 1.0, 6.0, ((0, 32),), (0, 2, 32, 2.75))
    segment_ids = draw_segment_ids(jax.random.fold_in(key_list[20], 71), 0)
    keep_rows = draw_keep_rows(jax.random.fold_in(key_list[20], 71), 0)
    index_map = place_ends(jax.random.randint(key_list[4], (IMG_TOK, IMG_TOK), 0, REL), jax.random.fold_in(key_list[4], 1), 0, REL - 1).astype(jnp.int32)
    ln1_gain = jnp.clip(1.0 + 0.1 * jax.random.normal(key_list[5], (D,), jnp.float32), 0.5, 1.5).astype(jnp.bfloat16)
    ln1_bias = noise(key_list[6], (D,), 0.5, 3.0, ((0, 32),))
    qkv_weight = noise(key_list[7], (D, 3 * D), D ** -0.5, 0.21875, ((0, 32),))
    qv_bias = noise(key_list[8], (2, D), 0.5, 3.0, ((1, 32),))
    out_weight = noise(key_list[9], (D, D), (D // 64) ** -0.5, 1.75, ((1, 32),))
    out_bias = noise(key_list[10], (D,), 0.3, 2.0, ((0, 32),))
    gamma_attn = jnp.clip(jnp.exp(math.log(2.0) - 1.3862944 * jax.random.uniform(key_list[11], (D,), jnp.float32) ** levels(key_list[11], (D,), ((0, 32),), -0.2, 0.2)), 0.5, 2.0).astype(jnp.bfloat16)
    rel_table = noise(key_list[12], (HEADS, REL_PAD), 1.0, 4.0, ((1, 32),))
    ln2_gain = jnp.clip(1.0 + 0.1 * jax.random.normal(key_list[13], (D,), jnp.float32), 0.5, 1.5).astype(jnp.bfloat16)
    ln2_bias = noise(key_list[14], (D,), 0.5, 3.0, ((0, 32),))
    fc1_weight = noise(key_list[15], (D, FF), D ** -0.5, 0.21875, ((0, 32),))
    fc1_bias = noise(key_list[16], (FF,), 0.5, 3.0, ((0, 32),))
    fc2_weight = noise(key_list[17], (FF, D), FF ** -0.5, 0.109375, ((1, 32),))
    fc2_bias = noise(key_list[18], (D,), 0.3, 2.0, ((0, 32),))
    gamma_mlp = jnp.clip(jnp.exp(math.log(2.0) - 1.3862944 * jax.random.uniform(key_list[19], (D,), jnp.float32) ** levels(key_list[19], (D,), ((0, 32),), -0.2, 0.2)), 0.5, 2.0).astype(jnp.bfloat16)
    return {"inputs": inputs, "cotangent": cotangent, "segment_ids": segment_ids, "keep_rows": keep_rows, "index_map": index_map, "ln1_gain": ln1_gain, "ln1_bias": ln1_bias, "qkv_weight": qkv_weight, "qv_bias": qv_bias, "out_weight": out_weight, "out_bias": out_bias, "gamma_attn": gamma_attn, "rel_table": rel_table, "ln2_gain": ln2_gain, "ln2_bias": ln2_bias, "fc1_weight": fc1_weight, "fc1_bias": fc1_bias, "fc2_weight": fc2_weight, "fc2_bias": fc2_bias, "gamma_mlp": gamma_mlp}


epsilon = 1e-06
masked_score = -1e+30
highest = lax.Precision.HIGHEST

@jax.custom_vjp
def low(v):
    return lax.optimization_barrier(v.astype(jnp.bfloat16)).astype(jnp.float32)

@jax.custom_vjp
def low_back(v):
    return v

def low_keep(v):
    return (low(v), None)

def low_pass(kept, grad):
    return (grad,)

def back_keep(v):
    return (v, None)

def back_low(kept, grad):
    return (low(grad),)
low.defvjp(low_keep, low_pass)
low_back.defvjp(back_keep, back_low)

def normalize(values, norm_gain, norm_shift):
    average = lax.optimization_barrier(jnp.mean(values, axis=-1, keepdims=True))
    centred = values - average
    spread = lax.optimization_barrier(jnp.mean(centred * centred, axis=-1, keepdims=True))
    return centred * lax.rsqrt(spread + epsilon) * norm_gain + norm_shift

def layout(segment_row, keep_row):
    length = segment_row.shape[0]
    row_ids = jnp.arange(length, dtype=jnp.int32)
    labels = jnp.arange(IMGS, dtype=jnp.int32)
    in_label = segment_row[None, :] == labels[:, None]
    kept_rows = keep_row == 1
    first_row = lax.optimization_barrier(jnp.min(jnp.where(in_label & kept_rows[None, :], row_ids[None, :], length), axis=1)).astype(jnp.int32)
    row_start = lax.optimization_barrier(jnp.max(jnp.where(in_label, first_row[:, None], 0), axis=0)).astype(jnp.int32)
    positions = jnp.where(kept_rows, row_ids - row_start, 0).astype(jnp.int32)
    same_image = segment_row[:, None] == segment_row[None, :]
    both_kept = same_image & kept_rows[:, None] & kept_rows[None, :]
    allowed = same_image & kept_rows[None, :] | (row_ids[:, None] == row_ids[None, :])
    return (positions, both_kept, allowed)

def project(values, weight):
    return jnp.einsum('gld,de->gle', values, weight, precision=highest)

def layer(group_in, params, index_map, positions, both_kept, allowed):
    ln1_gain, ln1_bias, qkv_weight, qv_bias, out_weight, out_bias, gamma_attn, rel_table, ln2_gain, ln2_bias, fc1_weight, fc1_bias, fc2_weight, fc2_bias, gamma_mlp = params
    group_size, length, model_width = group_in.shape
    head_count = rel_table.shape[0]
    head_dim = model_width // head_count
    first_low = low(normalize(group_in, ln1_gain, ln1_bias))
    full_bias = jnp.concatenate([qv_bias[0], jnp.zeros((model_width,), jnp.float32), qv_bias[1]])
    packed = low(low_back(project(first_low, qkv_weight) + full_bias))
    queries = packed[..., :model_width].reshape(group_size, length, head_count, head_dim)
    key_rows = packed[..., model_width:2 * model_width].reshape(group_size, length, head_count, head_dim)
    value_rows = packed[..., 2 * model_width:].reshape(group_size, length, head_count, head_dim)
    scores = jnp.einsum('gqhd,gkhd->ghqk', queries, key_rows, precision=highest) * head_dim ** (-0.5)
    image_table = jnp.take(rel_table, index_map, axis=1)
    table_fetch = jax.vmap(lambda place_ids: jnp.take(jnp.take(image_table, place_ids, axis=1), place_ids, axis=2))(positions)
    scores = low_back(scores + jnp.where(both_kept[:, None], table_fetch, 0.0))
    scores = jnp.where(allowed[:, None], scores, masked_score)
    row_max = lax.optimization_barrier(jnp.max(scores, axis=-1, keepdims=True))
    raised = jnp.exp(scores - row_max)
    attention = raised / lax.optimization_barrier(jnp.sum(raised, axis=-1, keepdims=True))
    mixed = jnp.einsum('ghqk,gkhd->gqhd', low(attention), value_rows, precision=highest)
    mixed = low(low_back(mixed.reshape(group_size, length, model_width)))
    attn_branch = low_back(project(mixed, out_weight) + out_bias)
    after_attn = group_in + gamma_attn * attn_branch
    second_low = low(normalize(after_attn, ln2_gain, ln2_bias))
    hidden_pre = low_back(project(second_low, fc1_weight) + fc1_bias)
    hidden_low = low(jax.nn.gelu(hidden_pre, approximate=False))
    feedforward_branch = low_back(project(hidden_low, fc2_weight) + fc2_bias)
    return after_attn + gamma_mlp * feedforward_branch

def reference(inputs, cotangent, segment_ids, keep_rows, index_map, ln1_gain, ln1_bias, qkv_weight, qv_bias, out_weight, out_bias, gamma_attn, rel_table, ln2_gain, ln2_bias, fc1_weight, fc1_bias, fc2_weight, fc2_bias, gamma_mlp):
    params = tuple((member.astype(jnp.float32) for member in (ln1_gain, ln1_bias, qkv_weight, qv_bias, out_weight, out_bias, gamma_attn, rel_table, ln2_gain, ln2_bias, fc1_weight, fc1_bias, fc2_weight, fc2_bias, gamma_mlp)))
    group_count = SEQS // 4
    stacked_in = inputs.astype(jnp.float32).reshape(group_count, 4, SEQ_LEN, D)
    stacked_cot = cotangent.astype(jnp.float32).reshape(group_count, 4, SEQ_LEN, D)
    stacked_seg = segment_ids.reshape(group_count, 4, SEQ_LEN)
    stacked_keep = keep_rows.reshape(group_count, 4, SEQ_LEN)

    def group_step(totals, batch):
        group_in, group_cot, group_seg, group_keep = batch
        positions, both_kept, allowed = jax.vmap(layout)(group_seg, group_keep)

        def forward(values, weights):
            return layer(values, weights, index_map, positions, both_kept, allowed)
        result, pullback = jax.vjp(forward, group_in, params)
        group_grad, param_grads = pullback(group_cot)
        return (jax.tree.map(jnp.add, totals, param_grads), (result, group_grad))
    start_totals = jax.tree.map(jnp.zeros_like, params)
    totals, (results, input_grads) = lax.scan(group_step, start_totals, (stacked_in, stacked_cot, stacked_seg, stacked_keep))
    output = results.reshape(SEQS, SEQ_LEN, D).astype(jnp.bfloat16)
    input_grad = input_grads.reshape(SEQS, SEQ_LEN, D).astype(jnp.bfloat16)
    return (output, input_grad, totals[0], totals[1], totals[2], totals[3], totals[4], totals[5], totals[6], totals[7], totals[8], totals[9], totals[10], totals[11], totals[12], totals[13], totals[14])
```

```python
import functools
import jax
import jax.numpy as jnp
from jax import lax
from jax.experimental import pallas as pl
from jax.experimental.pallas import tpu as pltpu
from jax.sharding import PartitionSpec as P

AX = ("dp", "fsdp")
IMGS = 4
EPS = 1e-06
MASKED = -1e30
ROOT_HALF = 0.7071067811865476
INV_ROOT_TAU = 0.3989422804014327
F32 = jnp.float32
BF16 = jnp.bfloat16
VMEM_LIMIT = 60 * 1024 * 1024

LN1_G, LN1_B, Q_B, V_B, OUT_B, GAM_A, LN2_G, LN2_B, FC2_B, GAM_M = range(10)
FC1_B = 16
TABLE = 32
SMALL = 128
G_LN1_G, G_LN1_B, G_Q_B, G_V_B, G_OUT_B, G_GAM_A, G_LN2_G, G_LN2_B, G_FC2_B, G_GAM_M = range(10)


def nn(a, b):
    return lax.dot_general(a, b, (((1,), (0,)), ((), ())), preferred_element_type=F32)


def nt(a, b):
    return lax.dot_general(a, b, (((1,), (1,)), ((), ())), preferred_element_type=F32)


def tn(a, b):
    return lax.dot_general(a, b, (((0,), (0,)), ((), ())), preferred_element_type=F32)


def full(shape):
    return pl.BlockSpec(shape, lambda *_: (0,) * len(shape))


def params(grid_rank=1):
    return pltpu.CompilerParams(
        dimension_semantics=("arbitrary",) * grid_rank, vmem_limit_bytes=VMEM_LIMIT
    )


def smem():
    return pl.BlockSpec(memory_space=pltpu.SMEM)


def block_source(first, number, rows, image, length):
    at = first + image * number + rows
    at = jnp.where(at >= length, at - length, at)
    return jnp.where(rows < image, at, -1)


def place_rows(first, source, target_rows, image):
    length = source.shape[0]

    def one(number):
        rows = lax.broadcasted_iota(jnp.int32, (target_rows, 1), 0)
        wanted = block_source(first, number, rows, image, length)
        columns = lax.broadcasted_iota(jnp.int32, (target_rows, length), 1)
        return nn((columns == wanted).astype(BF16), source)

    return one


def restore_rows(first, blocked, block_rows, image, length):
    lanes = lax.broadcasted_iota(jnp.int32, (1, block_rows), 1)
    wanted = jnp.concatenate(
        [block_source(first, number, lanes, image, length) for number in range(IMGS)], axis=1
    )
    rows = lax.broadcasted_iota(jnp.int32, (length, IMGS * block_rows), 0)
    return nn((rows == wanted).astype(BF16), blocked)


def prepare_body(image, block_rows, info, x_ref, cot_ref, xb_ref, cb_ref, normed_ref, inv_ref):
    first = info[0]
    for number in range(IMGS):
        here = pl.ds(number * block_rows, block_rows)
        values = place_rows(first, x_ref[...], block_rows, image)(number)
        xb_ref[here, :] = values.astype(BF16)
        average = jnp.mean(values, axis=-1, keepdims=True)
        centred = values - average
        inverse = lax.rsqrt(jnp.mean(centred * centred, axis=-1, keepdims=True) + EPS)
        normed_ref[here, :] = centred * inverse
        inv_ref[here, :] = jnp.broadcast_to(inverse, (block_rows, 128))
        cb_ref[here, :] = place_rows(first, cot_ref[...], block_rows, image)(number).astype(BF16)


def prepare(info, x, cot, image, block_rows):
    length, width = x.shape
    rows = IMGS * block_rows
    return pl.pallas_call(
        functools.partial(prepare_body, image, block_rows),
        grid=(1,),
        in_specs=[smem(), full((length, width)), full((length, width))],
        out_specs=[full((rows, width)), full((rows, width)), full((rows, width)), full((rows, 128))],
        out_shape=[
            jax.ShapeDtypeStruct((rows, width), BF16),
            jax.ShapeDtypeStruct((rows, width), BF16),
            jax.ShapeDtypeStruct((rows, width), F32),
            jax.ShapeDtypeStruct((rows, 128), F32),
        ],
        compiler_params=params(),
        name="prepare",
    )(info, x, cot)


def expand_body(heads, small_ref, index_ref, vec_ref, fc1b_ref, table_ref):
    eye = (
        lax.broadcasted_iota(jnp.int32, (SMALL, SMALL), 0)
        == lax.broadcasted_iota(jnp.int32, (SMALL, SMALL), 1)
    ).astype(BF16)
    width = small_ref.shape[0]
    hidden = fc1b_ref.shape[1]
    ratio = hidden // width
    rows = nt(eye, small_ref[...])
    vec_ref[...] = rows[: vec_ref.shape[0]]
    spread = (
        lax.broadcasted_iota(jnp.int32, (width, hidden), 0)
        == lax.broadcasted_iota(jnp.int32, (width, hidden), 1) // ratio
    ).astype(BF16)
    wide = nn(rows[FC1_B : FC1_B + 8].astype(BF16), spread)
    which = lax.broadcasted_iota(jnp.int32, (8, hidden), 1) % ratio
    mine = lax.broadcasted_iota(jnp.int32, (8, hidden), 0)
    total = jnp.sum(jnp.where(which == mine, wide, 0.0), axis=0, keepdims=True)
    fc1b_ref[...] = jnp.broadcast_to(total, fc1b_ref.shape)
    length, lanes = index_ref.shape
    image = lanes - 59
    for half in range(lanes // 128):
        index = index_ref[:, half * 128 : (half + 1) * 128]
        low = jnp.bitwise_and(index, 127)
        high = jnp.right_shift(index, 7)
        for head in range(heads):
            found = jnp.zeros((length, 128), F32)
            for part in range(width // 128):
                entries = jnp.broadcast_to(
                    rows[TABLE + head : TABLE + head + 1, part * 128 : (part + 1) * 128],
                    (length, 128),
                )
                taken = jnp.take_along_axis(entries, low, axis=1)
                found = jnp.where(high == part, taken, found)
            table_ref[head, :, half * 128 : (half + 1) * 128] = jnp.where(index < 0, MASKED, found)


def expand(gathered, index, heads, hidden, at):
    width = gathered.shape[0]
    length, lanes = index.shape
    return pl.pallas_call(
        functools.partial(expand_body, heads),
        grid=(1,),
        in_specs=[pl.BlockSpec((width, SMALL), lambda i: (0, at // SMALL)), full((length, lanes))],
        out_specs=[full((64, width)), full((8, hidden)), full((heads, length, lanes))],
        out_shape=[
            jax.ShapeDtypeStruct((64, width), F32),
            jax.ShapeDtypeStruct((8, hidden), F32),
            jax.ShapeDtypeStruct((heads, length, lanes), F32),
        ],
        compiler_params=params(),
        name="expand",
    )(gathered, index)


def project_body(scale, normed_ref, vec_ref, weight_ref, packed_ref, low_ref):
    step = pl.program_id(0)

    @pl.when(step == 0)
    def _():
        low_ref[...] = (
            normed_ref[...] * vec_ref[LN1_G : LN1_G + 1, :] + vec_ref[LN1_B : LN1_B + 1, :]
        ).astype(BF16)

    bias = jnp.where(
        step == 0,
        vec_ref[Q_B : Q_B + 1, :],
        jnp.where(step == 2, vec_ref[V_B : V_B + 1, :], 0.0),
    )
    result = (nn(low_ref[...], weight_ref[...]) + bias).astype(BF16)
    packed_ref[...] = (result.astype(F32) * jnp.where(step == 0, scale, 1.0)).astype(BF16)


def project(normed, vec, gathered, head_dim):
    rows, width = normed.shape
    return pl.pallas_call(
        functools.partial(project_body, head_dim**-0.5),
        grid=(3,),
        in_specs=[
            full((rows, width)),
            full(vec.shape),
            pl.BlockSpec((width, width), lambda i: (0, i)),
        ],
        out_specs=[pl.BlockSpec((rows, width), lambda i: (0, i)), full((rows, width))],
        out_shape=[
            jax.ShapeDtypeStruct((rows, 3 * width), BF16),
            jax.ShapeDtypeStruct((rows, width), BF16),
        ],
        compiler_params=params(),
        name="project",
    )(normed, vec, gathered)


def halves(values):
    lanes = lax.broadcasted_iota(jnp.int32, values.shape, 1)
    zero = jnp.zeros((), values.dtype)
    side = values.shape[1] // 2
    return (jnp.where(lanes < side, values, zero), jnp.where(lanes >= side, values, zero))


def attend_body(block_rows, info, q_ref, k_ref, v_ref, table_ref, mixed_ref, weight_ref):
    padded = info[1] == 1
    rows = lax.broadcasted_iota(jnp.int32, (block_rows, block_rows), 0)
    columns = lax.broadcasted_iota(jnp.int32, (block_rows, block_rows), 1)
    alone = jnp.where(rows == columns, 0.0, MASKED)
    for number in range(IMGS):
        here = pl.ds(number * block_rows, block_rows)
        queries = halves(q_ref[here, :])
        values = halves(v_ref[here, :])
        keys = k_ref[here, :]
        mixed = None
        for side in range(2):
            bias = table_ref[side, :, :block_rows]
            if number == IMGS - 1:
                bias = jnp.where(padded, alone, bias)
            scores = nt(queries[side], keys) + bias
            raised = jnp.exp(scores - jnp.max(scores, axis=1, keepdims=True))
            weights = raised * (1.0 / jnp.sum(raised, axis=1, keepdims=True))
            weight_ref[side, number] = weights
            part = nn(weights.astype(BF16), values[side])
            mixed = part if mixed is None else mixed + part
        mixed_ref[here, :] = mixed.astype(BF16)


def attend(info, packed, table, block_rows):
    rows, three = packed.shape
    pairs = three // (3 * 128)
    heads, length, lanes = table.shape
    return pl.pallas_call(
        functools.partial(attend_body, block_rows),
        grid=(pairs,),
        in_specs=[
            smem(),
            pl.BlockSpec((rows, 128), lambda p: (0, p)),
            pl.BlockSpec((rows, 128), lambda p: (0, pairs + p)),
            pl.BlockSpec((rows, 128), lambda p: (0, 2 * pairs + p)),
            pl.BlockSpec((2, length, lanes), lambda p: (p, 0, 0)),
        ],
        out_specs=[
            pl.BlockSpec((rows, 128), lambda p: (0, p)),
            pl.BlockSpec((2, IMGS, block_rows, block_rows), lambda p: (p, 0, 0, 0)),
        ],
        out_shape=[
            jax.ShapeDtypeStruct((rows, pairs * 128), BF16),
            jax.ShapeDtypeStruct((heads, IMGS, block_rows, block_rows), F32),
        ],
        compiler_params=params(),
        name="attend",
    )(info, packed, packed, packed, table)


def attend_back_body(
    block_rows, scale, q_ref, k_ref, v_ref, weight_ref, grad_ref, dq_ref, dk_ref, dv_ref, table_ref
):
    for side in range(2):
        table_ref[side] = jnp.zeros(table_ref.shape[1:], F32)
    for number in range(IMGS):
        here = pl.ds(number * block_rows, block_rows)
        queries = halves(q_ref[here, :])
        keys = halves(k_ref[here, :])
        grads = halves(grad_ref[here, :])
        values = v_ref[here, :]
        dq = dk = dv = 0.0
        for side in range(2):
            weights = weight_ref[side, number]
            up = nt(grads[side], values)
            inner = jnp.sum(weights * up, axis=1, keepdims=True)
            score = (weights * (up - inner)).astype(BF16)
            dv += tn(weights.astype(BF16), grads[side])
            dq += nn(score, keys[side])
            dk += tn(score, queries[side])
            table_ref[side, :, :block_rows] += score.astype(F32)
        dq_ref[here, :] = (dq * scale).astype(BF16)
        dk_ref[here, :] = dk.astype(BF16)
        dv_ref[here, :] = dv.astype(BF16)


def attend_back(packed, weights, mixed_grad, head_dim, lanes):
    rows, three = packed.shape
    pairs = three // (3 * 128)
    heads, _, block_rows, _ = weights.shape
    part = pl.BlockSpec((rows, 128), lambda p: (0, p))
    shape = jax.ShapeDtypeStruct((rows, pairs * 128), BF16)
    return pl.pallas_call(
        functools.partial(attend_back_body, block_rows, head_dim**-0.5),
        grid=(pairs,),
        in_specs=[
            part,
            pl.BlockSpec((rows, 128), lambda p: (0, pairs + p)),
            pl.BlockSpec((rows, 128), lambda p: (0, 2 * pairs + p)),
            pl.BlockSpec((2, IMGS, block_rows, block_rows), lambda p: (p, 0, 0, 0)),
            part,
        ],
        out_specs=[part, part, part, pl.BlockSpec((2, block_rows, lanes), lambda p: (p, 0, 0))],
        out_shape=[shape, shape, shape, jax.ShapeDtypeStruct((heads, block_rows, lanes), F32)],
        compiler_params=params(),
        name="attend_back",
    )(packed, packed, packed, weights, mixed_grad)


def cumulative(values):
    squared = jnp.exp(-0.5 * values * values)
    size = jnp.abs(values) * ROOT_HALF
    t = 1.0 / (1.0 + 0.3275911 * size)
    poly = t * (
        0.254829592 + t * (-0.284496736 + t * (1.421413741 + t * (-1.453152027 + t * 1.061405429)))
    )
    tail = 0.5 * poly * squared
    return jnp.where(values < 0, tail, 1.0 - tail), squared * INV_ROOT_TAU


def feed_body(
    image,
    block_rows,
    steps,
    info,
    mixed_ref,
    xb_ref,
    cb_ref,
    vec_ref,
    bias_ref,
    out_w_ref,
    fc1_ref,
    fc2_ref,
    out_ref,
    grads_ref,
    mixed_grad_ref,
    after_grad_ref,
    sums_ref,
    fc1_sum_ref,
    branch_s,
    after_s,
    low_s,
    low_t_s,
    up_s,
    up_t_s,
    ff_s,
    second_s,
):
    step = pl.program_id(0)
    width = xb_ref.shape[1]

    def vec(row):
        return vec_ref[row : row + 1, :]

    def norm(values):
        average = jnp.mean(values, axis=-1, keepdims=True)
        centred = values - average
        inverse = lax.rsqrt(jnp.mean(centred * centred, axis=-1, keepdims=True) + EPS)
        return centred * inverse, inverse

    @pl.when(step == 0)
    def _():
        branch = nt(mixed_ref[...], out_w_ref[...]) + vec(OUT_B)
        branch_s[...] = branch
        after = xb_ref[...].astype(F32) + vec(GAM_A) * branch
        after_s[...] = after
        normed, _ = norm(after)
        low = (normed * vec(LN2_G) + vec(LN2_B)).astype(BF16)
        low_s[...] = low
        low_t_s[...] = low.T
        up = (vec(GAM_M) * cb_ref[...].astype(F32)).astype(BF16)
        up_s[...] = up
        up_t_s[...] = up.T
        ff_s[...] = jnp.zeros_like(ff_s)
        second_s[...] = jnp.zeros_like(second_s)

    @pl.when(step < steps)
    def _():
        pre = nn(low_s[...], fc1_ref[...]) + bias_ref[0:1, :]
        phi, density = cumulative(pre)
        hidden = (pre * phi).astype(BF16)
        slope = phi + pre * density
        grad = (nn(up_s[...], fc2_ref[...]) * slope).astype(BF16)
        ff_s[...] += nt(hidden, fc2_ref[...])
        second_s[...] += nt(grad, fc1_ref[...])
        tile = fc1_ref.shape[1]
        grads_ref[:, :tile] = nn(low_t_s[...], grad).astype(BF16)
        grads_ref[:, tile:] = nn(up_t_s[...], hidden).astype(BF16)
        fc1_sum_ref[...] = jnp.broadcast_to(
            jnp.sum(grad.astype(F32), axis=0, keepdims=True), fc1_sum_ref.shape
        )

    @pl.when(step == steps)
    def _():
        cot = cb_ref[...].astype(F32)
        branch = ff_s[...] + vec(FC2_B)
        result = (after_s[...] + vec(GAM_M) * branch).astype(BF16)
        out_ref[...] = restore_rows(info[0], result, block_rows, image, out_ref.shape[0]).astype(
            BF16
        )

        def put(row, values):
            sums_ref[row : row + 1, :] = jnp.sum(values, axis=0, keepdims=True)

        sums_ref[...] = jnp.zeros_like(sums_ref)
        put(G_GAM_M, cot * branch)
        put(G_FC2_B, up_s[...].astype(F32))
        normed, inverse = norm(after_s[...])
        second = second_s[...]
        put(G_LN2_G, second * normed)
        put(G_LN2_B, second)
        scaled = second * vec(LN2_G)
        inner = jnp.mean(scaled, axis=-1, keepdims=True)
        along = jnp.mean(scaled * normed, axis=-1, keepdims=True)
        after_grad = cot + inverse * (scaled - inner - normed * along)
        after_grad_ref[...] = after_grad
        put(G_GAM_A, after_grad * branch_s[...])
        low = (vec(GAM_A) * after_grad).astype(BF16)
        put(G_OUT_B, low.astype(F32))
        mixed_grad_ref[...] = nn(low, out_w_ref[...]).astype(BF16)
        grads_ref[:, :width] = tn(low, mixed_ref[...]).astype(BF16)
        grads_ref[:, width:] = jnp.zeros(
            (grads_ref.shape[0], grads_ref.shape[1] - width), BF16
        )


def feed(info, mixed, xb, cb, vec, fc1b, gathered, image, block_rows, length, tile):
    rows, width = xb.shape
    hidden = fc1b.shape[1]
    steps = hidden // tile
    out_at, fc1_at, fc2_at = 3 * width, 4 * width, 4 * width + hidden

    def last(i):
        return jnp.minimum(i, steps - 1)

    return pl.pallas_call(
        functools.partial(feed_body, image, block_rows, steps),
        grid=(steps + 1,),
        in_specs=[
            smem(),
            full((rows, width)),
            full((rows, width)),
            full((rows, width)),
            full(vec.shape),
            pl.BlockSpec((8, tile), lambda i: (0, last(i))),
            pl.BlockSpec((width, width), lambda i: (0, out_at // width)),
            pl.BlockSpec((width, tile), lambda i: (0, fc1_at // tile + last(i))),
            pl.BlockSpec((width, tile), lambda i: (0, fc2_at // tile + last(i))),
        ],
        out_specs=[
            full((length, width)),
            pl.BlockSpec((width, 2 * tile), lambda i: (0, i)),
            full((rows, width)),
            full((rows, width)),
            full((16, width)),
            pl.BlockSpec((8, tile), lambda i: (0, last(i))),
        ],
        out_shape=[
            jax.ShapeDtypeStruct((length, width), BF16),
            jax.ShapeDtypeStruct((width, 2 * tile * (steps + 1)), BF16),
            jax.ShapeDtypeStruct((rows, width), BF16),
            jax.ShapeDtypeStruct((rows, width), F32),
            jax.ShapeDtypeStruct((16, width), F32),
            jax.ShapeDtypeStruct((8, hidden), F32),
        ],
        scratch_shapes=[
            pltpu.VMEM((rows, width), F32),
            pltpu.VMEM((rows, width), F32),
            pltpu.VMEM((rows, width), BF16),
            pltpu.VMEM((width, rows), BF16),
            pltpu.VMEM((rows, width), BF16),
            pltpu.VMEM((width, rows), BF16),
            pltpu.VMEM((rows, width), F32),
            pltpu.VMEM((rows, width), F32),
        ],
        compiler_params=params(),
        name="feed",
    )(info, mixed, xb, cb, vec, fc1b, gathered, gathered, gathered)


def weight_grad_body(low_ref, dq_ref, dk_ref, dv_ref, grad_ref, low_t_s):
    step = pl.program_id(0)

    @pl.when(step == 0)
    def _():
        low_t_s[...] = low_ref[...].T

    for number, ref in enumerate((dq_ref, dk_ref, dv_ref)):

        @pl.when(step == number)
        def _(ref=ref):
            grad_ref[...] = nn(low_t_s[...], ref[...]).astype(BF16)


def weight_grad(low, dq, dk, dv):
    rows, width = low.shape
    return pl.pallas_call(
        weight_grad_body,
        grid=(3,),
        in_specs=[full((rows, width))] * 4,
        out_specs=pl.BlockSpec((width, width), lambda i: (0, i)),
        out_shape=jax.ShapeDtypeStruct((width, 3 * width), BF16),
        scratch_shapes=[pltpu.VMEM((width, rows), BF16)],
        compiler_params=params(),
        name="weight_grad",
    )(low, dq, dk, dv)


def input_grad_body(
    image,
    block_rows,
    info,
    dq_ref,
    dk_ref,
    dv_ref,
    wq_ref,
    wk_ref,
    wv_ref,
    normed_ref,
    inv_ref,
    after_grad_ref,
    vec_ref,
    out_ref,
    sums_ref,
):
    first = nt(dq_ref[...], wq_ref[...])
    first += nt(dk_ref[...], wk_ref[...])
    first += nt(dv_ref[...], wv_ref[...])

    def put(row, values):
        sums_ref[row : row + 1, :] = jnp.sum(values, axis=0, keepdims=True)

    sums_ref[...] = jnp.zeros_like(sums_ref)
    put(G_Q_B, dq_ref[...].astype(F32))
    put(G_V_B, dv_ref[...].astype(F32))
    normed = normed_ref[...]
    put(G_LN1_G, first * normed)
    put(G_LN1_B, first)
    scaled = first * vec_ref[LN1_G : LN1_G + 1, :]
    inner = jnp.mean(scaled, axis=-1, keepdims=True)
    along = jnp.mean(scaled * normed, axis=-1, keepdims=True)
    back = inv_ref[:, :1] * (scaled - inner - normed * along)
    result = (after_grad_ref[...] + back).astype(BF16)
    out_ref[...] = restore_rows(info[0], result, block_rows, image, out_ref.shape[0]).astype(BF16)


def input_grad(info, dq, dk, dv, gathered, normed, inv, after_grad, vec, image, block_rows, length):
    rows, width = normed.shape
    return pl.pallas_call(
        functools.partial(input_grad_body, image, block_rows),
        grid=(1,),
        in_specs=[
            smem(),
            full((rows, width)),
            full((rows, width)),
            full((rows, width)),
            pl.BlockSpec((width, width), lambda i: (0, 0)),
            pl.BlockSpec((width, width), lambda i: (0, 1)),
            pl.BlockSpec((width, width), lambda i: (0, 2)),
            full((rows, width)),
            full((rows, 128)),
            full((rows, width)),
            full(vec.shape),
        ],
        out_specs=[full((length, width)), full((16, width))],
        out_shape=[
            jax.ShapeDtypeStruct((length, width), BF16),
            jax.ShapeDtypeStruct((16, width), F32),
        ],
        compiler_params=params(),
        name="input_grad",
    )(info, dq, dk, dv, gathered, gathered, gathered, normed, inv, after_grad, vec)


def table_grad_body(heads, image, table_ref, index_ref, out_ref, acc):
    lanes = index_ref.shape[1]
    parts = out_ref.shape[1] // 128
    acc[...] = jnp.zeros_like(acc)
    slots = lax.broadcasted_iota(jnp.int32, (128, lanes), 0)

    def one(row, carry):
        index = index_ref[pl.ds(row, 1), :]
        low = jnp.bitwise_and(index, 127)
        high = jnp.right_shift(index, 7)
        chosen = (slots == low).astype(BF16)
        values = jnp.concatenate(
            [table_ref[:, pl.ds(row, 1), :].reshape(heads, lanes), jnp.zeros((16 - heads, lanes), F32)],
            axis=0,
        )
        coarse = values.astype(BF16)
        fine = (values - coarse.astype(F32)).astype(BF16)
        zero = jnp.zeros((), BF16)
        stacked = jnp.concatenate(
            [jnp.where(high == part, kind, zero) for kind in (coarse, fine) for part in range(parts)],
            axis=0,
        )
        acc[...] += nt(stacked, chosen)
        return carry

    lax.fori_loop(0, image, one, 0)
    half = parts * 16
    for part in range(parts):
        out_ref[:, part * 128 : (part + 1) * 128] = (
            acc[part * 16 : (part + 1) * 16, :] + acc[half + part * 16 : half + (part + 1) * 16, :]
        )


def table_grad(table, index, slots, image):
    heads, length, lanes = table.shape
    return pl.pallas_call(
        functools.partial(table_grad_body, heads, image),
        grid=(1,),
        in_specs=[full(table.shape), full(index.shape)],
        out_specs=full((16, slots)),
        out_shape=jax.ShapeDtypeStruct((16, slots), F32),
        scratch_shapes=[pltpu.VMEM((2 * 16 * slots // 128, 128), F32)],
        compiler_params=params(),
        name="table_grad",
    )(table, index)


def local(
    inputs,
    cotangent,
    segment_ids,
    keep_rows,
    index_map,
    ln1_gain,
    ln1_bias,
    qkv_weight,
    qv_bias,
    out_weight,
    out_bias,
    gamma_attn,
    rel_table,
    ln2_gain,
    ln2_bias,
    fc1_weight,
    fc1_bias,
    fc2_weight,
    fc2_bias,
    gamma_mlp,
):
    _, length, width = inputs.shape
    heads, per_device = rel_table.shape
    head_dim = width // heads
    own = ln1_gain.shape[0]
    count = width // own
    hidden = fc1_weight.shape[1]
    image = index_map.shape[0]
    block_rows = -(-image // 16) * 16

    keep = keep_rows[0] == 1
    ids = lax.iota(jnp.int32, length)
    info = jnp.stack([jnp.min(jnp.where(keep, ids, length)), jnp.max(jnp.where(keep, 0, 1))])
    moved = index_map // per_device * own + index_map % per_device
    moved = jnp.pad(moved, ((0, block_rows - image), (0, 256 - image)), constant_values=-1)

    small_columns = [
        ln1_gain,
        ln1_bias,
        qv_bias[0],
        qv_bias[1],
        out_bias,
        gamma_attn,
        ln2_gain,
        ln2_bias,
        fc2_bias,
        gamma_mlp,
    ]
    small = jnp.concatenate(
        [
            jnp.stack(small_columns, axis=1),
            jnp.zeros((own, FC1_B - len(small_columns)), BF16),
            fc1_bias.reshape(own, -1),
            jnp.zeros((own, TABLE - FC1_B - hidden // width), BF16),
            jnp.pad(rel_table.T, ((0, own - per_device), (0, SMALL - TABLE - heads))),
        ],
        axis=1,
    )
    payload = jnp.concatenate([qkv_weight, out_weight.T, fc1_weight, fc2_weight.T, small], axis=1)
    gathered = lax.all_gather(payload, AX, axis=0, tiled=True)
    xb, cb, normed, inv = prepare(info, inputs[0], cotangent[0], image, block_rows)
    vec, fc1b, table = expand(gathered, moved, heads, hidden, 4 * width + 2 * hidden)
    packed, low = project(normed, vec, gathered, head_dim)
    mixed, weights = attend(info, packed, table, block_rows)
    tile = 512
    out, feed_grads, mixed_grad, after_grad, sums2, fc1_sum = feed(
        info, mixed, xb, cb, vec, fc1b, gathered, image, block_rows, length, tile
    )
    feed_shard = lax.psum_scatter(feed_grads, AX, scatter_dimension=0, tiled=True)
    dq, dk, dv, table_sum = attend_back(packed, weights, mixed_grad, head_dim, 256)
    qkv_grads = weight_grad(low, dq, dk, dv)
    qkv_shard = lax.psum_scatter(qkv_grads, AX, scatter_dimension=0, tiled=True)
    in_grad, sums1 = input_grad(
        info, dq, dk, dv, gathered, normed, inv, after_grad, vec, image, block_rows, length
    )
    slot_sums = table_grad(table_sum, moved, own * count, image)

    rows = jnp.concatenate([sums1[:10] + sums2[:10], slot_sums[:heads]], axis=0)
    rows = jnp.transpose(rows.reshape(-1, count, own), (1, 0, 2))
    biases = fc1_sum[0].reshape(count, -1, own)
    swapped = lax.all_to_all(jnp.concatenate([rows, biases], axis=1), AX, 0, 0, tiled=True)
    small_shard = jnp.sum(swapped, axis=0)

    feed_wide = feed_shard.astype(F32)
    steps = hidden // tile
    pieces = feed_wide[:, : 2 * hidden].reshape(own, steps, 2, tile)
    grad_fc1 = pieces[:, :, 0].reshape(own, hidden)
    grad_fc2 = pieces[:, :, 1].reshape(own, hidden).T
    grad_out = feed_wide[:, 2 * hidden : 2 * hidden + width].T
    grad_table = small_shard[10 : 10 + heads, :per_device]
    grad_fc1_bias = small_shard[10 + heads :].reshape(-1)
    return (
        out[None],
        in_grad[None],
        small_shard[G_LN1_G],
        small_shard[G_LN1_B],
        qkv_shard.astype(F32),
        small_shard[G_Q_B : G_V_B + 1],
        grad_out,
        small_shard[G_OUT_B],
        small_shard[G_GAM_A],
        grad_table,
        small_shard[G_LN2_G],
        small_shard[G_LN2_B],
        grad_fc1,
        grad_fc1_bias,
        grad_fc2,
        small_shard[G_FC2_B],
        small_shard[G_GAM_M],
    )


def solution(mesh):
    rows = P(AX)
    columns = P(None, AX)
    return jax.shard_map(
        local,
        mesh=mesh,
        in_specs=(
            rows,
            rows,
            rows,
            rows,
            P(),
            rows,
            rows,
            rows,
            columns,
            columns,
            rows,
            rows,
            columns,
            rows,
            rows,
            rows,
            rows,
            columns,
            rows,
            rows,
        ),
        out_specs=(
            rows,
            rows,
            rows,
            rows,
            rows,
            columns,
            columns,
            rows,
            rows,
            columns,
            rows,
            rows,
            rows,
            rows,
            columns,
            rows,
            rows,
        ),
        check_vma=False,
    )
```

```python
import functools
import jax
import jax.numpy as jnp
from jax import lax
from jax.experimental import pallas as pl
from jax.experimental.pallas import tpu as pltpu
from jax.sharding import PartitionSpec as P

AX = ("dp", "fsdp")
IMGS = 4
EPS = 1e-06
MASKED = -1e30
ROOT_HALF = 0.7071067811865476
INV_ROOT_TAU = 0.3989422804014327
F32 = jnp.float32
BF16 = jnp.bfloat16
VMEM_LIMIT = 60 * 1024 * 1024

LN1_G, LN1_B, Q_B, V_B, OUT_B, GAM_A, LN2_G, LN2_B, FC2_B, GAM_M = range(10)
FC1_B = 16
TABLE = 32
SMALL = 128
G_LN1_G, G_LN1_B, G_Q_B, G_V_B, G_OUT_B, G_GAM_A, G_LN2_G, G_LN2_B, G_FC2_B, G_GAM_M = range(10)


def nn(a, b):
    return lax.dot_general(a, b, (((1,), (0,)), ((), ())), preferred_element_type=F32)


def nt(a, b):
    return lax.dot_general(a, b, (((1,), (1,)), ((), ())), preferred_element_type=F32)


def tn(a, b):
    return lax.dot_general(a, b, (((0,), (0,)), ((), ())), preferred_element_type=F32)


def full(shape):
    return pl.BlockSpec(shape, lambda *_: (0,) * len(shape))


def cost(gigaflops, megabytes=4):
    return pl.CostEstimate(
        flops=int(gigaflops * 2e7), bytes_accessed=int(megabytes * 2e4), transcendentals=0
    )


def after(value, *others):
    return lax.optimization_barrier((value, *others))[0]


def params(grid_rank=1):
    return pltpu.CompilerParams(
        dimension_semantics=("arbitrary",) * grid_rank, vmem_limit_bytes=VMEM_LIMIT
    )


def smem():
    return pl.BlockSpec(memory_space=pltpu.SMEM)


def exchange_orders(count):
    bits = count.bit_length() - 1
    if bits < 3:
        return (list(range(bits)),) * 2
    rest = list(range(2, bits - 1))
    return [0, 1, bits - 1] + rest, [0, bits - 1, 1] + rest[::-1]

def exchange(values, step, count):
    orders = exchange_orders(count)
    return lax.ppermute(values, AX, [(i, i ^ (1 << orders[i & 1][step])) for i in range(count)])


def exchange_owners(count):
    orders = exchange_orders(count)
    bits = len(orders[0])
    me = lax.axis_index(AX)
    spot = jnp.arange(count, dtype=jnp.int32)
    other = spot >> (bits - 1) if bits else spot
    kind = jnp.bitwise_xor(jnp.bitwise_and(me, 1), other)
    flips = other
    for step in range(1, bits):
        bit = jnp.bitwise_and(spot >> (bits - 1 - step), 1)
        flips = jnp.bitwise_or(
            flips, bit << jnp.where(kind == 1, orders[1][step], orders[0][step])
        )
    return jnp.bitwise_xor(me, flips)


def gather_halves(values, count, before):
    for number, step in enumerate(reversed(range(count.bit_length() - 1))):
        got = exchange(values, step, count)
        if number < len(before):
            got = after(got, *before[number])
        if step == 0:
            return values, got
        values = jnp.concatenate([values, got], axis=0)
    half = values.shape[0] // 2
    return values[:half], values[half:]


def scatter_step(keep, send, step, count, *others):
    got = after(exchange(send, step, count), *others)
    half = keep.shape[0] // 2
    if step == count.bit_length() - 2:
        return keep.astype(F32) + got.astype(F32), None
    return (
        (keep[:half].astype(F32) + got[:half].astype(F32)).astype(BF16),
        (keep[half:].astype(F32) + got[half:].astype(F32)).astype(BF16),
    )


def row_order(column):
    width = column.shape[0]
    return (lax.broadcasted_iota(jnp.int32, (width, width), 1) == column).astype(BF16)


def block_source(first, number, rows, image, length):
    at = first + image * number + rows
    at = jnp.where(at >= length, at - length, at)
    return jnp.where(rows < image, at, -1)


def place_rows(first, source, target_rows, image):
    length = source.shape[0]

    def one(number):
        rows = lax.broadcasted_iota(jnp.int32, (target_rows, 1), 0)
        wanted = block_source(first, number, rows, image, length)
        columns = lax.broadcasted_iota(jnp.int32, (target_rows, length), 1)
        return nn((columns == wanted).astype(BF16), source)

    return one


def restore_rows(first, blocked, block_rows, image, length):
    lanes = lax.broadcasted_iota(jnp.int32, (1, block_rows), 1)
    wanted = jnp.concatenate(
        [block_source(first, number, lanes, image, length) for number in range(IMGS)], axis=1
    )
    rows = lax.broadcasted_iota(jnp.int32, (length, IMGS * block_rows), 0)
    return nn((rows == wanted).astype(BF16), blocked)


def pack_body(bias_at, table_at, ratio, bias_ref, table_ref, *rest):
    *row_refs, out_ref, rows_s = rest
    own = out_ref.shape[0]
    rows_s[...] = jnp.zeros_like(rows_s)
    at_row = 0
    for ref in row_refs:
        rows_s[at_row : at_row + ref.shape[0], :] = ref[...].astype(F32)
        at_row += ref.shape[0]
    heads, slots = table_ref.shape
    rows_s[table_at : table_at + heads, :slots] = table_ref[...].astype(F32)
    eye = (
        lax.broadcasted_iota(jnp.int32, (own, own), 0)
        == lax.broadcasted_iota(jnp.int32, (own, own), 1)
    ).astype(BF16)
    small = nt(eye, rows_s[...].astype(BF16))
    biases = jnp.broadcast_to(bias_ref[...].astype(F32), (own, own * ratio))
    at = lax.broadcasted_iota(jnp.int32, (own, own * ratio), 1)
    row = lax.broadcasted_iota(jnp.int32, (own, own * ratio), 0)
    lane = lax.broadcasted_iota(jnp.int32, (own, SMALL), 1)
    for number in range(ratio):
        column = jnp.sum(
            jnp.where(at == row * ratio + number, biases, 0.0), axis=1, keepdims=True
        )
        small = small + jnp.where(lane == bias_at + number, column, 0.0)
    out_ref[...] = small.astype(BF16)


def pack(rows, bias, table, bias_at, table_at, ratio):
    own = rows[0].shape[1]
    operands = (bias, table, *rows)
    return pl.pallas_call(
        functools.partial(pack_body, bias_at, table_at, ratio),
        grid=(1,),
        in_specs=[full(value.shape) for value in operands],
        out_specs=full((own, SMALL)),
        out_shape=jax.ShapeDtypeStruct((own, SMALL), BF16),
        scratch_shapes=[pltpu.VMEM((SMALL, own), F32)],
        compiler_params=params(),
        name="pack",
    )(*operands)


def prepare_body(image, block_rows, info, x_ref, cot_ref, xb_ref, cb_ref, normed_ref, inv_ref):
    first = info[0]

    def one(number, carry):
        here = pl.ds(pl.multiple_of(number * block_rows, 16), block_rows)
        values = place_rows(first, x_ref[...], block_rows, image)(number)
        xb_ref[here, :] = values.astype(BF16)
        normed, inverse = normal(values)
        normed_ref[here, :] = normed
        inv_ref[here, :] = jnp.broadcast_to(inverse, (block_rows, 128))
        cb_ref[here, :] = place_rows(first, cot_ref[...], block_rows, image)(number).astype(BF16)
        return carry

    lax.fori_loop(0, IMGS, one, 0)


def prepare(info, x, cot, image, block_rows):
    length, width = x.shape
    rows = IMGS * block_rows
    return pl.pallas_call(
        functools.partial(prepare_body, image, block_rows),
        grid=(1,),
        in_specs=[smem(), full((length, width)), full((length, width))],
        out_specs=[full((rows, width))] * 3 + [full((rows, 128))],
        out_shape=[
            jax.ShapeDtypeStruct((rows, width), BF16),
            jax.ShapeDtypeStruct((rows, width), BF16),
            jax.ShapeDtypeStruct((rows, width), F32),
            jax.ShapeDtypeStruct((rows, 128), F32),
        ],
        compiler_params=params(),
        cost_estimate=cost(4),
        name="prepare",
    )(info, x, cot)


def expand_body(heads, small_ref, index_ref, vec_ref, fc1b_ref, table_ref, entries_s):
    eye = (
        lax.broadcasted_iota(jnp.int32, (SMALL, SMALL), 0)
        == lax.broadcasted_iota(jnp.int32, (SMALL, SMALL), 1)
    ).astype(BF16)
    width = small_ref.shape[0]
    hidden = fc1b_ref.shape[1]
    ratio = hidden // width
    rows = nt(eye, small_ref[...])
    vec_ref[...] = rows[: vec_ref.shape[0]]
    spread = (
        lax.broadcasted_iota(jnp.int32, (width, hidden), 0)
        == lax.broadcasted_iota(jnp.int32, (width, hidden), 1) // ratio
    ).astype(BF16)
    wide = nn(rows[FC1_B : FC1_B + 8].astype(BF16), spread)
    which = lax.broadcasted_iota(jnp.int32, (8, hidden), 1) % ratio
    mine = lax.broadcasted_iota(jnp.int32, (8, hidden), 0)
    total = jnp.sum(jnp.where(which == mine, wide, 0.0), axis=0, keepdims=True)
    fc1b_ref[...] = jnp.broadcast_to(total, fc1b_ref.shape)
    length, lanes = index_ref.shape
    parts = width // 128
    for head in range(heads):
        for part in range(parts):
            entries_s[head * parts + part] = jnp.broadcast_to(
                rows[TABLE + head : TABLE + head + 1, part * 128 : (part + 1) * 128], (8, 128)
            )

    def one(step, carry):
        at = pl.ds(pl.multiple_of(step * 8, 8), 8)
        for half in range(lanes // 128):
            columns = slice(half * 128, (half + 1) * 128)
            index = index_ref[at, columns]
            low = jnp.bitwise_and(index, 127)
            high = jnp.right_shift(index, 7)
            found = [jnp.full((8, 128), MASKED, F32)] * heads
            for part in range(parts):
                chosen = high == part
                for head in range(heads):
                    taken = jnp.take_along_axis(
                        entries_s[head * parts + part], low, axis=1, mode="promise_in_bounds"
                    )
                    found[head] = jnp.where(chosen, taken, found[head])
            for head in range(heads):
                table_ref[head, at, columns] = found[head]
        return carry

    lax.fori_loop(0, length // 8, one, 0)


def expand(small, index, heads, hidden):
    width = small.shape[0]
    length, lanes = index.shape
    return pl.pallas_call(
        functools.partial(expand_body, heads),
        grid=(1,),
        in_specs=[
            full((width, SMALL)),
            full((length, lanes)),
        ],
        out_specs=[full((64, width)), full((8, hidden)), full((heads, length, lanes))],
        out_shape=[
            jax.ShapeDtypeStruct((64, width), F32),
            jax.ShapeDtypeStruct((8, hidden), F32),
            jax.ShapeDtypeStruct((heads, length, lanes), F32),
        ],
        scratch_shapes=[pltpu.VMEM((heads * width // 128, 8, 128), F32)],
        compiler_params=params(),
        cost_estimate=cost(5),
        name="expand",
    )(small, index)


def project_body(
    scale,
    owners,
    normed_ref,
    vec_ref,
    mine_any,
    got_any,
    packed_ref,
    low_ref,
    weight_any,
    weight_s,
    sems,
    out_sem,
):
    step = pl.program_id(0)
    half = mine_any.shape[0]
    width = normed_ref.shape[1]
    keeping = pltpu.make_async_copy(weight_s, weight_any, out_sem)

    @pl.when(step == 0)
    def _():
        copies = []
        for spot in range(2 * half):
            source = mine_any.at[spot] if spot < half else got_any.at[spot - half]
            copy = pltpu.make_async_copy(source, weight_s.at[owners[spot]], sems.at[spot])
            copy.start()
            copies.append(copy)
        low_ref[...] = (
            normed_ref[...] * vec_ref[LN1_G : LN1_G + 1, :] + vec_ref[LN1_B : LN1_B + 1, :]
        ).astype(BF16)
        for copy in copies:
            copy.wait()
        keeping.start()

    bias = jnp.where(
        step == 0,
        vec_ref[Q_B : Q_B + 1, :],
        jnp.where(step == 2, vec_ref[V_B : V_B + 1, :], 0.0),
    )
    for number in range(3):

        @pl.when(step == number)
        def _(number=number):
            weight = weight_s[:, :, number * width : (number + 1) * width].reshape(width, width)
            result = (nn(low_ref[...], weight) + bias).astype(BF16)
            if number == 0:
                result = (result.astype(F32) * scale).astype(BF16)
            packed_ref[...] = result

    @pl.when(step == 2)
    def _():
        keeping.wait()


def project(owners, normed, vec, mine, got, head_dim):
    rows, width = normed.shape
    count = owners.shape[0]
    wide = mine.shape[1]
    own = width // count
    anywhere = pl.BlockSpec(memory_space=pl.ANY)
    half = -(-count // 2)
    return pl.pallas_call(
        functools.partial(project_body, head_dim**-0.5),
        grid=(3,),
        in_specs=[smem(), full((rows, width)), full(vec.shape), anywhere, anywhere],
        out_specs=[
            pl.BlockSpec((rows, width), lambda i: (0, i)),
            full((rows, width)),
            anywhere,
        ],
        out_shape=[
            jax.ShapeDtypeStruct((rows, wide), BF16),
            jax.ShapeDtypeStruct((rows, width), BF16),
            jax.ShapeDtypeStruct((count, own, wide), BF16),
        ],
        scratch_shapes=[
            pltpu.VMEM((count, own, wide), BF16),
            pltpu.SemaphoreType.DMA((2 * half,)),
            pltpu.SemaphoreType.DMA,
        ],
        compiler_params=params(),
        cost_estimate=cost(4),
        name="project",
    )(owners, normed, vec, mine.reshape(half, own, wide), got.reshape(half, own, wide))


def turn_body(order_ref, vec_ref, cb_ref, low_ref, up_ref, up_t_ref, low_t_ref):
    order = row_order(order_ref[...])
    up = (vec_ref[GAM_M : GAM_M + 1, :] * cb_ref[...].astype(F32)).astype(BF16)
    up_ref[...] = up
    up_t_ref[...] = nt(order, up).astype(BF16)
    low_t_ref[...] = nt(order, low_ref[...]).astype(BF16)


def turn(order, vec, cb, low):
    rows, width = cb.shape
    return pl.pallas_call(
        turn_body,
        grid=(1,),
        in_specs=[full((width, 1)), full(vec.shape), full((rows, width)), full((rows, width))],
        out_specs=[full((rows, width)), full((width, rows)), full((width, rows))],
        out_shape=[
            jax.ShapeDtypeStruct((rows, width), BF16),
            jax.ShapeDtypeStruct((width, rows), BF16),
            jax.ShapeDtypeStruct((width, rows), BF16),
        ],
        compiler_params=params(),
        cost_estimate=cost(3),
        name="turn",
    )(order, vec, cb, low)


def combine_body(
    order_ref, mixed_ref, xb_ref, vec_ref, out_w_ref, branch_ref, after_ref, low_ref, low_t_ref
):
    branch = nt(mixed_ref[...], out_w_ref[...]) + vec_ref[OUT_B : OUT_B + 1, :]
    branch_ref[...] = branch
    after_attn = xb_ref[...].astype(F32) + vec_ref[GAM_A : GAM_A + 1, :] * branch
    after_ref[...] = after_attn
    normed, _ = normal(after_attn)
    low = (normed * vec_ref[LN2_G : LN2_G + 1, :] + vec_ref[LN2_B : LN2_B + 1, :]).astype(BF16)
    low_ref[...] = low
    low_t_ref[...] = nt(row_order(order_ref[...]), low).astype(BF16)


def combine(order, mixed, xb, vec, weights, at):
    rows, width = xb.shape
    return pl.pallas_call(
        combine_body,
        grid=(1,),
        in_specs=[
            full((width, 1)),
            full((rows, width)),
            full((rows, width)),
            full(vec.shape),
            pl.BlockSpec((width, width), lambda i: (0, at // width)),
        ],
        out_specs=[full((rows, width))] * 3 + [full((width, rows))],
        out_shape=[
            jax.ShapeDtypeStruct((rows, width), F32),
            jax.ShapeDtypeStruct((rows, width), F32),
            jax.ShapeDtypeStruct((rows, width), BF16),
            jax.ShapeDtypeStruct((width, rows), BF16),
        ],
        compiler_params=params(),
        cost_estimate=cost(4),
        name="combine",
    )(order, mixed, xb, vec, weights)


def halves(values):
    lanes = lax.broadcasted_iota(jnp.int32, values.shape, 1)
    zero = jnp.zeros((), values.dtype)
    side = values.shape[1] // 2
    return (jnp.where(lanes < side, values, zero), jnp.where(lanes >= side, values, zero))


def attend_body(block_rows, info, q_ref, k_ref, v_ref, table_ref, mixed_ref, weight_ref):
    rows = lax.broadcasted_iota(jnp.int32, (block_rows, block_rows), 0)
    columns = lax.broadcasted_iota(jnp.int32, (block_rows, block_rows), 1)
    alone = jnp.where(rows == columns, 0.0, MASKED)

    def one(number, carry):
        padded = jnp.logical_and(info[1] == 1, number == IMGS - 1)
        here = pl.ds(pl.multiple_of(number * block_rows, 16), block_rows)
        queries = halves(q_ref[here, :])
        values = halves(v_ref[here, :])
        keys = k_ref[here, :]
        mixed = None
        for side in range(2):
            bias = jnp.where(padded, alone, table_ref[side, :, :block_rows])
            scores = nt(queries[side], keys) + bias
            raised = jnp.exp(scores - jnp.max(scores, axis=1, keepdims=True))
            weights = raised * (1.0 / jnp.sum(raised, axis=1, keepdims=True))
            weight_ref[side, number] = weights
            part = nn(weights.astype(BF16), values[side])
            mixed = part if mixed is None else mixed + part
        mixed_ref[here, :] = mixed.astype(BF16)
        return carry

    lax.fori_loop(0, IMGS, one, 0, unroll=True)


def attend(info, packed, table, block_rows):
    rows, three = packed.shape
    pairs = three // (3 * 128)
    heads, length, lanes = table.shape
    return pl.pallas_call(
        functools.partial(attend_body, block_rows),
        grid=(pairs,),
        in_specs=[
            smem(),
            pl.BlockSpec((rows, 128), lambda p: (0, p)),
            pl.BlockSpec((rows, 128), lambda p: (0, pairs + p)),
            pl.BlockSpec((rows, 128), lambda p: (0, 2 * pairs + p)),
            pl.BlockSpec((2, length, lanes), lambda p: (p, 0, 0)),
        ],
        out_specs=[
            pl.BlockSpec((rows, 128), lambda p: (0, p)),
            pl.BlockSpec((2, IMGS, block_rows, block_rows), lambda p: (p, 0, 0, 0)),
        ],
        out_shape=[
            jax.ShapeDtypeStruct((rows, pairs * 128), BF16),
            jax.ShapeDtypeStruct((heads, IMGS, block_rows, block_rows), F32),
        ],
        compiler_params=params(),
        cost_estimate=cost(6),
        name="attend",
    )(info, packed, packed, packed, table)


def attend_back_body(
    block_rows, scale, q_ref, k_ref, v_ref, weight_ref, grad_ref, packed_ref, table_ref
):
    for side in range(2):
        table_ref[side] = jnp.zeros(table_ref.shape[1:], F32)

    def one(number, carry):
        here = pl.ds(pl.multiple_of(number * block_rows, 16), block_rows)
        queries = halves(q_ref[here, :])
        keys = halves(k_ref[here, :])
        grads = halves(grad_ref[here, :])
        values = v_ref[here, :]
        dq = dk = dv = 0.0
        for side in range(2):
            weights = weight_ref[side, number]
            up = nt(grads[side], values)
            inner = jnp.sum(weights * up, axis=1, keepdims=True)
            score = (weights * (up - inner)).astype(BF16)
            dv += tn(weights.astype(BF16), grads[side])
            dq += nn(score, keys[side])
            dk += tn(score, queries[side])
            table_ref[side, :, :block_rows] += score.astype(F32)
        packed_ref[0, here, :] = (dq * scale).astype(BF16)
        packed_ref[1, here, :] = dk.astype(BF16)
        packed_ref[2, here, :] = dv.astype(BF16)
        return carry

    lax.fori_loop(0, IMGS, one, 0, unroll=True)


def attend_back(packed, weights, mixed_grad, head_dim, lanes):
    rows, three = packed.shape
    pairs = three // (3 * 128)
    heads, _, block_rows, _ = weights.shape
    part = pl.BlockSpec((rows, 128), lambda p: (0, p))
    return pl.pallas_call(
        functools.partial(attend_back_body, block_rows, head_dim**-0.5),
        grid=(pairs,),
        in_specs=[
            part,
            pl.BlockSpec((rows, 128), lambda p: (0, pairs + p)),
            pl.BlockSpec((rows, 128), lambda p: (0, 2 * pairs + p)),
            pl.BlockSpec((2, IMGS, block_rows, block_rows), lambda p: (p, 0, 0, 0)),
            part,
        ],
        out_specs=[
            pl.BlockSpec((3, rows, 128), lambda p: (0, 0, p)),
            pl.BlockSpec((2, block_rows, lanes), lambda p: (p, 0, 0)),
        ],
        out_shape=[
            jax.ShapeDtypeStruct((3, rows, pairs * 128), BF16),
            jax.ShapeDtypeStruct((heads, block_rows, lanes), F32),
        ],
        compiler_params=params(),
        cost_estimate=cost(8),
        name="attend_back",
    )(packed, packed, packed, weights, mixed_grad)


def cumulative(values):
    squared = jnp.exp(-0.5 * values * values)
    size = jnp.abs(values) * ROOT_HALF
    t = 1.0 / (1.0 + 0.3275911 * size)
    poly = t * (
        0.254829592 + t * (-0.284496736 + t * (1.421413741 + t * (-1.453152027 + t * 1.061405429)))
    )
    tail = 0.5 * poly * squared
    return jnp.where(values < 0, tail, 1.0 - tail), squared * INV_ROOT_TAU


def normal(values):
    average = jnp.mean(values, axis=-1, keepdims=True)
    centred = values - average
    inverse = lax.rsqrt(jnp.mean(centred * centred, axis=-1, keepdims=True) + EPS)
    return centred * inverse, inverse


def column_sum(ref, row, values):
    ref[row : row + 1, :] = jnp.sum(values, axis=0, keepdims=True)


class Late:
    def __init__(self, sources, targets, sems):
        self.copies = [
            pltpu.make_async_copy(source, target, sems.at[number])
            for number, (source, target) in enumerate(zip(sources, targets, strict=True))
        ]

    def start(self):
        for copy in self.copies:
            copy.start()

    def wait(self):
        for copy in self.copies:
            copy.wait()


def feed_body(
    image,
    block_rows,
    out_at,
    info,
    order_ref,
    low_ref,
    low_t_ref,
    up_ref,
    up_t_ref,
    vec_ref,
    bias_ref,
    fc1_ref,
    fc2_ref,
    cb_any,
    mixed_any,
    after_any,
    branch_any,
    out_w_any,
    out_ref,
    keep_ref,
    send_ref,
    fc1_sum_ref,
    mixed_grad_ref,
    after_grad_ref,
    sums_ref,
    ff_s,
    second_s,
    cb_s,
    mixed_s,
    after_s,
    branch_s,
    out_w_s,
    sems,
):
    step = pl.program_id(0)
    last = pl.num_programs(0) - 1
    rows, width = low_ref.shape
    late = Late(
        (cb_any, mixed_any, after_any, branch_any, out_w_any.at[:, pl.ds(out_at, width)]),
        (cb_s, mixed_s, after_s, branch_s, out_w_s),
        sems,
    )

    def put_grads(columns, values):
        half = keep_ref.shape[0]
        keep_ref[:, columns] = values[:half].astype(BF16)
        send_ref[:, columns] = values[half:].astype(BF16)

    @pl.when(step == 0)
    def _():
        late.start()
        ff_s[...] = jnp.zeros_like(ff_s)
        second_s[...] = jnp.zeros_like(second_s)

    @pl.when(step < last)
    def _():
        pre = nn(low_ref[...], fc1_ref[...]) + bias_ref[0:1, :]
        phi, density = cumulative(pre)
        hidden = (pre * phi).astype(BF16)
        slope = phi + pre * density
        grad = (nn(up_ref[...], fc2_ref[...]) * slope).astype(BF16)
        ff_s[...] += nt(hidden, fc2_ref[...])
        second_s[...] += nt(grad, fc1_ref[...])
        tile = fc1_ref.shape[1]
        put_grads(slice(0, tile), nn(low_t_ref[...], grad))
        put_grads(slice(tile, 2 * tile), nn(up_t_ref[...], hidden))
        fc1_sum_ref[...] = jnp.broadcast_to(
            jnp.sum(grad.astype(F32), axis=0, keepdims=True), fc1_sum_ref.shape
        )

    @pl.when(step == last)
    def _():
        late.wait()
        cot = cb_s[...].astype(F32)
        sums_ref[...] = jnp.zeros_like(sums_ref)
        normed, inverse = normal(after_s[...])
        second = second_s[...]
        column_sum(sums_ref, G_LN2_G, second * normed)
        column_sum(sums_ref, G_LN2_B, second)
        scaled = second * vec_ref[LN2_G : LN2_G + 1, :]
        inner = jnp.mean(scaled, axis=-1, keepdims=True)
        along = jnp.mean(scaled * normed, axis=-1, keepdims=True)
        after_grad = cot + inverse * (scaled - inner - normed * along)
        after_grad_ref[...] = after_grad
        column_sum(sums_ref, G_GAM_A, after_grad * branch_s[...])
        low = (vec_ref[GAM_A : GAM_A + 1, :] * after_grad).astype(BF16)
        column_sum(sums_ref, G_OUT_B, low.astype(F32))
        mixed_grad_ref[...] = nn(low, out_w_s[...]).astype(BF16)
        turned = nt(row_order(order_ref[...]), low).astype(BF16)
        put_grads(slice(0, width), nn(turned, mixed_s[...]))
        rest = keep_ref.shape[1] - width
        put_grads(slice(width, width + rest), jnp.zeros((width, rest), F32))
        branch = ff_s[...] + vec_ref[FC2_B : FC2_B + 1, :]
        result = (after_s[...] + vec_ref[GAM_M : GAM_M + 1, :] * branch).astype(BF16)
        out_ref[...] = restore_rows(info[0], result, block_rows, image, out_ref.shape[0]).astype(
            BF16
        )
        column_sum(sums_ref, G_GAM_M, cot * branch)
        column_sum(sums_ref, G_FC2_B, up_ref[...].astype(F32))


def feed(
    info,
    order,
    low,
    low_t,
    up,
    up_t,
    vec,
    fc1b,
    weights,
    cb,
    mixed,
    after_attn,
    branch,
    image,
    block_rows,
    length,
    tile,
):
    rows, width = low.shape
    hidden = fc1b.shape[1]
    steps = hidden // tile
    anywhere = pl.BlockSpec(memory_space=pl.ANY)
    once = pl.Buffered(1)

    def at(i):
        return jnp.minimum(i, steps - 1)

    def fixed(shape):
        return pl.BlockSpec(shape, lambda i: (0, 0), pipeline_mode=once)

    return pl.pallas_call(
        functools.partial(feed_body, image, block_rows, 2 * hidden),
        grid=(steps + 1,),
        in_specs=[
            smem(),
            fixed((width, 1)),
            fixed((rows, width)),
            fixed((width, rows)),
            fixed((rows, width)),
            fixed((width, rows)),
            fixed(vec.shape),
            pl.BlockSpec((8, tile), lambda i: (0, at(i))),
            pl.BlockSpec((width, tile), lambda i: (0, at(i))),
            pl.BlockSpec((width, tile), lambda i: (0, steps + at(i))),
        ]
        + [anywhere] * 5,
        out_specs=[
            full((length, width)),
            pl.BlockSpec((width // 2, 2 * tile), lambda i: (0, i)),
            pl.BlockSpec((width // 2, 2 * tile), lambda i: (0, i)),
            pl.BlockSpec((8, tile), lambda i: (0, at(i))),
            full((rows, width)),
            full((rows, width)),
            full((16, width)),
        ],
        out_shape=[
            jax.ShapeDtypeStruct((length, width), BF16),
            jax.ShapeDtypeStruct((width // 2, 2 * hidden + width), BF16),
            jax.ShapeDtypeStruct((width // 2, 2 * hidden + width), BF16),
            jax.ShapeDtypeStruct((8, hidden), F32),
            jax.ShapeDtypeStruct((rows, width), BF16),
            jax.ShapeDtypeStruct((rows, width), F32),
            jax.ShapeDtypeStruct((16, width), F32),
        ],
        scratch_shapes=[
            pltpu.VMEM((rows, width), F32),
            pltpu.VMEM((rows, width), F32),
            pltpu.VMEM((rows, width), BF16),
            pltpu.VMEM((rows, width), BF16),
            pltpu.VMEM((rows, width), F32),
            pltpu.VMEM((rows, width), F32),
            pltpu.VMEM((width, width), BF16),
            pltpu.SemaphoreType.DMA((5,)),
        ],
        compiler_params=params(),
        cost_estimate=cost(28),
        name="feed",
    )(
        info,
        order,
        low,
        low_t,
        up,
        up_t,
        vec,
        fc1b,
        weights,
        weights,
        cb,
        mixed,
        after_attn,
        branch,
        weights,
    )


def weight_grad_body(low_t_ref, packed_ref, keep_ref, send_ref):
    half = keep_ref.shape[0]
    keep_ref[...] = nn(low_t_ref[:half], packed_ref[...]).astype(BF16)
    send_ref[...] = nn(low_t_ref[half:], packed_ref[...]).astype(BF16)


def weight_grad(low_t, packed_grad):
    width, rows = low_t.shape
    return pl.pallas_call(
        weight_grad_body,
        grid=(3,),
        in_specs=[full((width, rows)), pl.BlockSpec((None, rows, width), lambda i: (i, 0, 0))],
        out_specs=[pl.BlockSpec((width // 2, width), lambda i: (0, i))] * 2,
        out_shape=[jax.ShapeDtypeStruct((width // 2, 3 * width), BF16)] * 2,
        compiler_params=params(),
        cost_estimate=cost(5),
        name="weight_grad",
    )(low_t, packed_grad)


def input_grad_body(
    image,
    block_rows,
    info,
    packed_ref,
    weight_ref,
    vec_ref,
    normed_any,
    inv_any,
    after_grad_any,
    out_ref,
    sums_ref,
    first_s,
    normed_s,
    inv_s,
    after_grad_s,
    sems,
):
    step = pl.program_id(0)
    late = Late((normed_any, inv_any, after_grad_any), (normed_s, inv_s, after_grad_s), sems)

    @pl.when(step == 0)
    def _():
        late.start()
        first_s[...] = jnp.zeros_like(first_s)
        sums_ref[...] = jnp.zeros_like(sums_ref)
        column_sum(sums_ref, G_Q_B, packed_ref[...].astype(F32))

    first_s[...] += nt(packed_ref[...], weight_ref[...])

    @pl.when(step == 2)
    def _():
        late.wait()
        column_sum(sums_ref, G_V_B, packed_ref[...].astype(F32))
        first = first_s[...]
        normed = normed_s[...]
        column_sum(sums_ref, G_LN1_G, first * normed)
        column_sum(sums_ref, G_LN1_B, first)
        scaled = first * vec_ref[LN1_G : LN1_G + 1, :]
        inner = jnp.mean(scaled, axis=-1, keepdims=True)
        along = jnp.mean(scaled * normed, axis=-1, keepdims=True)
        back = inv_s[:, :1] * (scaled - inner - normed * along)
        result = (after_grad_s[...] + back).astype(BF16)
        out_ref[...] = restore_rows(info[0], result, block_rows, image, out_ref.shape[0]).astype(
            BF16
        )


def input_grad(info, packed_grad, weights, vec, normed, inv, after_grad, image, block_rows, length):
    rows, width = normed.shape
    anywhere = pl.BlockSpec(memory_space=pl.ANY)
    return pl.pallas_call(
        functools.partial(input_grad_body, image, block_rows),
        grid=(3,),
        in_specs=[
            smem(),
            pl.BlockSpec((None, rows, width), lambda i: (i, 0, 0)),
            pl.BlockSpec((width, width), lambda i: (0, i)),
            full(vec.shape),
            anywhere,
            anywhere,
            anywhere,
        ],
        out_specs=[full((length, width)), full((16, width))],
        out_shape=[
            jax.ShapeDtypeStruct((length, width), BF16),
            jax.ShapeDtypeStruct((16, width), F32),
        ],
        scratch_shapes=[
            pltpu.VMEM((rows, width), F32),
            pltpu.VMEM((rows, width), F32),
            pltpu.VMEM((rows, 128), F32),
            pltpu.VMEM((rows, width), F32),
            pltpu.SemaphoreType.DMA((3,)),
        ],
        compiler_params=params(),
        cost_estimate=cost(8),
        name="input_grad",
    )(info, packed_grad, weights, vec, normed, inv, after_grad)


def table_grad_body(heads, groups, table_ref, index_ref, out_ref, acc):
    lanes = index_ref.shape[1]
    parts = out_ref.shape[1] // 128
    acc[...] = jnp.zeros_like(acc)
    slots = lax.broadcasted_iota(jnp.int32, (128, lanes), 0).astype(F32).astype(BF16)
    one_bf, zero_bf = jnp.ones((), BF16), jnp.zeros((), BF16)
    zero = jnp.zeros((), BF16)
    group = 8

    def one(step, carry):
        at = pl.ds(pl.multiple_of(step * group, group), group)
        indices = index_ref[at, :]
        lows = jnp.bitwise_and(indices, 127).astype(F32)
        highs = jnp.right_shift(indices, 7).astype(F32)
        values = table_ref[:, at, :]
        left, right = [], []
        for row in range(group):
            low = jnp.broadcast_to(lows[row : row + 1, :], (16, lanes)).astype(BF16)
            high = jnp.broadcast_to(highs[row : row + 1, :], (16, lanes)).astype(BF16)
            right.append(
                jnp.concatenate(
                    [
                        jnp.where(slots[start : start + 16] == low, one_bf, zero_bf)
                        for start in range(0, 128, 16)
                    ],
                    axis=0,
                )
            )
            here = jnp.concatenate(
                [values[:, row, :], jnp.zeros((16 - heads, lanes), F32)], axis=0
            )
            coarse = here.astype(BF16)
            fine = (here - coarse.astype(F32)).astype(BF16)
            masks = [high == jnp.asarray(part, BF16) for part in range(parts)]
            left.append(
                jnp.concatenate(
                    [jnp.where(mask, kind, zero) for kind in (coarse, fine) for mask in masks],
                    axis=0,
                )
            )
        acc[...] += nt(jnp.concatenate(left, axis=1), jnp.concatenate(right, axis=1))
        return carry

    lax.fori_loop(groups[0], groups[1], one, 0)
    half = parts * 16
    for part in range(parts):
        out_ref[:, part * 128 : (part + 1) * 128] = (
            acc[part * 16 : (part + 1) * 16, :] + acc[half + part * 16 : half + (part + 1) * 16, :]
        )


def table_grad(table, index, slots, groups):
    heads, length, lanes = table.shape
    return pl.pallas_call(
        functools.partial(table_grad_body, heads, groups),
        grid=(1,),
        in_specs=[full(table.shape), full(index.shape)],
        out_specs=full((16, slots)),
        out_shape=jax.ShapeDtypeStruct((16, slots), F32),
        scratch_shapes=[pltpu.VMEM((2 * 16 * slots // 128, 128), F32)],
        compiler_params=params(),
        cost_estimate=cost(8),
        name="table_grad",
    )(table, index)


def local(
    inputs,
    cotangent,
    segment_ids,
    keep_rows,
    index_map,
    ln1_gain,
    ln1_bias,
    qkv_weight,
    qv_bias,
    out_weight,
    out_bias,
    gamma_attn,
    rel_table,
    ln2_gain,
    ln2_bias,
    fc1_weight,
    fc1_bias,
    fc2_weight,
    fc2_bias,
    gamma_mlp,
):
    _, length, width = inputs.shape
    heads, per_device = rel_table.shape
    head_dim = width // heads
    own = ln1_gain.shape[0]
    count = width // own
    hidden = fc1_weight.shape[1]
    image = index_map.shape[0]
    block_rows = -(-image // 16) * 16

    keep = keep_rows[0] == 1
    ids = lax.iota(jnp.int32, length)
    info = jnp.stack([jnp.min(jnp.where(keep, ids, length)), jnp.max(jnp.where(keep, 0, 1))])
    moved = index_map // per_device * own + index_map % per_device
    moved = jnp.pad(moved, ((0, block_rows - image), (0, 256 - image)), constant_values=-1)

    small_rows = [
        ln1_gain[None],
        ln1_bias[None],
        qv_bias,
        out_bias[None],
        gamma_attn[None],
        ln2_gain[None],
        ln2_bias[None],
        fc2_bias[None],
        gamma_mlp[None],
    ]
    owners = exchange_owners(count)
    order = (owners[:, None] * own + jnp.arange(own, dtype=jnp.int32)).reshape(-1, 1)
    later = lax.all_gather(
        jnp.concatenate([fc1_weight, fc2_weight.T, out_weight.T], axis=1), AX, axis=0, tiled=True
    )
    xb, cb, normed, inv = prepare(info, inputs[0], cotangent[0], image, block_rows)
    small = pack(small_rows, fc1_bias[None], rel_table, FC1_B, TABLE, hidden // width)
    small = jnp.broadcast_to(after(small, xb)[None], (count, own, SMALL))
    small = lax.all_to_all(small, AX, 0, 0, tiled=True).reshape(width, SMALL)
    vec, fc1b, table = expand(small, moved, heads, hidden)
    mine, got = gather_halves(qkv_weight, count, [(xb,), (small,), (table,)])
    packed, low, qkv_full = project(owners, normed, vec, mine, got, head_dim)
    qkv_full = qkv_full.reshape(width, -1)
    mixed, weights = attend(info, packed, table, block_rows)
    up, up_t, low_t = turn(order, vec, after(cb, mixed), low)
    branch, after_attn, low2, low2_t = combine(
        order, mixed, after(xb, up), vec, later, 2 * hidden
    )
    tile = 512
    out, feed_keep, feed_send, fc1_sum, mixed_grad, after_grad, sums2 = feed(
        info,
        order,
        low2,
        low2_t,
        up,
        up_t,
        vec,
        fc1b,
        later,
        cb,
        mixed,
        after_attn,
        branch,
        image,
        block_rows,
        length,
        tile,
    )
    packed_grad, table_sum = attend_back(packed, weights, mixed_grad, head_dim, 256)
    a_keep, a_send = scatter_step(feed_keep, feed_send, 0, count, packed_grad)
    qkv_keep, qkv_send = weight_grad(after(low_t, a_send), packed_grad)
    in_grad, sums1 = input_grad(
        info,
        packed_grad,
        qkv_full,
        vec,
        normed,
        after(inv, qkv_keep),
        after_grad,
        image,
        block_rows,
        length,
    )
    groups = -(-image // 8)
    slots = own * count
    b_keep, b_send = scatter_step(qkv_keep, qkv_send, 0, count, in_grad)
    slot_sums = table_grad(after(table_sum, b_send), moved, slots, (0, groups // 2))
    a_keep, a_send = scatter_step(a_keep, a_send, 1, count, slot_sums)
    more_sums = table_grad(after(table_sum, a_send), moved, slots, (groups // 2, groups))
    b_keep, b_send = scatter_step(b_keep, b_send, 1, count, more_sums)
    a_keep, a_send = scatter_step(a_keep, a_send, 2, count, b_send)
    slot_sums = slot_sums + after(more_sums, a_send)

    rows = jnp.concatenate([sums1[:10] + sums2[:10], slot_sums[:heads]], axis=0)
    rows = jnp.transpose(rows.reshape(-1, count, own), (1, 0, 2))
    biases = fc1_sum[0].reshape(count, -1, own)
    swapped = lax.all_to_all(jnp.concatenate([rows, biases], axis=1), AX, 0, 0, tiled=True)
    b_keep, b_send = scatter_step(b_keep, b_send, 2, count, swapped)
    for step in range(3, count.bit_length() - 1):
        a_keep, a_send = scatter_step(a_keep, a_send, step, count, b_keep)
        b_keep, b_send = scatter_step(b_keep, b_send, step, count, a_keep)
    feed_wide, qkv_shard = a_keep, b_keep
    small_shard = jnp.sum(swapped, axis=0)

    pieces = feed_wide[:, : 2 * hidden].reshape(own, hidden // tile, 2, tile)
    grad_fc1 = pieces[:, :, 0].reshape(own, hidden)
    grad_fc2 = pieces[:, :, 1].reshape(own, hidden).T
    grad_out = feed_wide[:, 2 * hidden :].T
    grad_table = small_shard[10 : 10 + heads, :per_device]
    grad_fc1_bias = small_shard[10 + heads :].reshape(-1)
    return (
        out[None],
        in_grad[None],
        small_shard[G_LN1_G],
        small_shard[G_LN1_B],
        qkv_shard,
        small_shard[G_Q_B : G_V_B + 1],
        grad_out,
        small_shard[G_OUT_B],
        small_shard[G_GAM_A],
        grad_table,
        small_shard[G_LN2_G],
        small_shard[G_LN2_B],
        grad_fc1,
        grad_fc1_bias,
        grad_fc2,
        small_shard[G_FC2_B],
        small_shard[G_GAM_M],
    )


def solution(mesh):
    rows = P(AX)
    columns = P(None, AX)
    return jax.shard_map(
        local,
        mesh=mesh,
        in_specs=(
            rows,
            rows,
            rows,
            rows,
            P(),
            rows,
            rows,
            rows,
            columns,
            columns,
            rows,
            rows,
            columns,
            rows,
            rows,
            rows,
            rows,
            columns,
            rows,
            rows,
        ),
        out_specs=(
            rows,
            rows,
            rows,
            rows,
            rows,
            columns,
            columns,
            rows,
            rows,
            columns,
            rows,
            rows,
            rows,
            rows,
            columns,
            rows,
            rows,
        ),
        check_vma=False,
    )
```

```python
import functools
import jax
import jax.numpy as jnp
from jax import lax
from jax.experimental import pallas as pl
from jax.experimental.pallas import tpu as pltpu
from jax.sharding import PartitionSpec as P

AX = ("dp", "fsdp")
IMGS = 4
EPS = 1e-06
MASKED = -1e30
ROOT_HALF = 0.7071067811865476
INV_ROOT_TAU = 0.3989422804014327
F32 = jnp.float32
BF16 = jnp.bfloat16
VMEM_LIMIT = 60 * 1024 * 1024

LN1_G, LN1_B, Q_B, V_B, OUT_B, GAM_A, LN2_G, LN2_B, FC2_B, GAM_M = range(10)
FC1_B = 16
TABLE = 32
SMALL = 128
G_LN1_G, G_LN1_B, G_Q_B, G_V_B, G_OUT_B, G_GAM_A, G_LN2_G, G_LN2_B, G_FC2_B, G_GAM_M = range(10)


def nn(a, b):
    return lax.dot_general(a, b, (((1,), (0,)), ((), ())), preferred_element_type=F32)


def nt(a, b):
    return lax.dot_general(a, b, (((1,), (1,)), ((), ())), preferred_element_type=F32)


def tn(a, b):
    return lax.dot_general(a, b, (((0,), (0,)), ((), ())), preferred_element_type=F32)


def full(shape):
    return pl.BlockSpec(shape, lambda *_: (0,) * len(shape))


def cost(gigaflops, megabytes=4):
    return pl.CostEstimate(
        flops=int(gigaflops * 2e7), bytes_accessed=int(megabytes * 2e4), transcendentals=0
    )


def after(value, *others):
    return lax.optimization_barrier((value, others))[0]


def params(grid_rank=1):
    return pltpu.CompilerParams(
        dimension_semantics=("arbitrary",) * grid_rank, vmem_limit_bytes=VMEM_LIMIT
    )


def smem():
    return pl.BlockSpec(memory_space=pltpu.SMEM)


def exchange_orders(count):
    bits = count.bit_length() - 1
    if bits < 3:
        return (list(range(bits)),) * 2
    rest = list(range(2, bits - 1))
    return [0, 1, bits - 1] + rest, [0, bits - 1, 1] + rest[::-1]

def exchange(values, step, count):
    orders = exchange_orders(count)
    return lax.ppermute(values, AX, [(i, i ^ (1 << orders[i & 1][step])) for i in range(count)])


def exchange_owners(count):
    orders = exchange_orders(count)
    bits = len(orders[0])
    me = lax.axis_index(AX)
    spot = jnp.arange(count, dtype=jnp.int32)
    other = spot >> (bits - 1) if bits else spot
    kind = jnp.bitwise_xor(jnp.bitwise_and(me, 1), other)
    flips = other
    for step in range(1, bits):
        bit = jnp.bitwise_and(spot >> (bits - 1 - step), 1)
        flips = jnp.bitwise_or(
            flips, bit << jnp.where(kind == 1, orders[1][step], orders[0][step])
        )
    return jnp.bitwise_xor(me, flips)


def gather_halves(values, count, before):
    for number, step in enumerate(reversed(range(count.bit_length() - 1))):
        got = exchange(values, step, count)
        if number < len(before):
            got = after(got, *before[number])
        if step == 0:
            return values, got
        values = jnp.concatenate([values, got], axis=0)
    half = values.shape[0] // 2
    return values[:half], values[half:]


def scatter_step(pieces, send, step, count, *others):
    got = after(exchange(send, step, count), *others)
    pieces = pieces + [got]
    rows = got.shape[0]
    if step == count.bit_length() - 2:
        return sum(piece[:rows].astype(F32) for piece in pieces), None
    send = sum(piece[rows // 2 : rows].astype(F32) for piece in pieces).astype(BF16)
    return pieces, send


def in_chunks(rows, size, body):
    def one(number, carry):
        body(pl.ds(pl.multiple_of(number * size, 16), size))
        return carry

    lax.fori_loop(0, rows // size, one, 0)


def row_order(column, width):
    rows = column.shape[0]
    return (lax.broadcasted_iota(jnp.int32, (rows, width), 1) == column).astype(BF16)


def block_source(first, number, rows, image, length):
    at = first + image * number + rows
    at = jnp.where(at >= length, at - length, at)
    return jnp.where(rows < image, at, -1)


def place_rows(first, source, target_rows, image):
    length = source.shape[0]

    def one(number):
        rows = lax.broadcasted_iota(jnp.int32, (target_rows, 1), 0)
        wanted = block_source(first, number, rows, image, length)
        columns = lax.broadcasted_iota(jnp.int32, (target_rows, length), 1)
        return nn((columns == wanted).astype(BF16), source)

    return one


def restore_rows(first, blocked, block_rows, image, length):
    lanes = lax.broadcasted_iota(jnp.int32, (1, block_rows), 1)
    wanted = jnp.concatenate(
        [block_source(first, number, lanes, image, length) for number in range(IMGS)], axis=1
    )
    rows = lax.broadcasted_iota(jnp.int32, (length, IMGS * block_rows), 0)
    return nn((rows == wanted).astype(BF16), blocked)


def pack_body(bias_at, table_at, ratio, bias_ref, table_ref, *rest):
    *row_refs, out_ref, rows_s = rest
    own = out_ref.shape[0]
    rows_s[...] = jnp.zeros_like(rows_s)
    at_row = 0
    for ref in row_refs:
        rows_s[at_row : at_row + ref.shape[0], :] = ref[...].astype(F32)
        at_row += ref.shape[0]
    heads, slots = table_ref.shape
    rows_s[table_at : table_at + heads, :slots] = table_ref[...].astype(F32)
    eye = (
        lax.broadcasted_iota(jnp.int32, (own, own), 0)
        == lax.broadcasted_iota(jnp.int32, (own, own), 1)
    ).astype(BF16)
    small = nt(eye, rows_s[...].astype(BF16))
    biases = jnp.broadcast_to(bias_ref[...].astype(F32), (own, own * ratio))
    at = lax.broadcasted_iota(jnp.int32, (own, own * ratio), 1)
    row = lax.broadcasted_iota(jnp.int32, (own, own * ratio), 0)
    lane = lax.broadcasted_iota(jnp.int32, (own, SMALL), 1)
    for number in range(ratio):
        column = jnp.sum(
            jnp.where(at == row * ratio + number, biases, 0.0), axis=1, keepdims=True
        )
        small = small + jnp.where(lane == bias_at + number, column, 0.0)
    out_ref[...] = small.astype(BF16)


def pack(rows, bias, table, bias_at, table_at, ratio):
    own = rows[0].shape[1]
    operands = (bias, table, *rows)
    return pl.pallas_call(
        functools.partial(pack_body, bias_at, table_at, ratio),
        grid=(1,),
        in_specs=[full(value.shape) for value in operands],
        out_specs=full((own, SMALL)),
        out_shape=jax.ShapeDtypeStruct((own, SMALL), BF16),
        scratch_shapes=[pltpu.VMEM((SMALL, own), F32)],
        compiler_params=params(),
        name="pack",
    )(*operands)


def prepare_body(image, block_rows, info, x_ref, cot_ref, xb_ref, cb_ref, normed_ref, inv_ref):
    first = info[0]

    def one(number, carry):
        here = pl.ds(pl.multiple_of(number * block_rows, 16), block_rows)
        values = place_rows(first, x_ref[...], block_rows, image)(number)
        xb_ref[here, :] = values.astype(BF16)
        normed, inverse = normal(values)
        normed_ref[here, :] = normed
        inv_ref[here, :] = jnp.broadcast_to(inverse, (block_rows, 128))
        cb_ref[here, :] = place_rows(first, cot_ref[...], block_rows, image)(number).astype(BF16)
        return carry

    lax.fori_loop(0, IMGS, one, 0)


def prepare(info, x, cot, image, block_rows):
    length, width = x.shape
    rows = IMGS * block_rows
    return pl.pallas_call(
        functools.partial(prepare_body, image, block_rows),
        grid=(1,),
        in_specs=[smem(), full((length, width)), full((length, width))],
        out_specs=[full((rows, width))] * 3 + [full((rows, 128))],
        out_shape=[
            jax.ShapeDtypeStruct((rows, width), BF16),
            jax.ShapeDtypeStruct((rows, width), BF16),
            jax.ShapeDtypeStruct((rows, width), F32),
            jax.ShapeDtypeStruct((rows, 128), F32),
        ],
        compiler_params=params(),
        cost_estimate=cost(4),
        name="prepare",
    )(info, x, cot)


def expand_body(heads, small_ref, index_ref, vec_ref, fc1b_ref, table_ref, entries_s):
    eye = (
        lax.broadcasted_iota(jnp.int32, (SMALL, SMALL), 0)
        == lax.broadcasted_iota(jnp.int32, (SMALL, SMALL), 1)
    ).astype(BF16)
    width = small_ref.shape[0]
    hidden = fc1b_ref.shape[1]
    ratio = hidden // width
    rows = nt(eye, small_ref[...])
    vec_ref[...] = rows[: vec_ref.shape[0]]
    spread = (
        lax.broadcasted_iota(jnp.int32, (width, hidden), 0)
        == lax.broadcasted_iota(jnp.int32, (width, hidden), 1) // ratio
    ).astype(BF16)
    wide = nn(rows[FC1_B : FC1_B + 8].astype(BF16), spread)
    which = lax.broadcasted_iota(jnp.int32, (8, hidden), 1) % ratio
    mine = lax.broadcasted_iota(jnp.int32, (8, hidden), 0)
    total = jnp.sum(jnp.where(which == mine, wide, 0.0), axis=0, keepdims=True)
    fc1b_ref[...] = jnp.broadcast_to(total, fc1b_ref.shape)
    length, lanes = index_ref.shape
    parts = width // 128
    for head in range(heads):
        for part in range(parts):
            entries_s[head * parts + part] = jnp.broadcast_to(
                rows[TABLE + head : TABLE + head + 1, part * 128 : (part + 1) * 128], (8, 128)
            )

    def one(step, carry):
        at = pl.ds(pl.multiple_of(step * 8, 8), 8)
        for half in range(lanes // 128):
            columns = slice(half * 128, (half + 1) * 128)
            index = index_ref[at, columns]
            low = jnp.bitwise_and(index, 127)
            high = jnp.right_shift(index, 7)
            found = [jnp.full((8, 128), MASKED, F32)] * heads
            for part in range(parts):
                chosen = high == part
                for head in range(heads):
                    taken = jnp.take_along_axis(
                        entries_s[head * parts + part], low, axis=1, mode="promise_in_bounds"
                    )
                    found[head] = jnp.where(chosen, taken, found[head])
            for head in range(heads):
                table_ref[head, at, columns] = found[head]
        return carry

    lax.fori_loop(0, length // 8, one, 0)


def expand(small, index, heads, hidden):
    width = small.shape[0]
    length, lanes = index.shape
    return pl.pallas_call(
        functools.partial(expand_body, heads),
        grid=(1,),
        in_specs=[
            full((width, SMALL)),
            full((length, lanes)),
        ],
        out_specs=[full((64, width)), full((8, hidden)), full((heads, length, lanes))],
        out_shape=[
            jax.ShapeDtypeStruct((64, width), F32),
            jax.ShapeDtypeStruct((8, hidden), F32),
            jax.ShapeDtypeStruct((heads, length, lanes), F32),
        ],
        scratch_shapes=[pltpu.VMEM((heads * width // 128, 8, 128), F32)],
        compiler_params=params(),
        cost_estimate=cost(5),
        name="expand",
    )(small, index)


def project_body(
    scale,
    owners,
    normed_ref,
    vec_ref,
    mine_any,
    got_any,
    packed_ref,
    low_ref,
    weight_any,
    weight_s,
    sems,
    out_sem,
):
    step = pl.program_id(0)
    half = mine_any.shape[0]
    width = normed_ref.shape[1]
    keeping = pltpu.make_async_copy(weight_s, weight_any, out_sem)

    @pl.when(step == 0)
    def _():
        copies = []
        for spot in range(2 * half):
            source = mine_any.at[spot] if spot < half else got_any.at[spot - half]
            copy = pltpu.make_async_copy(source, weight_s.at[owners[spot]], sems.at[spot])
            copy.start()
            copies.append(copy)
        low_ref[...] = (
            normed_ref[...] * vec_ref[LN1_G : LN1_G + 1, :] + vec_ref[LN1_B : LN1_B + 1, :]
        ).astype(BF16)
        for copy in copies:
            copy.wait()
        keeping.start()

    bias = jnp.where(
        step == 0,
        vec_ref[Q_B : Q_B + 1, :],
        jnp.where(step == 2, vec_ref[V_B : V_B + 1, :], 0.0),
    )
    columns = pl.ds(pl.multiple_of(step * width, 128), width)
    weight = weight_s[:, :, columns].reshape(width, width)
    result = (nn(low_ref[...], weight) + bias).astype(BF16)
    packed_ref[...] = (result.astype(F32) * jnp.where(step == 0, scale, 1.0)).astype(BF16)

    @pl.when(step == 2)
    def _():
        keeping.wait()


def project(owners, normed, vec, mine, got, head_dim):
    rows, width = normed.shape
    count = owners.shape[0]
    wide = mine.shape[1]
    own = width // count
    anywhere = pl.BlockSpec(memory_space=pl.ANY)
    half = -(-count // 2)
    return pl.pallas_call(
        functools.partial(project_body, head_dim**-0.5),
        grid=(3,),
        in_specs=[smem(), full((rows, width)), full(vec.shape), anywhere, anywhere],
        out_specs=[
            pl.BlockSpec((rows, width), lambda i: (0, i)),
            full((rows, width)),
            anywhere,
        ],
        out_shape=[
            jax.ShapeDtypeStruct((rows, wide), BF16),
            jax.ShapeDtypeStruct((rows, width), BF16),
            jax.ShapeDtypeStruct((count, own, wide), BF16),
        ],
        scratch_shapes=[
            pltpu.VMEM((count, own, wide), BF16),
            pltpu.SemaphoreType.DMA((2 * half,)),
            pltpu.SemaphoreType.DMA,
        ],
        compiler_params=params(),
        cost_estimate=cost(4),
        name="project",
    )(owners, normed, vec, mine.reshape(half, own, wide), got.reshape(half, own, wide))


def turn_body(order_ref, vec_ref, cb_ref, low_ref, up_ref, up_t_ref, low_t_ref):
    up = (vec_ref[GAM_M : GAM_M + 1, :] * cb_ref[...].astype(F32)).astype(BF16)
    up_ref[...] = up
    width = low_ref.shape[1]

    def turned(here):
        order = row_order(order_ref[here, :], width)
        up_t_ref[here, :] = nt(order, up_ref[...]).astype(BF16)
        low_t_ref[here, :] = nt(order, low_ref[...]).astype(BF16)

    in_chunks(width, width // 2, turned)


def turn(order, vec, cb, low):
    rows, width = cb.shape
    return pl.pallas_call(
        turn_body,
        grid=(1,),
        in_specs=[full((width, 1)), full(vec.shape), full((rows, width)), full((rows, width))],
        out_specs=[full((rows, width)), full((width, rows)), full((width, rows))],
        out_shape=[
            jax.ShapeDtypeStruct((rows, width), BF16),
            jax.ShapeDtypeStruct((width, rows), BF16),
            jax.ShapeDtypeStruct((width, rows), BF16),
        ],
        compiler_params=params(),
        cost_estimate=cost(3),
        name="turn",
    )(order, vec, cb, low)


def halves(values):
    lanes = lax.broadcasted_iota(jnp.int32, values.shape, 1)
    zero = jnp.zeros((), values.dtype)
    side = values.shape[1] // 2
    return (jnp.where(lanes < side, values, zero), jnp.where(lanes >= side, values, zero))


def attend_body(block_rows, info, q_ref, k_ref, v_ref, table_ref, mixed_ref, weight_ref):
    rows = lax.broadcasted_iota(jnp.int32, (block_rows, block_rows), 0)
    columns = lax.broadcasted_iota(jnp.int32, (block_rows, block_rows), 1)
    alone = jnp.where(rows == columns, 0.0, MASKED)

    def one(number, carry):
        padded = jnp.logical_and(info[1] == 1, number == IMGS - 1)
        here = pl.ds(pl.multiple_of(number * block_rows, 16), block_rows)
        queries = halves(q_ref[here, :])
        values = halves(v_ref[here, :])
        keys = k_ref[here, :]
        mixed = None
        for side in range(2):
            bias = jnp.where(padded, alone, table_ref[side, :, :block_rows])
            scores = nt(queries[side], keys) + bias
            raised = jnp.exp(scores - jnp.max(scores, axis=1, keepdims=True))
            weights = raised * (1.0 / jnp.sum(raised, axis=1, keepdims=True))
            weight_ref[side, number] = weights
            part = nn(weights.astype(BF16), values[side])
            mixed = part if mixed is None else mixed + part
        mixed_ref[here, :] = mixed.astype(BF16)
        return carry

    lax.fori_loop(0, IMGS, one, 0, unroll=True)


def attend(info, packed, table, block_rows):
    rows, three = packed.shape
    pairs = three // (3 * 128)
    heads, length, lanes = table.shape
    return pl.pallas_call(
        functools.partial(attend_body, block_rows),
        grid=(pairs,),
        in_specs=[
            smem(),
            pl.BlockSpec((rows, 128), lambda p: (0, p)),
            pl.BlockSpec((rows, 128), lambda p: (0, pairs + p)),
            pl.BlockSpec((rows, 128), lambda p: (0, 2 * pairs + p)),
            pl.BlockSpec((2, length, lanes), lambda p: (p, 0, 0)),
        ],
        out_specs=[
            pl.BlockSpec((rows, 128), lambda p: (0, p)),
            pl.BlockSpec((2, IMGS, block_rows, block_rows), lambda p: (p, 0, 0, 0)),
        ],
        out_shape=[
            jax.ShapeDtypeStruct((rows, pairs * 128), BF16),
            jax.ShapeDtypeStruct((heads, IMGS, block_rows, block_rows), F32),
        ],
        compiler_params=params(),
        cost_estimate=cost(6),
        name="attend",
    )(info, packed, packed, packed, table)


def attend_back_body(block_rows, scale, q_ref, k_ref, v_ref, weight_ref, grad_ref, *rest):
    packed_ref, table_ref = rest[-2:]
    for side in range(2):
        table_ref[side] = jnp.zeros(table_ref.shape[1:], F32)

    def one(number, carry):
        here = pl.ds(pl.multiple_of(number * block_rows, 16), block_rows)
        queries = halves(q_ref[here, :])
        keys = halves(k_ref[here, :])
        grads = halves(grad_ref[here, :])
        values = v_ref[here, :]
        dq = dk = dv = 0.0
        for side in range(2):
            weights = weight_ref[side, number]
            up = nt(grads[side], values)
            inner = jnp.sum(weights * up, axis=1, keepdims=True)
            score = (weights * (up - inner)).astype(BF16)
            dv += tn(weights.astype(BF16), grads[side])
            dq += nn(score, keys[side])
            dk += tn(score, queries[side])
            table_ref[side, :, :block_rows] += score.astype(F32)
        packed_ref[0, here, :] = (dq * scale).astype(BF16)
        packed_ref[1, here, :] = dk.astype(BF16)
        packed_ref[2, here, :] = dv.astype(BF16)
        return carry

    lax.fori_loop(0, IMGS, one, 0, unroll=True)


def attend_back(packed, weights, mixed_grad, head_dim, lanes, first, last, earlier=()):
    rows, three = packed.shape
    pairs = three // (3 * 128)
    heads, _, block_rows, _ = weights.shape
    part = pl.BlockSpec((rows, 128), lambda p: (0, first + p))
    return pl.pallas_call(
        functools.partial(attend_back_body, block_rows, head_dim**-0.5),
        grid=(last - first,),
        in_specs=[
            part,
            pl.BlockSpec((rows, 128), lambda p: (0, pairs + first + p)),
            pl.BlockSpec((rows, 128), lambda p: (0, 2 * pairs + first + p)),
            pl.BlockSpec((2, IMGS, block_rows, block_rows), lambda p: (first + p, 0, 0, 0)),
            part,
        ]
        + [pl.BlockSpec(memory_space=pl.ANY)] * len(earlier),
        out_specs=[
            pl.BlockSpec((3, rows, 128), lambda p: (0, 0, first + p)),
            pl.BlockSpec((2, block_rows, lanes), lambda p: (first + p, 0, 0)),
        ],
        out_shape=[
            jax.ShapeDtypeStruct((3, rows, pairs * 128), BF16),
            jax.ShapeDtypeStruct((heads, block_rows, lanes), F32),
        ],
        input_output_aliases={5: 0, 6: 1} if earlier else {},
        compiler_params=params(),
        cost_estimate=cost(4),
        name="attend_back",
    )(packed, packed, packed, weights, mixed_grad, *earlier)


def cumulative(values):
    squared = jnp.exp(-0.5 * values * values)
    size = jnp.abs(values) * ROOT_HALF
    t = 1.0 / (1.0 + 0.3275911 * size)
    poly = t * (
        0.254829592 + t * (-0.284496736 + t * (1.421413741 + t * (-1.453152027 + t * 1.061405429)))
    )
    tail = 0.5 * poly * squared
    return jnp.where(values < 0, tail, 1.0 - tail), squared * INV_ROOT_TAU


def normal(values):
    average = jnp.mean(values, axis=-1, keepdims=True)
    centred = values - average
    inverse = lax.rsqrt(jnp.mean(centred * centred, axis=-1, keepdims=True) + EPS)
    return centred * inverse, inverse


def column_sum(ref, row, values):
    ref[row : row + 1, :] = jnp.sum(values, axis=0, keepdims=True)


class Late:
    def __init__(self, sources, targets, sems):
        self.copies = [
            pltpu.make_async_copy(source, target, sems.at[number])
            for number, (source, target) in enumerate(zip(sources, targets, strict=True))
        ]

    def start(self):
        for copy in self.copies:
            copy.start()

    def wait(self):
        for copy in self.copies:
            copy.wait()


def feed_body(
    image,
    block_rows,
    info,
    order_ref,
    mixed_ref,
    xb_ref,
    up_ref,
    up_t_ref,
    vec_ref,
    bias_ref,
    out_w_ref,
    fc1_ref,
    fc2_ref,
    cb_any,
    out_ref,
    keep_ref,
    send_ref,
    fc1_sum_ref,
    mixed_grad_ref,
    after_grad_ref,
    sums_ref,
    ff_s,
    second_s,
    cb_s,
    after_s,
    branch_s,
    low_s,
    turned_s,
    sems,
):
    step = pl.program_id(0)
    last = pl.num_programs(0) - 1
    rows, width = xb_ref.shape
    late = Late((cb_any,), (cb_s,), sems)

    half = keep_ref.shape[0]

    def put_grads(columns, turned_ref, values):
        def one(here):
            size = here.size
            keep_ref[here, columns] = nn(turned_ref[here, :], values).astype(BF16)
            there = pl.ds(pl.multiple_of(half + here.start, 16), size)
            send_ref[here, columns] = nn(turned_ref[there, :], values).astype(BF16)

        in_chunks(half, half // 2, one)

    def turn_low():
        def turned(here):
            order = row_order(order_ref[here, :], width)
            turned_s[here, :] = nt(order, low_s[...]).astype(BF16)

        in_chunks(width, width // 2, turned)

    @pl.when(step == 0)
    def _():
        late.start()
        ff_s[...] = jnp.zeros_like(ff_s)
        second_s[...] = jnp.zeros_like(second_s)

        def one(here):
            branch = nt(mixed_ref[here, :], out_w_ref[...]) + vec_ref[OUT_B : OUT_B + 1, :]
            branch_s[here, :] = branch
            after_attn = xb_ref[here, :].astype(F32) + vec_ref[GAM_A : GAM_A + 1, :] * branch
            after_s[here, :] = after_attn
            normed, _ = normal(after_attn)
            low_s[here, :] = (
                normed * vec_ref[LN2_G : LN2_G + 1, :] + vec_ref[LN2_B : LN2_B + 1, :]
            ).astype(BF16)

        in_chunks(rows, rows // 2, one)
        turn_low()

    @pl.when(step < last)
    def _():
        tile = fc1_ref.shape[1]
        pre = nn(low_s[...], fc1_ref[...]) + bias_ref[0:1, :]
        phi, density = cumulative(pre)
        hidden = (pre * phi).astype(BF16)
        slope = phi + pre * density
        grad = (nn(up_ref[...], fc2_ref[...]) * slope).astype(BF16)
        ff_s[...] += nt(hidden, fc2_ref[...])
        second_s[...] += nt(grad, fc1_ref[...])
        for columns, values in (
            (slice(0, tile), nn(turned_s[...], grad)),
            (slice(tile, 2 * tile), nn(up_t_ref[...], hidden)),
        ):
            keep_ref[:, columns] = values[:half].astype(BF16)
            send_ref[:, columns] = values[half:].astype(BF16)
        fc1_sum_ref[...] = jnp.broadcast_to(
            jnp.sum(grad.astype(F32), axis=0, keepdims=True), fc1_sum_ref.shape
        )

    @pl.when(step == last)
    def _():
        late.wait()
        cot = cb_s[...].astype(F32)
        sums_ref[...] = jnp.zeros_like(sums_ref)
        normed, inverse = normal(after_s[...])
        second = second_s[...]
        column_sum(sums_ref, G_LN2_G, second * normed)
        column_sum(sums_ref, G_LN2_B, second)
        scaled = second * vec_ref[LN2_G : LN2_G + 1, :]
        inner = jnp.mean(scaled, axis=-1, keepdims=True)
        along = jnp.mean(scaled * normed, axis=-1, keepdims=True)
        after_grad = cot + inverse * (scaled - inner - normed * along)
        after_grad_ref[...] = after_grad
        column_sum(sums_ref, G_GAM_A, after_grad * branch_s[...])
        low = (vec_ref[GAM_A : GAM_A + 1, :] * after_grad).astype(BF16)
        column_sum(sums_ref, G_OUT_B, low.astype(F32))
        mixed_grad_ref[...] = nn(low, out_w_ref[...]).astype(BF16)
        low_s[...] = low
        turn_low()
        put_grads(slice(0, width), turned_s, mixed_ref[...])
        branch = ff_s[...] + vec_ref[FC2_B : FC2_B + 1, :]
        result = (after_s[...] + vec_ref[GAM_M : GAM_M + 1, :] * branch).astype(BF16)
        out_ref[...] = restore_rows(info[0], result, block_rows, image, out_ref.shape[0]).astype(
            BF16
        )
        column_sum(sums_ref, G_GAM_M, cot * branch)
        column_sum(sums_ref, G_FC2_B, up_ref[...].astype(F32))


def feed(
    info,
    order,
    mixed,
    xb,
    up,
    up_t,
    vec,
    fc1b,
    weights,
    cb,
    image,
    block_rows,
    length,
    tile,
):
    rows, width = xb.shape
    hidden = fc1b.shape[1]
    steps = hidden // tile
    anywhere = pl.BlockSpec(memory_space=pl.ANY)
    once = pl.Buffered(1)

    def at(i):
        return jnp.minimum(i, steps - 1)

    def fixed(shape):
        return pl.BlockSpec(shape, lambda i: (0, 0), pipeline_mode=once)

    return pl.pallas_call(
        functools.partial(feed_body, image, block_rows),
        grid=(steps + 1,),
        in_specs=[
            smem(),
            fixed((width, 1)),
            fixed((rows, width)),
            fixed((rows, width)),
            fixed((rows, width)),
            fixed((width, rows)),
            fixed(vec.shape),
            pl.BlockSpec((8, tile), lambda i: (0, at(i))),
            pl.BlockSpec((width, width), lambda i: (0, 2 * hidden // width), pipeline_mode=once),
            pl.BlockSpec((width, tile), lambda i: (0, at(i))),
            pl.BlockSpec((width, tile), lambda i: (0, steps + at(i))),
        ]
        + [anywhere],
        out_specs=[
            full((length, width)),
            pl.BlockSpec((width // 2, 2 * tile), lambda i: (0, i)),
            pl.BlockSpec((width // 2, 2 * tile), lambda i: (0, i)),
            pl.BlockSpec((8, tile), lambda i: (0, at(i))),
            full((rows, width)),
            full((rows, width)),
            full((16, width)),
        ],
        out_shape=[
            jax.ShapeDtypeStruct((length, width), BF16),
            jax.ShapeDtypeStruct((width // 2, 2 * hidden + width), BF16),
            jax.ShapeDtypeStruct((width // 2, 2 * hidden + width), BF16),
            jax.ShapeDtypeStruct((8, hidden), F32),
            jax.ShapeDtypeStruct((rows, width), BF16),
            jax.ShapeDtypeStruct((rows, width), F32),
            jax.ShapeDtypeStruct((16, width), F32),
        ],
        scratch_shapes=[
            pltpu.VMEM((rows, width), F32),
            pltpu.VMEM((rows, width), F32),
            pltpu.VMEM((rows, width), BF16),
            pltpu.VMEM((rows, width), F32),
            pltpu.VMEM((rows, width), F32),
            pltpu.VMEM((rows, width), BF16),
            pltpu.VMEM((width, rows), BF16),
            pltpu.SemaphoreType.DMA((1,)),
        ],
        compiler_params=params(),
        cost_estimate=cost(28),
        name="feed",
    )(
        info,
        order,
        mixed,
        xb,
        up,
        up_t,
        vec,
        fc1b,
        weights,
        weights,
        weights,
        cb,
    )


def weight_grad_body(low_t_ref, packed_ref, keep_ref, send_ref):
    half = keep_ref.shape[0]
    keep_ref[...] = nn(low_t_ref[:half], packed_ref[...]).astype(BF16)
    send_ref[...] = nn(low_t_ref[half:], packed_ref[...]).astype(BF16)


def weight_grad(low_t, packed_grad):
    width, rows = low_t.shape
    return pl.pallas_call(
        weight_grad_body,
        grid=(3,),
        in_specs=[full((width, rows)), pl.BlockSpec((None, rows, width), lambda i: (i, 0, 0))],
        out_specs=[pl.BlockSpec((width // 2, width), lambda i: (0, i))] * 2,
        out_shape=[jax.ShapeDtypeStruct((width // 2, 3 * width), BF16)] * 2,
        compiler_params=params(),
        cost_estimate=cost(5),
        name="weight_grad",
    )(low_t, packed_grad)


def input_grad_body(
    image,
    block_rows,
    info,
    packed_ref,
    weight_ref,
    vec_ref,
    normed_any,
    inv_any,
    after_grad_any,
    out_ref,
    sums_ref,
    first_s,
    normed_s,
    inv_s,
    after_grad_s,
    sems,
):
    step = pl.program_id(0)
    late = Late((normed_any, inv_any, after_grad_any), (normed_s, inv_s, after_grad_s), sems)

    @pl.when(step == 0)
    def _():
        late.start()
        first_s[...] = jnp.zeros_like(first_s)
        sums_ref[...] = jnp.zeros_like(sums_ref)
        column_sum(sums_ref, G_Q_B, packed_ref[...].astype(F32))

    def one(here):
        first_s[here, :] += nt(packed_ref[here, :], weight_ref[...])

    in_chunks(first_s.shape[0], first_s.shape[0] // 2, one)

    @pl.when(step == 2)
    def _():
        late.wait()
        column_sum(sums_ref, G_V_B, packed_ref[...].astype(F32))
        first = first_s[...]
        normed = normed_s[...]
        column_sum(sums_ref, G_LN1_G, first * normed)
        column_sum(sums_ref, G_LN1_B, first)
        scaled = first * vec_ref[LN1_G : LN1_G + 1, :]
        inner = jnp.mean(scaled, axis=-1, keepdims=True)
        along = jnp.mean(scaled * normed, axis=-1, keepdims=True)
        back = inv_s[:, :1] * (scaled - inner - normed * along)
        result = (after_grad_s[...] + back).astype(BF16)
        out_ref[...] = restore_rows(info[0], result, block_rows, image, out_ref.shape[0]).astype(
            BF16
        )


def input_grad(info, packed_grad, weights, vec, normed, inv, after_grad, image, block_rows, length):
    rows, width = normed.shape
    anywhere = pl.BlockSpec(memory_space=pl.ANY)
    return pl.pallas_call(
        functools.partial(input_grad_body, image, block_rows),
        grid=(3,),
        in_specs=[
            smem(),
            pl.BlockSpec((None, rows, width), lambda i: (i, 0, 0)),
            pl.BlockSpec((width, width), lambda i: (0, i)),
            full(vec.shape),
            anywhere,
            anywhere,
            anywhere,
        ],
        out_specs=[full((length, width)), full((16, width))],
        out_shape=[
            jax.ShapeDtypeStruct((length, width), BF16),
            jax.ShapeDtypeStruct((16, width), F32),
        ],
        scratch_shapes=[
            pltpu.VMEM((rows, width), F32),
            pltpu.VMEM((rows, width), F32),
            pltpu.VMEM((rows, 128), F32),
            pltpu.VMEM((rows, width), F32),
            pltpu.SemaphoreType.DMA((3,)),
        ],
        compiler_params=params(),
        cost_estimate=cost(8),
        name="input_grad",
    )(info, packed_grad, weights, vec, normed, inv, after_grad)


def table_grad_body(heads, groups, table_ref, index_ref, out_ref, acc):
    lanes = index_ref.shape[1]
    parts = out_ref.shape[1] // 128
    acc[...] = jnp.zeros_like(acc)
    slots = lax.broadcasted_iota(jnp.int32, (128, lanes), 0).astype(F32).astype(BF16)
    one_bf, zero_bf = jnp.ones((), BF16), jnp.zeros((), BF16)
    zero = jnp.zeros((), BF16)
    group = 8

    def one(step, carry):
        at = pl.ds(pl.multiple_of(step * group, group), group)
        indices = index_ref[at, :]
        lows = jnp.bitwise_and(indices, 127).astype(F32)
        highs = jnp.right_shift(indices, 7).astype(F32)
        values = table_ref[:, at, :]
        left, right = [], []
        for row in range(group):
            low = jnp.broadcast_to(lows[row : row + 1, :], (16, lanes)).astype(BF16)
            high = jnp.broadcast_to(highs[row : row + 1, :], (16, lanes)).astype(BF16)
            right.append(
                jnp.concatenate(
                    [
                        jnp.where(slots[start : start + 16] == low, one_bf, zero_bf)
                        for start in range(0, 128, 16)
                    ],
                    axis=0,
                )
            )
            here = jnp.concatenate(
                [values[:, row, :], jnp.zeros((16 - heads, lanes), F32)], axis=0
            )
            coarse = here.astype(BF16)
            fine = (here - coarse.astype(F32)).astype(BF16)
            masks = [high == jnp.asarray(part, BF16) for part in range(parts)]
            left.append(
                jnp.concatenate(
                    [jnp.where(mask, kind, zero) for kind in (coarse, fine) for mask in masks],
                    axis=0,
                )
            )
        acc[...] += nt(jnp.concatenate(left, axis=1), jnp.concatenate(right, axis=1))
        return carry

    lax.fori_loop(groups[0], groups[1], one, 0)
    half = parts * 16
    for part in range(parts):
        out_ref[:, part * 128 : (part + 1) * 128] = (
            acc[part * 16 : (part + 1) * 16, :] + acc[half + part * 16 : half + (part + 1) * 16, :]
        )


def table_grad(table, index, slots, groups):
    heads, length, lanes = table.shape
    return pl.pallas_call(
        functools.partial(table_grad_body, heads, groups),
        grid=(1,),
        in_specs=[full(table.shape), full(index.shape)],
        out_specs=full((16, slots)),
        out_shape=jax.ShapeDtypeStruct((16, slots), F32),
        scratch_shapes=[pltpu.VMEM((2 * 16 * slots // 128, 128), F32)],
        compiler_params=params(),
        cost_estimate=cost(8),
        name="table_grad",
    )(table, index)


def local(
    inputs,
    cotangent,
    segment_ids,
    keep_rows,
    index_map,
    ln1_gain,
    ln1_bias,
    qkv_weight,
    qv_bias,
    out_weight,
    out_bias,
    gamma_attn,
    rel_table,
    ln2_gain,
    ln2_bias,
    fc1_weight,
    fc1_bias,
    fc2_weight,
    fc2_bias,
    gamma_mlp,
):
    _, length, width = inputs.shape
    heads, per_device = rel_table.shape
    head_dim = width // heads
    own = ln1_gain.shape[0]
    count = width // own
    hidden = fc1_weight.shape[1]
    image = index_map.shape[0]
    block_rows = -(-image // 16) * 16

    keep = keep_rows[0] == 1
    ids = lax.iota(jnp.int32, length)
    info = jnp.stack([jnp.min(jnp.where(keep, ids, length)), jnp.max(jnp.where(keep, 0, 1))])
    moved = index_map // per_device * own + index_map % per_device
    moved = jnp.pad(moved, ((0, block_rows - image), (0, 256 - image)), constant_values=-1)

    small_rows = [
        ln1_gain[None],
        ln1_bias[None],
        qv_bias,
        out_bias[None],
        gamma_attn[None],
        ln2_gain[None],
        ln2_bias[None],
        fc2_bias[None],
        gamma_mlp[None],
    ]
    owners = exchange_owners(count)
    order = (owners[:, None] * own + jnp.arange(own, dtype=jnp.int32)).reshape(-1, 1)
    later = lax.all_gather(
        jnp.concatenate([fc1_weight, fc2_weight.T, out_weight.T], axis=1), AX, axis=0, tiled=True
    )
    xb, cb, normed, inv = prepare(info, inputs[0], cotangent[0], image, block_rows)
    small = pack(small_rows, fc1_bias[None], rel_table, FC1_B, TABLE, hidden // width)
    small = jnp.broadcast_to(after(small, xb)[None], (count, own, SMALL))
    small = lax.all_to_all(small, AX, 0, 0, tiled=True).reshape(width, SMALL)
    vec, fc1b, table = expand(small, moved, heads, hidden)
    mine, got = gather_halves(qkv_weight, count, [(xb,), (small,), (table,)])
    packed, low, qkv_full = project(owners, normed, vec, mine, got, head_dim)
    qkv_full = qkv_full.reshape(width, -1)
    mixed, weights = attend(info, packed, table, block_rows)
    up, up_t, low_t = turn(order, vec, after(cb, mixed), low)
    tile = 512
    out, feed_keep, feed_send, fc1_sum, mixed_grad, after_grad, sums2 = feed(
        info,
        order,
        mixed,
        xb,
        up,
        up_t,
        vec,
        fc1b,
        later,
        cb,
        image,
        block_rows,
        length,
        tile,
    )
    pairs = heads // 2
    some = attend_back(packed, weights, mixed_grad, head_dim, 256, 0, pairs // 2)
    a_pieces, a_send = scatter_step([feed_keep], feed_send, 0, count, some[0])
    packed_grad, table_sum = attend_back(
        packed, weights, after(mixed_grad, a_send), head_dim, 256, pairs // 2, pairs, some
    )
    qkv_keep, qkv_send = weight_grad(low_t, packed_grad)
    in_grad, sums1 = input_grad(
        info,
        packed_grad,
        qkv_full,
        vec,
        normed,
        after(inv, qkv_keep),
        after_grad,
        image,
        block_rows,
        length,
    )
    groups = -(-image // 8)
    slots = own * count
    b_pieces, b_send = scatter_step([qkv_keep], qkv_send, 0, count, in_grad)
    slot_sums = table_grad(after(table_sum, b_send), moved, slots, (0, groups // 2))
    a_pieces, a_send = scatter_step(a_pieces, a_send, 1, count, slot_sums)
    more_sums = table_grad(after(table_sum, a_send), moved, slots, (groups // 2, groups))
    b_pieces, b_send = scatter_step(b_pieces, b_send, 1, count, more_sums)
    a_pieces, a_send = scatter_step(a_pieces, a_send, 2, count, b_send)
    slot_sums = slot_sums + after(more_sums, a_send)

    rows = jnp.concatenate([sums1[:10] + sums2[:10], slot_sums[:heads]], axis=0)
    rows = jnp.transpose(rows.reshape(-1, count, own), (1, 0, 2))
    biases = fc1_sum[0].reshape(count, -1, own)
    swapped = lax.all_to_all(jnp.concatenate([rows, biases], axis=1), AX, 0, 0, tiled=True)
    b_pieces, b_send = scatter_step(b_pieces, b_send, 2, count, swapped)
    for step in range(3, count.bit_length() - 1):
        a_pieces, a_send = scatter_step(a_pieces, a_send, step, count, b_pieces)
        b_pieces, b_send = scatter_step(b_pieces, b_send, step, count, a_pieces)
    feed_wide, qkv_shard = a_pieces, b_pieces
    small_shard = jnp.sum(swapped, axis=0)

    pieces = feed_wide[:, : 2 * hidden].reshape(own, hidden // tile, 2, tile)
    grad_fc1 = pieces[:, :, 0].reshape(own, hidden)
    grad_fc2 = pieces[:, :, 1].reshape(own, hidden).T
    grad_out = feed_wide[:, 2 * hidden :].T
    grad_table = small_shard[10 : 10 + heads, :per_device]
    grad_fc1_bias = small_shard[10 + heads :].reshape(-1)
    return (
        out[None],
        in_grad[None],
        small_shard[G_LN1_G],
        small_shard[G_LN1_B],
        qkv_shard,
        small_shard[G_Q_B : G_V_B + 1],
        grad_out,
        small_shard[G_OUT_B],
        small_shard[G_GAM_A],
        grad_table,
        small_shard[G_LN2_G],
        small_shard[G_LN2_B],
        grad_fc1,
        grad_fc1_bias,
        grad_fc2,
        small_shard[G_FC2_B],
        small_shard[G_GAM_M],
    )


def solution(mesh):
    rows = P(AX)
    columns = P(None, AX)
    return jax.shard_map(
        local,
        mesh=mesh,
        in_specs=(
            rows,
            rows,
            rows,
            rows,
            P(),
            rows,
            rows,
            rows,
            columns,
            columns,
            rows,
            rows,
            columns,
            rows,
            rows,
            rows,
            rows,
            columns,
            rows,
            rows,
        ),
        out_specs=(
            rows,
            rows,
            rows,
            rows,
            rows,
            columns,
            columns,
            rows,
            rows,
            columns,
            rows,
            rows,
            rows,
            rows,
            columns,
            rows,
            rows,
        ),
        check_vma=False,
    )
```

```python
import functools
import jax
import jax.numpy as jnp
from jax import lax
from jax.experimental import pallas as pl
from jax.experimental.pallas import tpu as pltpu
from jax.sharding import PartitionSpec as P

AX = ("dp", "fsdp")
IMGS = 4
EPS = 1e-06
MASKED = -1e30
ROOT_HALF = 0.7071067811865476
INV_ROOT_TAU = 0.3989422804014327
F32 = jnp.float32
BF16 = jnp.bfloat16
VMEM_LIMIT = 60 * 1024 * 1024

LN1_G, LN1_B, Q_B, V_B, OUT_B, GAM_A, LN2_G, LN2_B, FC2_B, GAM_M = range(10)
FC1_B = 16
TABLE = 32
SMALL = 128
G_LN1_G, G_LN1_B, G_Q_B, G_V_B, G_OUT_B, G_GAM_A, G_LN2_G, G_LN2_B, G_FC2_B, G_GAM_M = range(10)


def nn(a, b):
    return lax.dot_general(a, b, (((1,), (0,)), ((), ())), preferred_element_type=F32)


def nt(a, b):
    return lax.dot_general(a, b, (((1,), (1,)), ((), ())), preferred_element_type=F32)


def tn(a, b):
    return lax.dot_general(a, b, (((0,), (0,)), ((), ())), preferred_element_type=F32)


def full(shape):
    return pl.BlockSpec(shape, lambda *_: (0,) * len(shape))


def cost(gigaflops, megabytes=4):
    return pl.CostEstimate(
        flops=int(gigaflops * 2e7), bytes_accessed=int(megabytes * 2e4), transcendentals=0
    )


def after(value, *others):
    return lax.optimization_barrier((value, others))[0]


def params(grid_rank=1):
    return pltpu.CompilerParams(
        dimension_semantics=("arbitrary",) * grid_rank, vmem_limit_bytes=VMEM_LIMIT
    )


def smem():
    return pl.BlockSpec(memory_space=pltpu.SMEM)


def exchange_orders(count, kind):
    bits = count.bit_length() - 1
    if bits < 3:
        return (list(range(bits)),) * 2
    rest = list(range(2, bits - 1))
    outer = [1, bits - 1]
    if kind == 0:
        return [0] + outer + rest, [0] + outer[::-1] + rest[::-1]
    return [0] + rest + outer, [0] + rest[::-1] + outer[::-1]


def exchange(values, step, count, kind):
    orders = exchange_orders(count, kind)
    return lax.ppermute(values, AX, [(i, i ^ (1 << orders[i & 1][step])) for i in range(count)])


def exchange_owners(count, kind):
    orders = exchange_orders(count, kind)
    bits = len(orders[0])
    me = lax.axis_index(AX)
    spot = jnp.arange(count, dtype=jnp.int32)
    other = spot >> (bits - 1) if bits else spot
    kind = jnp.bitwise_xor(jnp.bitwise_and(me, 1), other)
    flips = other
    for step in range(1, bits):
        bit = jnp.bitwise_and(spot >> (bits - 1 - step), 1)
        flips = jnp.bitwise_or(
            flips, bit << jnp.where(kind == 1, orders[1][step], orders[0][step])
        )
    return jnp.bitwise_xor(me, flips)


def gather_halves(values, count, before):
    for number, step in enumerate(reversed(range(count.bit_length() - 1))):
        got = exchange(values, step, count, 0)
        if number < len(before):
            got = after(got, *before[number])
        if step == 0:
            return values, got
        values = jnp.concatenate([values, got], axis=0)
    half = values.shape[0] // 2
    return values[:half], values[half:]


def scatter_step(kind, pieces, send, step, count, *others):
    got = after(exchange(send, step, count, kind), *others)
    pieces = pieces + [got]
    rows = got.shape[-2]

    def total(start, stop):
        return sum(piece[..., start:stop, :].astype(F32) for piece in pieces)

    if step == count.bit_length() - 2:
        return total(0, rows), None
    return pieces, total(rows // 2, rows).astype(BF16)


def in_chunks(rows, size, body):
    def one(number, carry):
        body(pl.ds(pl.multiple_of(number * size, 16), size))
        return carry

    lax.fori_loop(0, rows // size, one, 0)


def row_order(column, width):
    rows = column.shape[0]
    return (lax.broadcasted_iota(jnp.int32, (rows, width), 1) == column).astype(BF16)


def block_source(first, number, rows, image, length):
    at = first + image * number + rows
    at = jnp.where(at >= length, at - length, at)
    return jnp.where(rows < image, at, -1)


def place_rows(first, source, target_rows, image):
    length = source.shape[0]

    def one(number):
        rows = lax.broadcasted_iota(jnp.int32, (target_rows, 1), 0)
        wanted = block_source(first, number, rows, image, length)
        columns = lax.broadcasted_iota(jnp.int32, (target_rows, length), 1)
        return nn((columns == wanted).astype(BF16), source)

    return one


def restore_rows(first, blocked, block_rows, image, length):
    lanes = lax.broadcasted_iota(jnp.int32, (1, block_rows), 1)
    wanted = jnp.concatenate(
        [block_source(first, number, lanes, image, length) for number in range(IMGS)], axis=1
    )
    rows = lax.broadcasted_iota(jnp.int32, (length, IMGS * block_rows), 0)
    return nn((rows == wanted).astype(BF16), blocked)


def pack_body(bias_at, table_at, ratio, bias_ref, table_ref, *rest):
    *row_refs, out_ref, rows_s = rest
    own = out_ref.shape[0]
    rows_s[...] = jnp.zeros_like(rows_s)
    at_row = 0
    for ref in row_refs:
        rows_s[at_row : at_row + ref.shape[0], :] = ref[...].astype(F32)
        at_row += ref.shape[0]
    heads, slots = table_ref.shape
    rows_s[table_at : table_at + heads, :slots] = table_ref[...].astype(F32)
    eye = (
        lax.broadcasted_iota(jnp.int32, (own, own), 0)
        == lax.broadcasted_iota(jnp.int32, (own, own), 1)
    ).astype(BF16)
    small = nt(eye, rows_s[...].astype(BF16))
    biases = jnp.broadcast_to(bias_ref[...].astype(F32), (own, own * ratio))
    at = lax.broadcasted_iota(jnp.int32, (own, own * ratio), 1)
    row = lax.broadcasted_iota(jnp.int32, (own, own * ratio), 0)
    lane = lax.broadcasted_iota(jnp.int32, (own, SMALL), 1)
    for number in range(ratio):
        column = jnp.sum(
            jnp.where(at == row * ratio + number, biases, 0.0), axis=1, keepdims=True
        )
        small = small + jnp.where(lane == bias_at + number, column, 0.0)
    out_ref[...] = small.astype(BF16)


def pack(rows, bias, table, bias_at, table_at, ratio):
    own = rows[0].shape[1]
    operands = (bias, table, *rows)
    return pl.pallas_call(
        functools.partial(pack_body, bias_at, table_at, ratio),
        grid=(1,),
        in_specs=[full(value.shape) for value in operands],
        out_specs=full((own, SMALL)),
        out_shape=jax.ShapeDtypeStruct((own, SMALL), BF16),
        scratch_shapes=[pltpu.VMEM((SMALL, own), F32)],
        compiler_params=params(),
        name="pack",
    )(*operands)


def prepare_body(image, block_rows, info, x_ref, cot_ref, xb_ref, cb_ref, normed_ref, inv_ref):
    first = info[0]

    def one(number, carry):
        here = pl.ds(pl.multiple_of(number * block_rows, 16), block_rows)
        values = place_rows(first, x_ref[...], block_rows, image)(number)
        xb_ref[here, :] = values.astype(BF16)
        normed, inverse = normal(values)
        normed_ref[here, :] = normed
        inv_ref[here, :] = jnp.broadcast_to(inverse, (block_rows, 128))
        cb_ref[here, :] = place_rows(first, cot_ref[...], block_rows, image)(number).astype(BF16)
        return carry

    lax.fori_loop(0, IMGS, one, 0)


def prepare(info, x, cot, image, block_rows):
    length, width = x.shape
    rows = IMGS * block_rows
    return pl.pallas_call(
        functools.partial(prepare_body, image, block_rows),
        grid=(1,),
        in_specs=[smem(), full((length, width)), full((length, width))],
        out_specs=[full((rows, width))] * 3 + [full((rows, 128))],
        out_shape=[
            jax.ShapeDtypeStruct((rows, width), BF16),
            jax.ShapeDtypeStruct((rows, width), BF16),
            jax.ShapeDtypeStruct((rows, width), F32),
            jax.ShapeDtypeStruct((rows, 128), F32),
        ],
        compiler_params=params(),
        cost_estimate=cost(4),
        name="prepare",
    )(info, x, cot)


def expand_body(heads, small_ref, index_ref, vec_ref, fc1b_ref, table_ref, entries_s):
    eye = (
        lax.broadcasted_iota(jnp.int32, (SMALL, SMALL), 0)
        == lax.broadcasted_iota(jnp.int32, (SMALL, SMALL), 1)
    ).astype(BF16)
    width = small_ref.shape[0]
    hidden = fc1b_ref.shape[1]
    ratio = hidden // width
    rows = nt(eye, small_ref[...])
    vec_ref[...] = rows[: vec_ref.shape[0]]
    spread = (
        lax.broadcasted_iota(jnp.int32, (width, hidden), 0)
        == lax.broadcasted_iota(jnp.int32, (width, hidden), 1) // ratio
    ).astype(BF16)
    wide = nn(rows[FC1_B : FC1_B + 8].astype(BF16), spread)
    which = lax.broadcasted_iota(jnp.int32, (8, hidden), 1) % ratio
    mine = lax.broadcasted_iota(jnp.int32, (8, hidden), 0)
    total = jnp.sum(jnp.where(which == mine, wide, 0.0), axis=0, keepdims=True)
    fc1b_ref[...] = jnp.broadcast_to(total, fc1b_ref.shape)
    length, lanes = index_ref.shape
    parts = width // 128
    for head in range(heads):
        for part in range(parts):
            entries_s[head * parts + part] = jnp.broadcast_to(
                rows[TABLE + head : TABLE + head + 1, part * 128 : (part + 1) * 128], (8, 128)
            )

    def one(step, carry):
        at = pl.ds(pl.multiple_of(step * 8, 8), 8)
        for half in range(lanes // 128):
            columns = slice(half * 128, (half + 1) * 128)
            index = index_ref[at, columns]
            low = jnp.bitwise_and(index, 127)
            high = jnp.right_shift(index, 7)
            found = [jnp.full((8, 128), MASKED, F32)] * heads
            for part in range(parts):
                chosen = high == part
                for head in range(heads):
                    taken = jnp.take_along_axis(
                        entries_s[head * parts + part], low, axis=1, mode="promise_in_bounds"
                    )
                    found[head] = jnp.where(chosen, taken, found[head])
            for head in range(heads):
                table_ref[head, at, columns] = found[head]
        return carry

    lax.fori_loop(0, length // 8, one, 0)


def expand(small, index, heads, hidden):
    width = small.shape[0]
    length, lanes = index.shape
    return pl.pallas_call(
        functools.partial(expand_body, heads),
        grid=(1,),
        in_specs=[
            full((width, SMALL)),
            full((length, lanes)),
        ],
        out_specs=[full((64, width)), full((8, hidden)), full((heads, length, lanes))],
        out_shape=[
            jax.ShapeDtypeStruct((64, width), F32),
            jax.ShapeDtypeStruct((8, hidden), F32),
            jax.ShapeDtypeStruct((heads, length, lanes), F32),
        ],
        scratch_shapes=[pltpu.VMEM((heads * width // 128, 8, 128), F32)],
        compiler_params=params(),
        cost_estimate=cost(5),
        name="expand",
    )(small, index)


def project_body(
    scale,
    owners,
    normed_ref,
    vec_ref,
    mine_any,
    got_any,
    packed_ref,
    low_ref,
    weight_any,
    weight_s,
    sems,
    out_sem,
):
    step = pl.program_id(0)
    half = mine_any.shape[0]
    width = normed_ref.shape[1]
    keeping = pltpu.make_async_copy(weight_s, weight_any, out_sem)

    @pl.when(step == 0)
    def _():
        copies = []
        for spot in range(2 * half):
            source = mine_any.at[spot] if spot < half else got_any.at[spot - half]
            copy = pltpu.make_async_copy(source, weight_s.at[owners[spot]], sems.at[spot])
            copy.start()
            copies.append(copy)
        low_ref[...] = (
            normed_ref[...] * vec_ref[LN1_G : LN1_G + 1, :] + vec_ref[LN1_B : LN1_B + 1, :]
        ).astype(BF16)
        for copy in copies:
            copy.wait()
        keeping.start()

    bias = jnp.where(
        step == 0,
        vec_ref[Q_B : Q_B + 1, :],
        jnp.where(step == 2, vec_ref[V_B : V_B + 1, :], 0.0),
    )
    columns = pl.ds(pl.multiple_of(step * width, 128), width)
    weight = weight_s[:, :, columns].reshape(width, width)
    result = (nn(low_ref[...], weight) + bias).astype(BF16)
    packed_ref[...] = (result.astype(F32) * jnp.where(step == 0, scale, 1.0)).astype(BF16)

    @pl.when(step == 2)
    def _():
        keeping.wait()


def project(owners, normed, vec, mine, got, head_dim):
    rows, width = normed.shape
    count = owners.shape[0]
    wide = mine.shape[1]
    own = width // count
    anywhere = pl.BlockSpec(memory_space=pl.ANY)
    half = -(-count // 2)
    return pl.pallas_call(
        functools.partial(project_body, head_dim**-0.5),
        grid=(3,),
        in_specs=[smem(), full((rows, width)), full(vec.shape), anywhere, anywhere],
        out_specs=[
            pl.BlockSpec((rows, width), lambda i: (0, i)),
            full((rows, width)),
            anywhere,
        ],
        out_shape=[
            jax.ShapeDtypeStruct((rows, wide), BF16),
            jax.ShapeDtypeStruct((rows, width), BF16),
            jax.ShapeDtypeStruct((count, own, wide), BF16),
        ],
        scratch_shapes=[
            pltpu.VMEM((count, own, wide), BF16),
            pltpu.SemaphoreType.DMA((2 * half,)),
            pltpu.SemaphoreType.DMA,
        ],
        compiler_params=params(),
        cost_estimate=cost(4),
        name="project",
    )(owners, normed, vec, mine.reshape(half, own, wide), got.reshape(half, own, wide))


def turn_body(order_ref, qkv_order_ref, vec_ref, cb_ref, low_ref, up_ref, up_t_ref, low_t_ref):
    up_ref[...] = (vec_ref[GAM_M : GAM_M + 1, :] * cb_ref[...].astype(F32)).astype(BF16)
    width = low_ref.shape[1]

    def turned(here):
        up_t_ref[here, :] = nt(row_order(order_ref[here, :], width), up_ref[...]).astype(BF16)
        qkv_order = row_order(qkv_order_ref[here, :], width)
        low_t_ref[here, :] = nt(qkv_order, low_ref[...]).astype(BF16)

    in_chunks(width, width // 2, turned)


def turn(order, qkv_order, vec, cb, low):
    rows, width = cb.shape
    return pl.pallas_call(
        turn_body,
        grid=(1,),
        in_specs=[full((width, 1))] * 2
        + [full(vec.shape), full((rows, width)), full((rows, width))],
        out_specs=[full((rows, width)), full((width, rows)), full((width, rows))],
        out_shape=[
            jax.ShapeDtypeStruct((rows, width), BF16),
            jax.ShapeDtypeStruct((width, rows), BF16),
            jax.ShapeDtypeStruct((width, rows), BF16),
        ],
        compiler_params=params(),
        cost_estimate=cost(3),
        name="turn",
    )(order, qkv_order, vec, cb, low)


def halves(values):
    lanes = lax.broadcasted_iota(jnp.int32, values.shape, 1)
    zero = jnp.zeros((), values.dtype)
    side = values.shape[1] // 2
    return (jnp.where(lanes < side, values, zero), jnp.where(lanes >= side, values, zero))


def attend_body(block_rows, info, q_ref, k_ref, v_ref, table_ref, mixed_ref, weight_ref):
    rows = lax.broadcasted_iota(jnp.int32, (block_rows, block_rows), 0)
    columns = lax.broadcasted_iota(jnp.int32, (block_rows, block_rows), 1)
    alone = jnp.where(rows == columns, 0.0, MASKED)

    def one(number, carry):
        padded = jnp.logical_and(info[1] == 1, number == IMGS - 1)
        here = pl.ds(pl.multiple_of(number * block_rows, 16), block_rows)
        queries = halves(q_ref[here, :])
        values = halves(v_ref[here, :])
        keys = k_ref[here, :]
        mixed = None
        for side in range(2):
            bias = jnp.where(padded, alone, table_ref[side, :, :block_rows])
            scores = nt(queries[side], keys) + bias
            raised = jnp.exp(scores - jnp.max(scores, axis=1, keepdims=True))
            weights = raised * (1.0 / jnp.sum(raised, axis=1, keepdims=True))
            weight_ref[side, number] = weights
            part = nn(weights.astype(BF16), values[side])
            mixed = part if mixed is None else mixed + part
        mixed_ref[here, :] = mixed.astype(BF16)
        return carry

    lax.fori_loop(0, IMGS, one, 0, unroll=True)


def attend(info, packed, table, block_rows):
    rows, three = packed.shape
    pairs = three // (3 * 128)
    heads, length, lanes = table.shape
    return pl.pallas_call(
        functools.partial(attend_body, block_rows),
        grid=(pairs,),
        in_specs=[
            smem(),
            pl.BlockSpec((rows, 128), lambda p: (0, p)),
            pl.BlockSpec((rows, 128), lambda p: (0, pairs + p)),
            pl.BlockSpec((rows, 128), lambda p: (0, 2 * pairs + p)),
            pl.BlockSpec((2, length, lanes), lambda p: (p, 0, 0)),
        ],
        out_specs=[
            pl.BlockSpec((rows, 128), lambda p: (0, p)),
            pl.BlockSpec((2, IMGS, block_rows, block_rows), lambda p: (p, 0, 0, 0)),
        ],
        out_shape=[
            jax.ShapeDtypeStruct((rows, pairs * 128), BF16),
            jax.ShapeDtypeStruct((heads, IMGS, block_rows, block_rows), F32),
        ],
        compiler_params=params(),
        cost_estimate=cost(6),
        name="attend",
    )(info, packed, packed, packed, table)


def attend_back_body(block_rows, scale, q_ref, k_ref, v_ref, weight_ref, grad_ref, *rest):
    packed_ref, table_ref = rest[-2:]
    for side in range(2):
        table_ref[side] = jnp.zeros(table_ref.shape[1:], F32)

    def one(number, carry):
        here = pl.ds(pl.multiple_of(number * block_rows, 16), block_rows)
        queries = halves(q_ref[here, :])
        keys = halves(k_ref[here, :])
        grads = halves(grad_ref[here, :])
        values = v_ref[here, :]
        dq = dk = dv = 0.0
        for side in range(2):
            weights = weight_ref[side, number]
            up = nt(grads[side], values)
            inner = jnp.sum(weights * up, axis=1, keepdims=True)
            score = (weights * (up - inner)).astype(BF16)
            dv += tn(weights.astype(BF16), grads[side])
            dq += nn(score, keys[side])
            dk += tn(score, queries[side])
            table_ref[side, :, :block_rows] += score.astype(F32)
        packed_ref[0, here, :] = (dq * scale).astype(BF16)
        packed_ref[1, here, :] = dk.astype(BF16)
        packed_ref[2, here, :] = dv.astype(BF16)
        return carry

    lax.fori_loop(0, IMGS, one, 0, unroll=True)


def attend_back(packed, weights, mixed_grad, head_dim, lanes, first, last, earlier=()):
    rows, three = packed.shape
    pairs = three // (3 * 128)
    heads, _, block_rows, _ = weights.shape
    part = pl.BlockSpec((rows, 128), lambda p: (0, first + p))
    return pl.pallas_call(
        functools.partial(attend_back_body, block_rows, head_dim**-0.5),
        grid=(last - first,),
        in_specs=[
            part,
            pl.BlockSpec((rows, 128), lambda p: (0, pairs + first + p)),
            pl.BlockSpec((rows, 128), lambda p: (0, 2 * pairs + first + p)),
            pl.BlockSpec((2, IMGS, block_rows, block_rows), lambda p: (first + p, 0, 0, 0)),
            part,
        ]
        + [pl.BlockSpec(memory_space=pl.ANY)] * len(earlier),
        out_specs=[
            pl.BlockSpec((3, rows, 128), lambda p: (0, 0, first + p)),
            pl.BlockSpec((2, block_rows, lanes), lambda p: (first + p, 0, 0)),
        ],
        out_shape=[
            jax.ShapeDtypeStruct((3, rows, pairs * 128), BF16),
            jax.ShapeDtypeStruct((heads, block_rows, lanes), F32),
        ],
        input_output_aliases={5: 0, 6: 1} if earlier else {},
        compiler_params=params(),
        cost_estimate=cost(4),
        name="attend_back",
    )(packed, packed, packed, weights, mixed_grad, *earlier)


def cumulative(values):
    squared = jnp.exp(-0.5 * values * values)
    size = jnp.abs(values) * ROOT_HALF
    t = 1.0 / (1.0 + 0.3275911 * size)
    poly = t * (
        0.254829592 + t * (-0.284496736 + t * (1.421413741 + t * (-1.453152027 + t * 1.061405429)))
    )
    tail = 0.5 * poly * squared
    return jnp.where(values < 0, tail, 1.0 - tail), squared * INV_ROOT_TAU


def normal(values):
    average = jnp.mean(values, axis=-1, keepdims=True)
    centred = values - average
    inverse = lax.rsqrt(jnp.mean(centred * centred, axis=-1, keepdims=True) + EPS)
    return centred * inverse, inverse


def column_sum(ref, row, values):
    ref[row : row + 1, :] = jnp.sum(values, axis=0, keepdims=True)


class Late:
    def __init__(self, sources, targets, sems):
        self.copies = [
            pltpu.make_async_copy(source, target, sems.at[number])
            for number, (source, target) in enumerate(zip(sources, targets, strict=True))
        ]

    def start(self):
        for copy in self.copies:
            copy.start()

    def wait(self):
        for copy in self.copies:
            copy.wait()


def feed_body(
    image,
    block_rows,
    info,
    order_ref,
    mixed_ref,
    xb_ref,
    up_ref,
    up_t_ref,
    vec_ref,
    bias_ref,
    out_w_ref,
    fc1_ref,
    fc2_ref,
    cb_any,
    out_ref,
    keep_ref,
    send_ref,
    fc1_sum_ref,
    mixed_grad_ref,
    after_grad_ref,
    sums_ref,
    ff_s,
    second_s,
    cb_s,
    after_s,
    branch_s,
    low_s,
    turned_s,
    sems,
):
    step = pl.program_id(0)
    last = pl.num_programs(0) - 1
    rows, width = xb_ref.shape
    late = Late((cb_any,), (cb_s,), sems)

    half = keep_ref.shape[1]
    side = width // 2

    def put_out_grad(here):
        there = pl.ds(pl.multiple_of(half + here.start, 16), here.size)
        for ref, rows_here in ((keep_ref, here), (send_ref, there)):
            values = nn(turned_s[rows_here, :], mixed_ref[...]).astype(BF16)
            ref[0, here, :side] = values[:, :side]
            ref[1, here, :side] = values[:, side:]

    def turn_low():
        def turned(here):
            order = row_order(order_ref[here, :], width)
            turned_s[here, :] = nt(order, low_s[...]).astype(BF16)

        in_chunks(width, width // 2, turned)

    @pl.when(step == 0)
    def _():
        late.start()
        ff_s[...] = jnp.zeros_like(ff_s)
        second_s[...] = jnp.zeros_like(second_s)

        def one(here):
            branch = nt(mixed_ref[here, :], out_w_ref[...]) + vec_ref[OUT_B : OUT_B + 1, :]
            branch_s[here, :] = branch
            after_attn = xb_ref[here, :].astype(F32) + vec_ref[GAM_A : GAM_A + 1, :] * branch
            after_s[here, :] = after_attn
            normed, _ = normal(after_attn)
            low_s[here, :] = (
                normed * vec_ref[LN2_G : LN2_G + 1, :] + vec_ref[LN2_B : LN2_B + 1, :]
            ).astype(BF16)

        in_chunks(rows, rows // 2, one)
        turn_low()

    @pl.when(step < last)
    def _():
        pre = nn(low_s[...], fc1_ref[...]) + bias_ref[0:1, :]
        phi, density = cumulative(pre)
        hidden = (pre * phi).astype(BF16)
        slope = phi + pre * density
        grad = (nn(up_ref[...], fc2_ref[...]) * slope).astype(BF16)
        ff_s[...] += nt(hidden, fc2_ref[...])
        second_s[...] += nt(grad, fc1_ref[...])
        for plane, values in enumerate((nn(turned_s[...], grad), nn(up_t_ref[...], hidden))):
            keep_ref[plane] = values[:half].astype(BF16)
            send_ref[plane] = values[half:].astype(BF16)
        fc1_sum_ref[...] = jnp.broadcast_to(
            jnp.sum(grad.astype(F32), axis=0, keepdims=True), fc1_sum_ref.shape
        )

    @pl.when(step == last)
    def _():
        late.wait()
        cot = cb_s[...].astype(F32)
        sums_ref[...] = jnp.zeros_like(sums_ref)
        normed, inverse = normal(after_s[...])
        second = second_s[...]
        column_sum(sums_ref, G_LN2_G, second * normed)
        column_sum(sums_ref, G_LN2_B, second)
        scaled = second * vec_ref[LN2_G : LN2_G + 1, :]
        inner = jnp.mean(scaled, axis=-1, keepdims=True)
        along = jnp.mean(scaled * normed, axis=-1, keepdims=True)
        after_grad = cot + inverse * (scaled - inner - normed * along)
        after_grad_ref[...] = after_grad
        column_sum(sums_ref, G_GAM_A, after_grad * branch_s[...])
        low = (vec_ref[GAM_A : GAM_A + 1, :] * after_grad).astype(BF16)
        column_sum(sums_ref, G_OUT_B, low.astype(F32))
        mixed_grad_ref[...] = nn(low, out_w_ref[...]).astype(BF16)
        low_s[...] = low
        turn_low()
        in_chunks(half, half // 2, put_out_grad)
        branch = ff_s[...] + vec_ref[FC2_B : FC2_B + 1, :]
        result = (after_s[...] + vec_ref[GAM_M : GAM_M + 1, :] * branch).astype(BF16)
        out_ref[...] = restore_rows(info[0], result, block_rows, image, out_ref.shape[0]).astype(
            BF16
        )
        column_sum(sums_ref, G_GAM_M, cot * branch)
        column_sum(sums_ref, G_FC2_B, up_ref[...].astype(F32))


def feed(
    info,
    order,
    mixed,
    xb,
    up,
    up_t,
    vec,
    fc1b,
    weights,
    cb,
    image,
    block_rows,
    length,
    tile,
):
    rows, width = xb.shape
    hidden = fc1b.shape[1]
    steps = hidden // tile
    anywhere = pl.BlockSpec(memory_space=pl.ANY)
    once = pl.Buffered(1)

    def at(i):
        return jnp.minimum(i, steps - 1)

    def fixed(shape):
        return pl.BlockSpec(shape, lambda i: (0, 0), pipeline_mode=once)

    return pl.pallas_call(
        functools.partial(feed_body, image, block_rows),
        grid=(steps + 1,),
        in_specs=[
            smem(),
            fixed((width, 1)),
            fixed((rows, width)),
            fixed((rows, width)),
            fixed((rows, width)),
            fixed((width, rows)),
            fixed(vec.shape),
            pl.BlockSpec((8, tile), lambda i: (0, at(i))),
            pl.BlockSpec((width, width), lambda i: (0, 2 * hidden // width), pipeline_mode=once),
            pl.BlockSpec((width, tile), lambda i: (0, at(i))),
            pl.BlockSpec((width, tile), lambda i: (0, steps + at(i))),
        ]
        + [anywhere],
        out_specs=[
            full((length, width)),
            pl.BlockSpec((2, width // 2, tile), lambda i: (0, 0, i)),
            pl.BlockSpec((2, width // 2, tile), lambda i: (0, 0, i)),
            pl.BlockSpec((8, tile), lambda i: (0, at(i))),
            full((rows, width)),
            full((rows, width)),
            full((16, width)),
        ],
        out_shape=[
            jax.ShapeDtypeStruct((length, width), BF16),
            jax.ShapeDtypeStruct((2, width // 2, hidden + width // 2), BF16),
            jax.ShapeDtypeStruct((2, width // 2, hidden + width // 2), BF16),
            jax.ShapeDtypeStruct((8, hidden), F32),
            jax.ShapeDtypeStruct((rows, width), BF16),
            jax.ShapeDtypeStruct((rows, width), F32),
            jax.ShapeDtypeStruct((16, width), F32),
        ],
        scratch_shapes=[
            pltpu.VMEM((rows, width), F32),
            pltpu.VMEM((rows, width), F32),
            pltpu.VMEM((rows, width), BF16),
            pltpu.VMEM((rows, width), F32),
            pltpu.VMEM((rows, width), F32),
            pltpu.VMEM((rows, width), BF16),
            pltpu.VMEM((width, rows), BF16),
            pltpu.SemaphoreType.DMA((1,)),
        ],
        compiler_params=params(),
        cost_estimate=cost(28),
        name="feed",
    )(
        info,
        order,
        mixed,
        xb,
        up,
        up_t,
        vec,
        fc1b,
        weights,
        weights,
        weights,
        cb,
    )


def weight_grad_body(low_t_ref, packed_ref, keep_ref, send_ref):
    half = keep_ref.shape[0]
    keep_ref[...] = nn(low_t_ref[:half], packed_ref[...]).astype(BF16)
    send_ref[...] = nn(low_t_ref[half:], packed_ref[...]).astype(BF16)


def weight_grad(low_t, packed_grad):
    width, rows = low_t.shape
    return pl.pallas_call(
        weight_grad_body,
        grid=(3,),
        in_specs=[full((width, rows)), pl.BlockSpec((None, rows, width), lambda i: (i, 0, 0))],
        out_specs=[pl.BlockSpec((width // 2, width), lambda i: (0, i))] * 2,
        out_shape=[jax.ShapeDtypeStruct((width // 2, 3 * width), BF16)] * 2,
        compiler_params=params(),
        cost_estimate=cost(5),
        name="weight_grad",
    )(low_t, packed_grad)


def input_grad_body(
    image,
    block_rows,
    info,
    packed_ref,
    weight_ref,
    vec_ref,
    normed_any,
    inv_any,
    after_grad_any,
    out_ref,
    sums_ref,
    first_s,
    normed_s,
    inv_s,
    after_grad_s,
    sems,
):
    step = pl.program_id(0)
    late = Late((normed_any, inv_any, after_grad_any), (normed_s, inv_s, after_grad_s), sems)

    @pl.when(step == 0)
    def _():
        late.start()
        first_s[...] = jnp.zeros_like(first_s)
        sums_ref[...] = jnp.zeros_like(sums_ref)
        column_sum(sums_ref, G_Q_B, packed_ref[...].astype(F32))

    def one(here):
        first_s[here, :] += nt(packed_ref[here, :], weight_ref[...])

    in_chunks(first_s.shape[0], first_s.shape[0] // 2, one)

    @pl.when(step == 2)
    def _():
        late.wait()
        column_sum(sums_ref, G_V_B, packed_ref[...].astype(F32))
        first = first_s[...]
        normed = normed_s[...]
        column_sum(sums_ref, G_LN1_G, first * normed)
        column_sum(sums_ref, G_LN1_B, first)
        scaled = first * vec_ref[LN1_G : LN1_G + 1, :]
        inner = jnp.mean(scaled, axis=-1, keepdims=True)
        along = jnp.mean(scaled * normed, axis=-1, keepdims=True)
        back = inv_s[:, :1] * (scaled - inner - normed * along)
        result = (after_grad_s[...] + back).astype(BF16)
        out_ref[...] = restore_rows(info[0], result, block_rows, image, out_ref.shape[0]).astype(
            BF16
        )


def input_grad(info, packed_grad, weights, vec, normed, inv, after_grad, image, block_rows, length):
    rows, width = normed.shape
    anywhere = pl.BlockSpec(memory_space=pl.ANY)
    return pl.pallas_call(
        functools.partial(input_grad_body, image, block_rows),
        grid=(3,),
        in_specs=[
            smem(),
            pl.BlockSpec((None, rows, width), lambda i: (i, 0, 0)),
            pl.BlockSpec((width, width), lambda i: (0, i)),
            full(vec.shape),
            anywhere,
            anywhere,
            anywhere,
        ],
        out_specs=[full((length, width)), full((16, width))],
        out_shape=[
            jax.ShapeDtypeStruct((length, width), BF16),
            jax.ShapeDtypeStruct((16, width), F32),
        ],
        scratch_shapes=[
            pltpu.VMEM((rows, width), F32),
            pltpu.VMEM((rows, width), F32),
            pltpu.VMEM((rows, 128), F32),
            pltpu.VMEM((rows, width), F32),
            pltpu.SemaphoreType.DMA((3,)),
        ],
        compiler_params=params(),
        cost_estimate=cost(8),
        name="input_grad",
    )(info, packed_grad, weights, vec, normed, inv, after_grad)


def table_grad_body(heads, groups, table_ref, index_ref, out_ref, acc):
    lanes = index_ref.shape[1]
    parts = out_ref.shape[1] // 128
    acc[...] = jnp.zeros_like(acc)
    slots = lax.broadcasted_iota(jnp.int32, (128, lanes), 0).astype(F32).astype(BF16)
    one_bf, zero_bf = jnp.ones((), BF16), jnp.zeros((), BF16)
    zero = jnp.zeros((), BF16)
    group = 8

    def one(step, carry):
        at = pl.ds(pl.multiple_of(step * group, group), group)
        indices = index_ref[at, :]
        lows = jnp.bitwise_and(indices, 127).astype(F32)
        highs = jnp.right_shift(indices, 7).astype(F32)
        values = table_ref[:, at, :]
        left, right = [], []
        for row in range(group):
            low = jnp.broadcast_to(lows[row : row + 1, :], (16, lanes)).astype(BF16)
            high = jnp.broadcast_to(highs[row : row + 1, :], (16, lanes)).astype(BF16)
            right.append(
                jnp.concatenate(
                    [
                        jnp.where(slots[start : start + 16] == low, one_bf, zero_bf)
                        for start in range(0, 128, 16)
                    ],
                    axis=0,
                )
            )
            here = jnp.concatenate(
                [values[:, row, :], jnp.zeros((16 - heads, lanes), F32)], axis=0
            )
            coarse = here.astype(BF16)
            fine = (here - coarse.astype(F32)).astype(BF16)
            masks = [high == jnp.asarray(part, BF16) for part in range(parts)]
            left.append(
                jnp.concatenate(
                    [jnp.where(mask, kind, zero) for kind in (coarse, fine) for mask in masks],
                    axis=0,
                )
            )
        acc[...] += nt(jnp.concatenate(left, axis=1), jnp.concatenate(right, axis=1))
        return carry

    lax.fori_loop(groups[0], groups[1], one, 0)
    half = parts * 16
    for part in range(parts):
        out_ref[:, part * 128 : (part + 1) * 128] = (
            acc[part * 16 : (part + 1) * 16, :] + acc[half + part * 16 : half + (part + 1) * 16, :]
        )


def table_grad(table, index, slots, groups):
    heads, length, lanes = table.shape
    return pl.pallas_call(
        functools.partial(table_grad_body, heads, groups),
        grid=(1,),
        in_specs=[full(table.shape), full(index.shape)],
        out_specs=full((16, slots)),
        out_shape=jax.ShapeDtypeStruct((16, slots), F32),
        scratch_shapes=[pltpu.VMEM((2 * 16 * slots // 128, 128), F32)],
        compiler_params=params(),
        cost_estimate=cost(8),
        name="table_grad",
    )(table, index)


def local(
    inputs,
    cotangent,
    segment_ids,
    keep_rows,
    index_map,
    ln1_gain,
    ln1_bias,
    qkv_weight,
    qv_bias,
    out_weight,
    out_bias,
    gamma_attn,
    rel_table,
    ln2_gain,
    ln2_bias,
    fc1_weight,
    fc1_bias,
    fc2_weight,
    fc2_bias,
    gamma_mlp,
):
    _, length, width = inputs.shape
    heads, per_device = rel_table.shape
    head_dim = width // heads
    own = ln1_gain.shape[0]
    count = width // own
    hidden = fc1_weight.shape[1]
    image = index_map.shape[0]
    block_rows = -(-image // 16) * 16

    keep = keep_rows[0] == 1
    ids = lax.iota(jnp.int32, length)
    info = jnp.stack([jnp.min(jnp.where(keep, ids, length)), jnp.max(jnp.where(keep, 0, 1))])
    moved = index_map // per_device * own + index_map % per_device
    moved = jnp.pad(moved, ((0, block_rows - image), (0, 256 - image)), constant_values=-1)

    small_rows = [
        ln1_gain[None],
        ln1_bias[None],
        qv_bias,
        out_bias[None],
        gamma_attn[None],
        ln2_gain[None],
        ln2_bias[None],
        fc2_bias[None],
        gamma_mlp[None],
    ]
    owners = exchange_owners(count, 0)

    def row_places(owning):
        return (owning[:, None] * own + jnp.arange(own, dtype=jnp.int32)).reshape(-1, 1)

    order, qkv_order = row_places(owners), row_places(exchange_owners(count, 1))
    later = lax.all_gather(
        jnp.concatenate([fc1_weight, fc2_weight.T, out_weight.T], axis=1), AX, axis=0, tiled=True
    )
    xb, cb, normed, inv = prepare(info, inputs[0], cotangent[0], image, block_rows)
    small = pack(small_rows, fc1_bias[None], rel_table, FC1_B, TABLE, hidden // width)
    small = jnp.broadcast_to(after(small, xb)[None], (count, own, SMALL))
    small = lax.all_to_all(small, AX, 0, 0, tiled=True).reshape(width, SMALL)
    vec, fc1b, table = expand(small, moved, heads, hidden)
    mine, got = gather_halves(qkv_weight, count, [(xb,), (small,), (table,)])
    packed, low, qkv_full = project(owners, normed, vec, mine, got, head_dim)
    qkv_full = qkv_full.reshape(width, -1)
    mixed, weights = attend(info, packed, table, block_rows)
    up, up_t, low_t = turn(order, qkv_order, vec, after(cb, mixed), low)
    tile = 512
    out, feed_keep, feed_send, fc1_sum, mixed_grad, after_grad, sums2 = feed(
        info,
        order,
        mixed,
        xb,
        up,
        up_t,
        vec,
        fc1b,
        later,
        cb,
        image,
        block_rows,
        length,
        tile,
    )
    pairs = heads // 2
    some = attend_back(packed, weights, mixed_grad, head_dim, 256, 0, pairs // 2)
    a_pieces, a_send = scatter_step(0, [feed_keep], feed_send, 0, count, some[0])
    packed_grad, table_sum = attend_back(
        packed, weights, after(mixed_grad, a_send), head_dim, 256, pairs // 2, pairs, some
    )
    qkv_keep, qkv_send = weight_grad(low_t, packed_grad)
    biases = after(fc1_sum, qkv_keep)[0].reshape(count, -1, own)
    b_pieces, b_send = scatter_step(1, [qkv_keep], qkv_send, 0, count, biases)
    in_grad, sums1 = input_grad(
        info,
        packed_grad,
        qkv_full,
        vec,
        normed,
        after(inv, b_send),
        after_grad,
        image,
        block_rows,
        length,
    )
    groups = -(-image // 8)
    slots = own * count
    a_pieces, a_send = scatter_step(0, a_pieces, a_send, 1, count, in_grad)
    slot_sums = table_grad(after(table_sum, a_send), moved, slots, (0, groups // 2))
    b_pieces, b_send = scatter_step(1, b_pieces, b_send, 1, count, slot_sums)
    more_sums = table_grad(after(table_sum, b_send), moved, slots, (groups // 2, groups))
    a_pieces, a_send = scatter_step(0, a_pieces, a_send, 2, count, more_sums)
    b_pieces, b_send = scatter_step(1, b_pieces, b_send, 2, count, a_send)
    slot_sums = slot_sums + after(more_sums, b_send)

    rows = jnp.concatenate([sums1[:10] + sums2[:10], slot_sums[:heads]], axis=0)
    rows = jnp.transpose(rows.reshape(-1, count, own), (1, 0, 2))
    swapped = lax.all_to_all(jnp.concatenate([rows, biases], axis=1), AX, 0, 0, tiled=True)
    a_pieces, a_send = scatter_step(0, a_pieces, a_send, 3, count, swapped)
    b_pieces, b_send = scatter_step(1, b_pieces, b_send, 3, count, a_send)
    late_send = b_send
    for step in range(4, count.bit_length() - 1):
        a_pieces, a_send = scatter_step(0, a_pieces, a_send, step, count, b_send)
    for step in range(4, count.bit_length() - 1):
        b_pieces, b_send = scatter_step(1, b_pieces, b_send, step, count, a_pieces)
    feed_wide, qkv_shard = a_pieces, b_pieces
    small_shard = jnp.sum(after(swapped, late_send), axis=0)

    grad_fc1 = feed_wide[0, :, :hidden]
    grad_fc2 = feed_wide[1, :, :hidden].T
    grad_out = jnp.concatenate([feed_wide[0, :, hidden:], feed_wide[1, :, hidden:]], axis=1).T
    grad_table = small_shard[10 : 10 + heads, :per_device]
    grad_fc1_bias = small_shard[10 + heads :].reshape(-1)
    return (
        out[None],
        in_grad[None],
        small_shard[G_LN1_G],
        small_shard[G_LN1_B],
        qkv_shard,
        small_shard[G_Q_B : G_V_B + 1],
        grad_out,
        small_shard[G_OUT_B],
        small_shard[G_GAM_A],
        grad_table,
        small_shard[G_LN2_G],
        small_shard[G_LN2_B],
        grad_fc1,
        grad_fc1_bias,
        grad_fc2,
        small_shard[G_FC2_B],
        small_shard[G_GAM_M],
    )


def solution(mesh):
    rows = P(AX)
    columns = P(None, AX)
    return jax.shard_map(
        local,
        mesh=mesh,
        in_specs=(
            rows,
            rows,
            rows,
            rows,
            P(),
            rows,
            rows,
            rows,
            columns,
            columns,
            rows,
            rows,
            columns,
            rows,
            rows,
            rows,
            rows,
            columns,
            rows,
            rows,
        ),
        out_specs=(
            rows,
            rows,
            rows,
            rows,
            rows,
            columns,
            columns,
            rows,
            rows,
            columns,
            rows,
            rows,
            rows,
            rows,
            columns,
            rows,
            rows,
        ),
        check_vma=False,
    )
```

```python
import functools
import jax
import jax.numpy as jnp
from jax import lax
from jax.experimental import pallas as pl
from jax.experimental.pallas import tpu as pltpu
from jax.sharding import PartitionSpec as P

AX = ("dp", "fsdp")
IMGS = 4
EPS = 1e-06
MASKED = -1e30
ROOT_HALF = 0.7071067811865476
INV_ROOT_TAU = 0.3989422804014327
F32 = jnp.float32
BF16 = jnp.bfloat16
VMEM_LIMIT = 60 * 1024 * 1024

LN1_G, LN1_B, Q_B, V_B, OUT_B, GAM_A, LN2_G, LN2_B, FC2_B, GAM_M = range(10)
FC1_B = 16
TABLE = 32
SMALL = 128
G_LN1_G, G_LN1_B, G_Q_B, G_V_B, G_OUT_B, G_GAM_A, G_LN2_G, G_LN2_B, G_FC2_B, G_GAM_M = range(10)


def nn(a, b):
    return lax.dot_general(a, b, (((1,), (0,)), ((), ())), preferred_element_type=F32)


def nt(a, b):
    return lax.dot_general(a, b, (((1,), (1,)), ((), ())), preferred_element_type=F32)


def tn(a, b):
    return lax.dot_general(a, b, (((0,), (0,)), ((), ())), preferred_element_type=F32)


def full(shape):
    return pl.BlockSpec(shape, lambda *_: (0,) * len(shape))


def cost(gigaflops, megabytes=4):
    return pl.CostEstimate(
        flops=int(gigaflops * 2e7), bytes_accessed=int(megabytes * 2e4), transcendentals=0
    )


def after(value, *others):
    return lax.optimization_barrier((value, others))[0]


def params(grid_rank=1):
    return pltpu.CompilerParams(
        dimension_semantics=("arbitrary",) * grid_rank, vmem_limit_bytes=VMEM_LIMIT
    )


def smem():
    return pl.BlockSpec(memory_space=pltpu.SMEM)


def exchange_orders(count, kind):
    bits = count.bit_length() - 1
    if bits < 3:
        return (list(range(bits)),) * 2
    rest = list(range(2, bits - 1))
    outer = [1, bits - 1]
    if kind == 0:
        return [0] + outer + rest, [0] + outer[::-1] + rest[::-1]
    return [0] + rest + outer, [0] + rest[::-1] + outer[::-1]


def exchange(values, step, count, kind):
    orders = exchange_orders(count, kind)
    return lax.ppermute(values, AX, [(i, i ^ (1 << orders[i & 1][step])) for i in range(count)])


def exchange_owners(count, kind):
    orders = exchange_orders(count, kind)
    bits = len(orders[0])
    me = lax.axis_index(AX)
    spot = jnp.arange(count, dtype=jnp.int32)
    other = spot >> (bits - 1) if bits else spot
    kind = jnp.bitwise_xor(jnp.bitwise_and(me, 1), other)
    flips = other
    for step in range(1, bits):
        bit = jnp.bitwise_and(spot >> (bits - 1 - step), 1)
        flips = jnp.bitwise_or(
            flips, bit << jnp.where(kind == 1, orders[1][step], orders[0][step])
        )
    return jnp.bitwise_xor(me, flips)


def gather_halves(values, count, before):
    for number, step in enumerate(reversed(range(count.bit_length() - 1))):
        got = exchange(values, step, count, 0)
        if number < len(before):
            got = after(got, *before[number])
        if step == 0:
            return values, got
        values = jnp.concatenate([values, got], axis=0)
    half = values.shape[0] // 2
    return values[:half], values[half:]


def scatter_step(kind, pieces, send, step, count, *others):
    got = after(exchange(send, step, count, kind), *others)
    pieces = pieces + [got]
    rows = got.shape[-2]

    def total(start, stop):
        return sum(piece[..., start:stop, :].astype(F32) for piece in pieces)

    if step == count.bit_length() - 2:
        return total(0, rows), None
    return pieces, total(rows // 2, rows).astype(BF16)


def in_chunks(rows, size, body):
    def one(number, carry):
        body(pl.ds(pl.multiple_of(number * size, 16), size))
        return carry

    lax.fori_loop(0, rows // size, one, 0)


def row_order(column, width):
    rows = column.shape[0]
    return (lax.broadcasted_iota(jnp.int32, (rows, width), 1) == column).astype(BF16)


def block_source(first, number, rows, image, length):
    at = first + image * number + rows
    at = jnp.where(at >= length, at - length, at)
    return jnp.where(rows < image, at, -1)


def place_rows(first, source, target_rows, image):
    length = source.shape[0]

    def one(number):
        rows = lax.broadcasted_iota(jnp.int32, (target_rows, 1), 0)
        wanted = block_source(first, number, rows, image, length)
        columns = lax.broadcasted_iota(jnp.int32, (target_rows, length), 1)
        return nn((columns == wanted).astype(BF16), source)

    return one


def restore_rows(first, blocked, block_rows, image, length):
    lanes = lax.broadcasted_iota(jnp.int32, (1, block_rows), 1)
    wanted = jnp.concatenate(
        [block_source(first, number, lanes, image, length) for number in range(IMGS)], axis=1
    )
    rows = lax.broadcasted_iota(jnp.int32, (length, IMGS * block_rows), 0)
    return nn((rows == wanted).astype(BF16), blocked)


def pack_body(bias_at, table_at, ratio, bias_ref, table_ref, *rest):
    *row_refs, out_ref, rows_s = rest
    own = out_ref.shape[0]
    rows_s[...] = jnp.zeros_like(rows_s)
    at_row = 0
    for ref in row_refs:
        rows_s[at_row : at_row + ref.shape[0], :] = ref[...].astype(F32)
        at_row += ref.shape[0]
    heads, slots = table_ref.shape
    rows_s[table_at : table_at + heads, :slots] = table_ref[...].astype(F32)
    eye = (
        lax.broadcasted_iota(jnp.int32, (own, own), 0)
        == lax.broadcasted_iota(jnp.int32, (own, own), 1)
    ).astype(BF16)
    small = nt(eye, rows_s[...].astype(BF16))
    biases = jnp.broadcast_to(bias_ref[...].astype(F32), (own, own * ratio))
    at = lax.broadcasted_iota(jnp.int32, (own, own * ratio), 1)
    row = lax.broadcasted_iota(jnp.int32, (own, own * ratio), 0)
    lane = lax.broadcasted_iota(jnp.int32, (own, SMALL), 1)
    for number in range(ratio):
        column = jnp.sum(
            jnp.where(at == row * ratio + number, biases, 0.0), axis=1, keepdims=True
        )
        small = small + jnp.where(lane == bias_at + number, column, 0.0)
    out_ref[...] = small.astype(BF16)


def pack(rows, bias, table, bias_at, table_at, ratio):
    own = rows[0].shape[1]
    operands = (bias, table, *rows)
    return pl.pallas_call(
        functools.partial(pack_body, bias_at, table_at, ratio),
        grid=(1,),
        in_specs=[full(value.shape) for value in operands],
        out_specs=full((own, SMALL)),
        out_shape=jax.ShapeDtypeStruct((own, SMALL), BF16),
        scratch_shapes=[pltpu.VMEM((SMALL, own), F32)],
        compiler_params=params(),
        name="pack",
    )(*operands)


def prepare_body(image, block_rows, info, x_ref, cot_ref, xb_ref, cb_ref, normed_ref, inv_ref):
    first = info[0]

    def one(number, carry):
        here = pl.ds(pl.multiple_of(number * block_rows, 16), block_rows)
        values = place_rows(first, x_ref[...], block_rows, image)(number)
        xb_ref[here, :] = values.astype(BF16)
        normed, inverse = normal(values)
        normed_ref[here, :] = normed
        inv_ref[here, :] = jnp.broadcast_to(inverse, (block_rows, 128))
        cb_ref[here, :] = place_rows(first, cot_ref[...], block_rows, image)(number).astype(BF16)
        return carry

    lax.fori_loop(0, IMGS, one, 0)


def prepare(info, x, cot, image, block_rows):
    length, width = x.shape
    rows = IMGS * block_rows
    return pl.pallas_call(
        functools.partial(prepare_body, image, block_rows),
        grid=(1,),
        in_specs=[smem(), full((length, width)), full((length, width))],
        out_specs=[full((rows, width))] * 3 + [full((rows, 128))],
        out_shape=[
            jax.ShapeDtypeStruct((rows, width), BF16),
            jax.ShapeDtypeStruct((rows, width), BF16),
            jax.ShapeDtypeStruct((rows, width), F32),
            jax.ShapeDtypeStruct((rows, 128), F32),
        ],
        compiler_params=params(),
        cost_estimate=cost(4),
        name="prepare",
    )(info, x, cot)


def expand_body(heads, small_ref, index_ref, vec_ref, fc1b_ref, table_ref, entries_s):
    eye = (
        lax.broadcasted_iota(jnp.int32, (SMALL, SMALL), 0)
        == lax.broadcasted_iota(jnp.int32, (SMALL, SMALL), 1)
    ).astype(BF16)
    width = small_ref.shape[0]
    hidden = fc1b_ref.shape[1]
    ratio = hidden // width
    rows = nt(eye, small_ref[...])
    vec_ref[...] = rows[: vec_ref.shape[0]]
    spread = (
        lax.broadcasted_iota(jnp.int32, (width, hidden), 0)
        == lax.broadcasted_iota(jnp.int32, (width, hidden), 1) // ratio
    ).astype(BF16)
    wide = nn(rows[FC1_B : FC1_B + 8].astype(BF16), spread)
    which = lax.broadcasted_iota(jnp.int32, (8, hidden), 1) % ratio
    mine = lax.broadcasted_iota(jnp.int32, (8, hidden), 0)
    total = jnp.sum(jnp.where(which == mine, wide, 0.0), axis=0, keepdims=True)
    fc1b_ref[...] = jnp.broadcast_to(total, fc1b_ref.shape)
    length, lanes = index_ref.shape
    parts = width // 128
    for head in range(heads):
        for part in range(parts):
            entries_s[head * parts + part] = jnp.broadcast_to(
                rows[TABLE + head : TABLE + head + 1, part * 128 : (part + 1) * 128], (8, 128)
            )

    def one(step, carry):
        at = pl.ds(pl.multiple_of(step * 8, 8), 8)
        for half in range(lanes // 128):
            columns = slice(half * 128, (half + 1) * 128)
            index = index_ref[at, columns]
            low = jnp.bitwise_and(index, 127)
            high = jnp.right_shift(index, 7)
            found = [jnp.full((8, 128), MASKED, F32)] * heads
            for part in range(parts):
                chosen = high == part
                for head in range(heads):
                    taken = jnp.take_along_axis(
                        entries_s[head * parts + part], low, axis=1, mode="promise_in_bounds"
                    )
                    found[head] = jnp.where(chosen, taken, found[head])
            for head in range(heads):
                table_ref[head, at, columns] = found[head]
        return carry

    lax.fori_loop(0, length // 8, one, 0)


def expand(small, index, heads, hidden):
    width = small.shape[0]
    length, lanes = index.shape
    return pl.pallas_call(
        functools.partial(expand_body, heads),
        grid=(1,),
        in_specs=[
            full((width, SMALL)),
            full((length, lanes)),
        ],
        out_specs=[full((64, width)), full((8, hidden)), full((heads, length, lanes))],
        out_shape=[
            jax.ShapeDtypeStruct((64, width), F32),
            jax.ShapeDtypeStruct((8, hidden), F32),
            jax.ShapeDtypeStruct((heads, length, lanes), F32),
        ],
        scratch_shapes=[pltpu.VMEM((heads * width // 128, 8, 128), F32)],
        compiler_params=params(),
        cost_estimate=cost(5),
        name="expand",
    )(small, index)


def project_body(
    scale,
    owners,
    normed_ref,
    vec_ref,
    mine_any,
    got_any,
    packed_ref,
    low_ref,
    weight_any,
    weight_s,
    sems,
    out_sem,
):
    step = pl.program_id(0)
    half = mine_any.shape[0]
    width = normed_ref.shape[1]
    keeping = pltpu.make_async_copy(weight_s, weight_any, out_sem)

    @pl.when(step == 0)
    def _():
        copies = []
        for spot in range(2 * half):
            source = mine_any.at[spot] if spot < half else got_any.at[spot - half]
            copy = pltpu.make_async_copy(source, weight_s.at[owners[spot]], sems.at[spot])
            copy.start()
            copies.append(copy)
        low_ref[...] = (
            normed_ref[...] * vec_ref[LN1_G : LN1_G + 1, :] + vec_ref[LN1_B : LN1_B + 1, :]
        ).astype(BF16)
        for copy in copies:
            copy.wait()
        keeping.start()

    bias = jnp.where(
        step == 0,
        vec_ref[Q_B : Q_B + 1, :],
        jnp.where(step == 2, vec_ref[V_B : V_B + 1, :], 0.0),
    )
    columns = pl.ds(pl.multiple_of(step * width, 128), width)
    weight = weight_s[:, :, columns].reshape(width, width)
    result = (nn(low_ref[...], weight) + bias).astype(BF16)
    packed_ref[...] = (result.astype(F32) * jnp.where(step == 0, scale, 1.0)).astype(BF16)

    @pl.when(step == 2)
    def _():
        keeping.wait()


def project(owners, normed, vec, mine, got, head_dim):
    rows, width = normed.shape
    count = owners.shape[0]
    wide = mine.shape[1]
    own = width // count
    anywhere = pl.BlockSpec(memory_space=pl.ANY)
    half = -(-count // 2)
    return pl.pallas_call(
        functools.partial(project_body, head_dim**-0.5),
        grid=(3,),
        in_specs=[smem(), full((rows, width)), full(vec.shape), anywhere, anywhere],
        out_specs=[
            pl.BlockSpec((rows, width), lambda i: (0, i)),
            full((rows, width)),
            anywhere,
        ],
        out_shape=[
            jax.ShapeDtypeStruct((rows, wide), BF16),
            jax.ShapeDtypeStruct((rows, width), BF16),
            jax.ShapeDtypeStruct((count, own, wide), BF16),
        ],
        scratch_shapes=[
            pltpu.VMEM((count, own, wide), BF16),
            pltpu.SemaphoreType.DMA((2 * half,)),
            pltpu.SemaphoreType.DMA,
        ],
        compiler_params=params(),
        cost_estimate=cost(4),
        name="project",
    )(owners, normed, vec, mine.reshape(half, own, wide), got.reshape(half, own, wide))


def turn_body(order_ref, qkv_order_ref, vec_ref, cb_ref, low_ref, up_ref, up_t_ref, low_t_ref):
    up_ref[...] = (vec_ref[GAM_M : GAM_M + 1, :] * cb_ref[...].astype(F32)).astype(BF16)
    width = low_ref.shape[1]

    def turned(here):
        up_t_ref[here, :] = nt(row_order(order_ref[here, :], width), up_ref[...]).astype(BF16)
        qkv_order = row_order(qkv_order_ref[here, :], width)
        low_t_ref[here, :] = nt(qkv_order, low_ref[...]).astype(BF16)

    in_chunks(width, width // 2, turned)


def turn(order, qkv_order, vec, cb, low):
    rows, width = cb.shape
    return pl.pallas_call(
        turn_body,
        grid=(1,),
        in_specs=[full((width, 1))] * 2
        + [full(vec.shape), full((rows, width)), full((rows, width))],
        out_specs=[full((rows, width)), full((width, rows)), full((width, rows))],
        out_shape=[
            jax.ShapeDtypeStruct((rows, width), BF16),
            jax.ShapeDtypeStruct((width, rows), BF16),
            jax.ShapeDtypeStruct((width, rows), BF16),
        ],
        compiler_params=params(),
        cost_estimate=cost(3),
        name="turn",
    )(order, qkv_order, vec, cb, low)


def halves(values):
    lanes = lax.broadcasted_iota(jnp.int32, values.shape, 1)
    zero = jnp.zeros((), values.dtype)
    side = values.shape[1] // 2
    return (jnp.where(lanes < side, values, zero), jnp.where(lanes >= side, values, zero))


def attend_body(block_rows, info, q_ref, k_ref, v_ref, table_ref, mixed_ref, weight_ref):
    rows = lax.broadcasted_iota(jnp.int32, (block_rows, block_rows), 0)
    columns = lax.broadcasted_iota(jnp.int32, (block_rows, block_rows), 1)
    alone = jnp.where(rows == columns, 0.0, MASKED)

    def one(number, carry):
        padded = jnp.logical_and(info[1] == 1, number == IMGS - 1)
        here = pl.ds(pl.multiple_of(number * block_rows, 16), block_rows)
        queries = halves(q_ref[here, :])
        values = halves(v_ref[here, :])
        keys = k_ref[here, :]
        mixed = None
        for side in range(2):
            bias = jnp.where(padded, alone, table_ref[side, :, :block_rows])
            scores = nt(queries[side], keys) + bias
            raised = jnp.exp(scores - jnp.max(scores, axis=1, keepdims=True))
            weights = raised * (1.0 / jnp.sum(raised, axis=1, keepdims=True))
            weight_ref[side, number] = weights
            part = nn(weights.astype(BF16), values[side])
            mixed = part if mixed is None else mixed + part
        mixed_ref[here, :] = mixed.astype(BF16)
        return carry

    lax.fori_loop(0, IMGS, one, 0, unroll=True)


def attend(info, packed, table, block_rows):
    rows, three = packed.shape
    pairs = three // (3 * 128)
    heads, length, lanes = table.shape
    return pl.pallas_call(
        functools.partial(attend_body, block_rows),
        grid=(pairs,),
        in_specs=[
            smem(),
            pl.BlockSpec((rows, 128), lambda p: (0, p)),
            pl.BlockSpec((rows, 128), lambda p: (0, pairs + p)),
            pl.BlockSpec((rows, 128), lambda p: (0, 2 * pairs + p)),
            pl.BlockSpec((2, length, lanes), lambda p: (p, 0, 0)),
        ],
        out_specs=[
            pl.BlockSpec((rows, 128), lambda p: (0, p)),
            pl.BlockSpec((2, IMGS, block_rows, block_rows), lambda p: (p, 0, 0, 0)),
        ],
        out_shape=[
            jax.ShapeDtypeStruct((rows, pairs * 128), BF16),
            jax.ShapeDtypeStruct((heads, IMGS, block_rows, block_rows), F32),
        ],
        compiler_params=params(),
        cost_estimate=cost(6),
        name="attend",
    )(info, packed, packed, packed, table)


def attend_back_body(block_rows, scale, q_ref, k_ref, v_ref, weight_ref, grad_ref, *rest):
    packed_ref, table_ref = rest[-2:]
    for side in range(2):
        table_ref[side] = jnp.zeros(table_ref.shape[1:], F32)

    def one(number, carry):
        here = pl.ds(pl.multiple_of(number * block_rows, 16), block_rows)
        queries = halves(q_ref[here, :])
        keys = halves(k_ref[here, :])
        grads = halves(grad_ref[here, :])
        values = v_ref[here, :]
        dq = dk = dv = 0.0
        for side in range(2):
            weights = weight_ref[side, number]
            up = nt(grads[side], values)
            inner = jnp.sum(weights * up, axis=1, keepdims=True)
            score = (weights * (up - inner)).astype(BF16)
            dv += tn(weights.astype(BF16), grads[side])
            dq += nn(score, keys[side])
            dk += tn(score, queries[side])
            table_ref[side, :, :block_rows] += score.astype(F32)
        packed_ref[0, here, :] = (dq * scale).astype(BF16)
        packed_ref[1, here, :] = dk.astype(BF16)
        packed_ref[2, here, :] = dv.astype(BF16)
        return carry

    lax.fori_loop(0, IMGS, one, 0, unroll=True)


def attend_back(packed, weights, mixed_grad, head_dim, lanes, first, last, earlier=()):
    rows, three = packed.shape
    pairs = three // (3 * 128)
    heads, _, block_rows, _ = weights.shape
    part = pl.BlockSpec((rows, 128), lambda p: (0, first + p))
    return pl.pallas_call(
        functools.partial(attend_back_body, block_rows, head_dim**-0.5),
        grid=(last - first,),
        in_specs=[
            part,
            pl.BlockSpec((rows, 128), lambda p: (0, pairs + first + p)),
            pl.BlockSpec((rows, 128), lambda p: (0, 2 * pairs + first + p)),
            pl.BlockSpec((2, IMGS, block_rows, block_rows), lambda p: (first + p, 0, 0, 0)),
            part,
        ]
        + [pl.BlockSpec(memory_space=pl.ANY)] * len(earlier),
        out_specs=[
            pl.BlockSpec((3, rows, 128), lambda p: (0, 0, first + p)),
            pl.BlockSpec((2, block_rows, lanes), lambda p: (first + p, 0, 0)),
        ],
        out_shape=[
            jax.ShapeDtypeStruct((3, rows, pairs * 128), BF16),
            jax.ShapeDtypeStruct((heads, block_rows, lanes), F32),
        ],
        input_output_aliases={5: 0, 6: 1} if earlier else {},
        compiler_params=params(),
        cost_estimate=cost(4),
        name="attend_back",
    )(packed, packed, packed, weights, mixed_grad, *earlier)


def cumulative(values):
    squared = jnp.exp(-0.5 * values * values)
    size = jnp.abs(values) * ROOT_HALF
    t = 1.0 / (1.0 + 0.3275911 * size)
    poly = t * (
        0.254829592 + t * (-0.284496736 + t * (1.421413741 + t * (-1.453152027 + t * 1.061405429)))
    )
    tail = 0.5 * poly * squared
    return jnp.where(values < 0, tail, 1.0 - tail), squared * INV_ROOT_TAU


def normal(values):
    average = jnp.mean(values, axis=-1, keepdims=True)
    centred = values - average
    inverse = lax.rsqrt(jnp.mean(centred * centred, axis=-1, keepdims=True) + EPS)
    return centred * inverse, inverse


def column_sum(ref, row, values):
    ref[row : row + 1, :] = jnp.sum(values, axis=0, keepdims=True)


def add_column_sum(ref, row, values):
    ref[row : row + 1, :] += jnp.sum(values, axis=0, keepdims=True)


class Late:
    def __init__(self, sources, targets, sems):
        self.copies = [
            pltpu.make_async_copy(source, target, sems.at[number])
            for number, (source, target) in enumerate(zip(sources, targets, strict=True))
        ]

    def start(self):
        for copy in self.copies:
            copy.start()

    def wait(self):
        for copy in self.copies:
            copy.wait()


def feed_body(
    image,
    block_rows,
    info,
    order_ref,
    mixed_ref,
    xb_ref,
    up_ref,
    up_t_ref,
    vec_ref,
    bias_ref,
    out_w_ref,
    fc1_ref,
    fc2_ref,
    cb_any,
    out_ref,
    keep_ref,
    send_ref,
    fc1_sum_ref,
    mixed_grad_ref,
    after_grad_ref,
    sums_ref,
    ff_s,
    second_s,
    cb_s,
    after_s,
    branch_s,
    low_s,
    turned_s,
    sems,
):
    step = pl.program_id(0)
    last = pl.num_programs(0) - 1
    rows, width = xb_ref.shape
    late = Late((cb_any,), (cb_s,), sems)

    half = keep_ref.shape[1]
    side = width // 2

    def put_out_grad(here):
        there = pl.ds(pl.multiple_of(half + here.start, 16), here.size)
        for ref, rows_here in ((keep_ref, here), (send_ref, there)):
            values = nn(turned_s[rows_here, :], mixed_ref[...]).astype(BF16)
            ref[0, here, :side] = values[:, :side]
            ref[1, here, :side] = values[:, side:]

    def turn_low():
        def turned(here):
            order = row_order(order_ref[here, :], width)
            turned_s[here, :] = nt(order, low_s[...]).astype(BF16)

        in_chunks(width, width // 2, turned)

    @pl.when(step == 0)
    def _():
        late.start()
        ff_s[...] = jnp.zeros_like(ff_s)
        second_s[...] = jnp.zeros_like(second_s)

        def one(here):
            branch = nt(mixed_ref[here, :], out_w_ref[...]) + vec_ref[OUT_B : OUT_B + 1, :]
            branch_s[here, :] = branch
            after_attn = xb_ref[here, :].astype(F32) + vec_ref[GAM_A : GAM_A + 1, :] * branch
            after_s[here, :] = after_attn
            normed, _ = normal(after_attn)
            low_s[here, :] = (
                normed * vec_ref[LN2_G : LN2_G + 1, :] + vec_ref[LN2_B : LN2_B + 1, :]
            ).astype(BF16)

        in_chunks(rows, rows // 2, one)
        turn_low()

    @pl.when(step < last)
    def _():
        pre = nn(low_s[...], fc1_ref[...]) + bias_ref[0:1, :]
        phi, density = cumulative(pre)
        hidden = (pre * phi).astype(BF16)
        slope = phi + pre * density
        grad = (nn(up_ref[...], fc2_ref[...]) * slope).astype(BF16)
        ff_s[...] += nt(hidden, fc2_ref[...])
        second_s[...] += nt(grad, fc1_ref[...])
        for plane, values in enumerate((nn(turned_s[...], grad), nn(up_t_ref[...], hidden))):
            keep_ref[plane] = values[:half].astype(BF16)
            send_ref[plane] = values[half:].astype(BF16)
        fc1_sum_ref[...] = jnp.broadcast_to(
            jnp.sum(grad.astype(F32), axis=0, keepdims=True), fc1_sum_ref.shape
        )

    @pl.when(step == last)
    def _():
        late.wait()
        sums_ref[...] = jnp.zeros_like(sums_ref)

        def finish(here):
            cot = cb_s[here, :].astype(F32)
            normed, inverse = normal(after_s[here, :])
            second = second_s[here, :]
            add_column_sum(sums_ref, G_LN2_G, second * normed)
            add_column_sum(sums_ref, G_LN2_B, second)
            scaled = second * vec_ref[LN2_G : LN2_G + 1, :]
            inner = jnp.mean(scaled, axis=-1, keepdims=True)
            along = jnp.mean(scaled * normed, axis=-1, keepdims=True)
            after_grad = cot + inverse * (scaled - inner - normed * along)
            after_grad_ref[here, :] = after_grad
            add_column_sum(sums_ref, G_GAM_A, after_grad * branch_s[here, :])
            low = (vec_ref[GAM_A : GAM_A + 1, :] * after_grad).astype(BF16)
            low_s[here, :] = low
            add_column_sum(sums_ref, G_OUT_B, low.astype(F32))
            mixed_grad_ref[here, :] = nn(low, out_w_ref[...]).astype(BF16)
            branch = ff_s[here, :] + vec_ref[FC2_B : FC2_B + 1, :]
            add_column_sum(sums_ref, G_GAM_M, cot * branch)
            add_column_sum(sums_ref, G_FC2_B, up_ref[here, :].astype(F32))
            cb_s[here, :] = (after_s[here, :] + vec_ref[GAM_M : GAM_M + 1, :] * branch).astype(BF16)

        in_chunks(rows, rows // 4, finish)
        turn_low()
        in_chunks(half, half // 2, put_out_grad)
        out_ref[...] = restore_rows(
            info[0], cb_s[...], block_rows, image, out_ref.shape[0]
        ).astype(BF16)


def feed(
    info,
    order,
    mixed,
    xb,
    up,
    up_t,
    vec,
    fc1b,
    weights,
    cb,
    image,
    block_rows,
    length,
    tile,
):
    rows, width = xb.shape
    hidden = fc1b.shape[1]
    steps = hidden // tile
    anywhere = pl.BlockSpec(memory_space=pl.ANY)
    once = pl.Buffered(1)

    def at(i):
        return jnp.minimum(i, steps - 1)

    def fixed(shape):
        return pl.BlockSpec(shape, lambda i: (0, 0), pipeline_mode=once)

    return pl.pallas_call(
        functools.partial(feed_body, image, block_rows),
        grid=(steps + 1,),
        in_specs=[
            smem(),
            fixed((width, 1)),
            fixed((rows, width)),
            fixed((rows, width)),
            fixed((rows, width)),
            fixed((width, rows)),
            fixed(vec.shape),
            pl.BlockSpec((8, tile), lambda i: (0, at(i))),
            pl.BlockSpec((width, width), lambda i: (0, 2 * hidden // width), pipeline_mode=once),
            pl.BlockSpec((width, tile), lambda i: (0, at(i))),
            pl.BlockSpec((width, tile), lambda i: (0, steps + at(i))),
        ]
        + [anywhere],
        out_specs=[
            full((length, width)),
            pl.BlockSpec((2, width // 2, tile), lambda i: (0, 0, i)),
            pl.BlockSpec((2, width // 2, tile), lambda i: (0, 0, i)),
            pl.BlockSpec((8, tile), lambda i: (0, at(i))),
            full((rows, width)),
            full((rows, width)),
            full((16, width)),
        ],
        out_shape=[
            jax.ShapeDtypeStruct((length, width), BF16),
            jax.ShapeDtypeStruct((2, width // 2, hidden + width // 2), BF16),
            jax.ShapeDtypeStruct((2, width // 2, hidden + width // 2), BF16),
            jax.ShapeDtypeStruct((8, hidden), F32),
            jax.ShapeDtypeStruct((rows, width), BF16),
            jax.ShapeDtypeStruct((rows, width), F32),
            jax.ShapeDtypeStruct((16, width), F32),
        ],
        scratch_shapes=[
            pltpu.VMEM((rows, width), F32),
            pltpu.VMEM((rows, width), F32),
            pltpu.VMEM((rows, width), BF16),
            pltpu.VMEM((rows, width), F32),
            pltpu.VMEM((rows, width), F32),
            pltpu.VMEM((rows, width), BF16),
            pltpu.VMEM((width, rows), BF16),
            pltpu.SemaphoreType.DMA((1,)),
        ],
        compiler_params=params(),
        cost_estimate=cost(28),
        name="feed",
    )(
        info,
        order,
        mixed,
        xb,
        up,
        up_t,
        vec,
        fc1b,
        weights,
        weights,
        weights,
        cb,
    )


def weight_grad_body(low_t_ref, packed_ref, keep_ref, send_ref):
    half = keep_ref.shape[0]
    keep_ref[...] = nn(low_t_ref[:half], packed_ref[...]).astype(BF16)
    send_ref[...] = nn(low_t_ref[half:], packed_ref[...]).astype(BF16)


def weight_grad(low_t, packed_grad):
    width, rows = low_t.shape
    return pl.pallas_call(
        weight_grad_body,
        grid=(3,),
        in_specs=[full((width, rows)), pl.BlockSpec((None, rows, width), lambda i: (i, 0, 0))],
        out_specs=[pl.BlockSpec((width // 2, width), lambda i: (0, i))] * 2,
        out_shape=[jax.ShapeDtypeStruct((width // 2, 3 * width), BF16)] * 2,
        compiler_params=params(),
        cost_estimate=cost(5),
        name="weight_grad",
    )(low_t, packed_grad)


def input_grad_body(
    image,
    block_rows,
    info,
    packed_ref,
    weight_ref,
    vec_ref,
    normed_any,
    inv_any,
    after_grad_any,
    out_ref,
    sums_ref,
    first_s,
    normed_s,
    inv_s,
    after_grad_s,
    result_s,
    sems,
):
    step = pl.program_id(0)
    late = Late((normed_any, inv_any, after_grad_any), (normed_s, inv_s, after_grad_s), sems)

    @pl.when(step == 0)
    def _():
        late.start()
        first_s[...] = jnp.zeros_like(first_s)
        sums_ref[...] = jnp.zeros_like(sums_ref)
        column_sum(sums_ref, G_Q_B, packed_ref[...].astype(F32))

    def one(here):
        first_s[here, :] += nt(packed_ref[here, :], weight_ref[...])

    in_chunks(first_s.shape[0], first_s.shape[0] // 2, one)

    @pl.when(step == 2)
    def _():
        late.wait()
        column_sum(sums_ref, G_V_B, packed_ref[...].astype(F32))

        def finish(here):
            first = first_s[here, :]
            normed = normed_s[here, :]
            add_column_sum(sums_ref, G_LN1_G, first * normed)
            add_column_sum(sums_ref, G_LN1_B, first)
            scaled = first * vec_ref[LN1_G : LN1_G + 1, :]
            inner = jnp.mean(scaled, axis=-1, keepdims=True)
            along = jnp.mean(scaled * normed, axis=-1, keepdims=True)
            back = inv_s[here, :1] * (scaled - inner - normed * along)
            result_s[here, :] = (after_grad_s[here, :] + back).astype(BF16)

        in_chunks(first_s.shape[0], first_s.shape[0] // 4, finish)
        out_ref[...] = restore_rows(
            info[0], result_s[...], block_rows, image, out_ref.shape[0]
        ).astype(BF16)


def input_grad(info, packed_grad, weights, vec, normed, inv, after_grad, image, block_rows, length):
    rows, width = normed.shape
    anywhere = pl.BlockSpec(memory_space=pl.ANY)
    return pl.pallas_call(
        functools.partial(input_grad_body, image, block_rows),
        grid=(3,),
        in_specs=[
            smem(),
            pl.BlockSpec((None, rows, width), lambda i: (i, 0, 0)),
            pl.BlockSpec((width, width), lambda i: (0, i)),
            full(vec.shape),
            anywhere,
            anywhere,
            anywhere,
        ],
        out_specs=[full((length, width)), full((16, width))],
        out_shape=[
            jax.ShapeDtypeStruct((length, width), BF16),
            jax.ShapeDtypeStruct((16, width), F32),
        ],
        scratch_shapes=[
            pltpu.VMEM((rows, width), F32),
            pltpu.VMEM((rows, width), F32),
            pltpu.VMEM((rows, 128), F32),
            pltpu.VMEM((rows, width), F32),
            pltpu.VMEM((rows, width), BF16),
            pltpu.SemaphoreType.DMA((3,)),
        ],
        compiler_params=params(),
        cost_estimate=cost(8),
        name="input_grad",
    )(info, packed_grad, weights, vec, normed, inv, after_grad)


def table_grad_body(heads, groups, table_ref, index_ref, out_ref, acc):
    lanes = index_ref.shape[1]
    parts = out_ref.shape[1] // 128
    acc[...] = jnp.zeros_like(acc)
    slots = lax.broadcasted_iota(jnp.int32, (128, lanes), 0).astype(F32).astype(BF16)
    one_bf, zero_bf = jnp.ones((), BF16), jnp.zeros((), BF16)
    zero = jnp.zeros((), BF16)
    group = 8

    def one(step, carry):
        at = pl.ds(pl.multiple_of(step * group, group), group)
        indices = index_ref[at, :]
        lows = jnp.bitwise_and(indices, 127).astype(F32)
        highs = jnp.right_shift(indices, 7).astype(F32)
        values = table_ref[:, at, :]
        left, right = [], []
        for row in range(group):
            low = jnp.broadcast_to(lows[row : row + 1, :], (16, lanes)).astype(BF16)
            high = jnp.broadcast_to(highs[row : row + 1, :], (16, lanes)).astype(BF16)
            right.append(
                jnp.concatenate(
                    [
                        jnp.where(slots[start : start + 16] == low, one_bf, zero_bf)
                        for start in range(0, 128, 16)
                    ],
                    axis=0,
                )
            )
            here = jnp.concatenate(
                [values[:, row, :], jnp.zeros((16 - heads, lanes), F32)], axis=0
            )
            coarse = here.astype(BF16)
            fine = (here - coarse.astype(F32)).astype(BF16)
            masks = [high == jnp.asarray(part, BF16) for part in range(parts)]
            left.append(
                jnp.concatenate(
                    [jnp.where(mask, kind, zero) for kind in (coarse, fine) for mask in masks],
                    axis=0,
                )
            )
        acc[...] += nt(jnp.concatenate(left, axis=1), jnp.concatenate(right, axis=1))
        return carry

    lax.fori_loop(groups[0], groups[1], one, 0)
    half = parts * 16
    for part in range(parts):
        out_ref[:, part * 128 : (part + 1) * 128] = (
            acc[part * 16 : (part + 1) * 16, :] + acc[half + part * 16 : half + (part + 1) * 16, :]
        )


def table_grad(table, index, slots, groups):
    heads, length, lanes = table.shape
    return pl.pallas_call(
        functools.partial(table_grad_body, heads, groups),
        grid=(1,),
        in_specs=[full(table.shape), full(index.shape)],
        out_specs=full((16, slots)),
        out_shape=jax.ShapeDtypeStruct((16, slots), F32),
        scratch_shapes=[pltpu.VMEM((2 * 16 * slots // 128, 128), F32)],
        compiler_params=params(),
        cost_estimate=cost(8),
        name="table_grad",
    )(table, index)


def local(
    inputs,
    cotangent,
    segment_ids,
    keep_rows,
    index_map,
    ln1_gain,
    ln1_bias,
    qkv_weight,
    qv_bias,
    out_weight,
    out_bias,
    gamma_attn,
    rel_table,
    ln2_gain,
    ln2_bias,
    fc1_weight,
    fc1_bias,
    fc2_weight,
    fc2_bias,
    gamma_mlp,
):
    _, length, width = inputs.shape
    heads, per_device = rel_table.shape
    head_dim = width // heads
    own = ln1_gain.shape[0]
    count = width // own
    hidden = fc1_weight.shape[1]
    image = index_map.shape[0]
    block_rows = -(-image // 16) * 16

    keep = keep_rows[0] == 1
    ids = lax.iota(jnp.int32, length)
    info = jnp.stack([jnp.min(jnp.where(keep, ids, length)), jnp.max(jnp.where(keep, 0, 1))])
    moved = index_map // per_device * own + index_map % per_device
    moved = jnp.pad(moved, ((0, block_rows - image), (0, 256 - image)), constant_values=-1)

    small_rows = [
        ln1_gain[None],
        ln1_bias[None],
        qv_bias,
        out_bias[None],
        gamma_attn[None],
        ln2_gain[None],
        ln2_bias[None],
        fc2_bias[None],
        gamma_mlp[None],
    ]
    owners = exchange_owners(count, 0)

    def row_places(owning):
        return (owning[:, None] * own + jnp.arange(own, dtype=jnp.int32)).reshape(-1, 1)

    order, qkv_order = row_places(owners), row_places(exchange_owners(count, 1))
    later = lax.all_gather(
        jnp.concatenate([fc1_weight, fc2_weight.T, out_weight.T], axis=1), AX, axis=0, tiled=True
    )
    xb, cb, normed, inv = prepare(info, inputs[0], cotangent[0], image, block_rows)
    small = pack(small_rows, fc1_bias[None], rel_table, FC1_B, TABLE, hidden // width)
    small = jnp.broadcast_to(after(small, xb)[None], (count, own, SMALL))
    small = lax.all_to_all(small, AX, 0, 0, tiled=True).reshape(width, SMALL)
    vec, fc1b, table = expand(small, moved, heads, hidden)
    mine, got = gather_halves(qkv_weight, count, [(xb,), (small,), (table,)])
    packed, low, qkv_full = project(owners, normed, vec, mine, got, head_dim)
    qkv_full = qkv_full.reshape(width, -1)
    mixed, weights = attend(info, packed, table, block_rows)
    up, up_t, low_t = turn(order, qkv_order, vec, after(cb, mixed), low)
    tile = 1024
    out, feed_keep, feed_send, fc1_sum, mixed_grad, after_grad, sums2 = feed(
        info,
        order,
        mixed,
        xb,
        up,
        up_t,
        vec,
        fc1b,
        later,
        cb,
        image,
        block_rows,
        length,
        tile,
    )
    pairs = heads // 2
    some = attend_back(packed, weights, mixed_grad, head_dim, 256, 0, pairs // 2)
    a_pieces, a_send = scatter_step(0, [feed_keep], feed_send, 0, count, some[0])
    packed_grad, table_sum = attend_back(
        packed, weights, after(mixed_grad, a_send), head_dim, 256, pairs // 2, pairs, some
    )
    qkv_keep, qkv_send = weight_grad(low_t, packed_grad)
    biases = after(fc1_sum, qkv_keep)[0].reshape(count, -1, own)
    b_pieces, b_send = scatter_step(1, [qkv_keep], qkv_send, 0, count, biases)
    in_grad, sums1 = input_grad(
        info,
        packed_grad,
        qkv_full,
        vec,
        normed,
        after(inv, b_send),
        after_grad,
        image,
        block_rows,
        length,
    )
    groups = -(-image // 8)
    slots = own * count
    a_pieces, a_send = scatter_step(0, a_pieces, a_send, 1, count, in_grad)
    slot_sums = table_grad(after(table_sum, a_send), moved, slots, (0, groups // 2))
    b_pieces, b_send = scatter_step(1, b_pieces, b_send, 1, count, slot_sums)
    more_sums = table_grad(after(table_sum, b_send), moved, slots, (groups // 2, groups))
    a_pieces, a_send = scatter_step(0, a_pieces, a_send, 2, count, more_sums)
    b_pieces, b_send = scatter_step(1, b_pieces, b_send, 2, count, a_send)
    slot_sums = slot_sums + after(more_sums, b_send)

    rows = jnp.concatenate([sums1[:10] + sums2[:10], slot_sums[:heads]], axis=0)
    rows = jnp.transpose(rows.reshape(-1, count, own), (1, 0, 2))
    swapped = lax.all_to_all(jnp.concatenate([rows, biases], axis=1), AX, 0, 0, tiled=True)
    a_pieces, a_send = scatter_step(0, a_pieces, a_send, 3, count, swapped)
    b_pieces, b_send = scatter_step(1, b_pieces, b_send, 3, count, a_send)
    late_send = b_send
    for step in range(4, count.bit_length() - 1):
        a_pieces, a_send = scatter_step(0, a_pieces, a_send, step, count, b_send)
    for step in range(4, count.bit_length() - 1):
        b_pieces, b_send = scatter_step(1, b_pieces, b_send, step, count, a_pieces)
    feed_wide, qkv_shard = a_pieces, b_pieces
    small_shard = jnp.sum(after(swapped, late_send), axis=0)

    grad_fc1 = feed_wide[0, :, :hidden]
    grad_fc2 = feed_wide[1, :, :hidden].T
    grad_out = jnp.concatenate([feed_wide[0, :, hidden:], feed_wide[1, :, hidden:]], axis=1).T
    grad_table = small_shard[10 : 10 + heads, :per_device]
    grad_fc1_bias = small_shard[10 + heads :].reshape(-1)
    return (
        out[None],
        in_grad[None],
        small_shard[G_LN1_G],
        small_shard[G_LN1_B],
        qkv_shard,
        small_shard[G_Q_B : G_V_B + 1],
        grad_out,
        small_shard[G_OUT_B],
        small_shard[G_GAM_A],
        grad_table,
        small_shard[G_LN2_G],
        small_shard[G_LN2_B],
        grad_fc1,
        grad_fc1_bias,
        grad_fc2,
        small_shard[G_FC2_B],
        small_shard[G_GAM_M],
    )


def solution(mesh):
    rows = P(AX)
    columns = P(None, AX)
    return jax.shard_map(
        local,
        mesh=mesh,
        in_specs=(
            rows,
            rows,
            rows,
            rows,
            P(),
            rows,
            rows,
            rows,
            columns,
            columns,
            rows,
            rows,
            columns,
            rows,
            rows,
            rows,
            rows,
            columns,
            rows,
            rows,
        ),
        out_specs=(
            rows,
            rows,
            rows,
            rows,
            rows,
            columns,
            columns,
            rows,
            rows,
            columns,
            rows,
            rows,
            rows,
            rows,
            columns,
            rows,
            rows,
        ),
        check_vma=False,
    )
```

```python
import functools
import jax
import jax.numpy as jnp
from jax import lax
from jax.experimental import pallas as pl
from jax.experimental.pallas import tpu as pltpu
from jax.sharding import PartitionSpec as P

AX = ("dp", "fsdp")
IMGS = 4
EPS = 1e-06
MASKED = -1e30
ROOT_HALF = 0.7071067811865476
INV_ROOT_TAU = 0.3989422804014327
F32 = jnp.float32
BF16 = jnp.bfloat16
VMEM_LIMIT = 60 * 1024 * 1024

LN1_G, LN1_B, Q_B, V_B, OUT_B, GAM_A, LN2_G, LN2_B, FC2_B, GAM_M = range(10)
FC1_B = 16
TABLE = 32
SMALL = 128
G_LN1_G, G_LN1_B, G_Q_B, G_V_B, G_OUT_B, G_GAM_A, G_LN2_G, G_LN2_B, G_FC2_B, G_GAM_M = range(10)


def nn(a, b):
    return lax.dot_general(a, b, (((1,), (0,)), ((), ())), preferred_element_type=F32)


def nt(a, b):
    return lax.dot_general(a, b, (((1,), (1,)), ((), ())), preferred_element_type=F32)


def tn(a, b):
    return lax.dot_general(a, b, (((0,), (0,)), ((), ())), preferred_element_type=F32)


def full(shape):
    return pl.BlockSpec(shape, lambda *_: (0,) * len(shape))


def cost(gigaflops, megabytes=4):
    return pl.CostEstimate(
        flops=int(gigaflops * 2e7), bytes_accessed=int(megabytes * 2e4), transcendentals=0
    )


def after(value, *others):
    return lax.optimization_barrier((value, others))[0]


def params(grid_rank=1):
    return pltpu.CompilerParams(
        dimension_semantics=("arbitrary",) * grid_rank, vmem_limit_bytes=VMEM_LIMIT
    )


def smem():
    return pl.BlockSpec(memory_space=pltpu.SMEM)


def exchange_orders(count, kind):
    bits = count.bit_length() - 1
    if bits < 3:
        return (list(range(bits)),) * 2
    rest = list(range(2, bits - 1))
    outer = [1, bits - 1]
    if kind == 0:
        return [0] + outer + rest, [0] + outer[::-1] + rest[::-1]
    return [0] + rest + outer, [0] + rest[::-1] + outer[::-1]


def exchange(values, step, count, kind):
    orders = exchange_orders(count, kind)
    return lax.ppermute(values, AX, [(i, i ^ (1 << orders[i & 1][step])) for i in range(count)])


def exchange_owners(count, kind):
    orders = exchange_orders(count, kind)
    bits = len(orders[0])
    me = lax.axis_index(AX)
    spot = jnp.arange(count, dtype=jnp.int32)
    other = spot >> (bits - 1) if bits else spot
    kind = jnp.bitwise_xor(jnp.bitwise_and(me, 1), other)
    flips = other
    for step in range(1, bits):
        bit = jnp.bitwise_and(spot >> (bits - 1 - step), 1)
        flips = jnp.bitwise_or(
            flips, bit << jnp.where(kind == 1, orders[1][step], orders[0][step])
        )
    return jnp.bitwise_xor(me, flips)


def gather_halves(values, count, before):
    for number, step in enumerate(reversed(range(count.bit_length() - 1))):
        got = exchange(values, step, count, 0)
        if number < len(before):
            got = after(got, *before[number])
        if step == 0:
            return values, got
        values = jnp.concatenate([values, got], axis=0)
    half = values.shape[0] // 2
    return values[:half], values[half:]


def scatter_step(kind, pieces, send, step, count, *others):
    got = after(exchange(send, step, count, kind), *others)
    pieces = pieces + [got]
    rows = got.shape[-2]

    def total(start, stop):
        return sum(piece[..., start:stop, :].astype(F32) for piece in pieces)

    if step == count.bit_length() - 2:
        return total(0, rows), None
    return pieces, total(rows // 2, rows).astype(BF16)


def in_chunks(rows, size, body):
    def one(number, carry):
        body(pl.ds(pl.multiple_of(number * size, 16), size))
        return carry

    lax.fori_loop(0, rows // size, one, 0)


def row_order(column, width):
    rows = column.shape[0]
    return (lax.broadcasted_iota(jnp.int32, (rows, width), 1) == column).astype(BF16)


def block_source(first, number, rows, image, length):
    at = first + image * number + rows
    at = jnp.where(at >= length, at - length, at)
    return jnp.where(rows < image, at, -1)


def place_rows(first, source, target_rows, image):
    length = source.shape[0]

    def one(number):
        rows = lax.broadcasted_iota(jnp.int32, (target_rows, 1), 0)
        wanted = block_source(first, number, rows, image, length)
        columns = lax.broadcasted_iota(jnp.int32, (target_rows, length), 1)
        return nn((columns == wanted).astype(BF16), source)

    return one


def restore_body(image, block_rows, info, *refs):
    sources, targets = refs[: len(refs) // 2], refs[len(refs) // 2 :]
    length = targets[0].shape[0]
    lanes = lax.broadcasted_iota(jnp.int32, (1, block_rows), 1)
    wanted = jnp.concatenate(
        [block_source(info[0], number, lanes, image, length) for number in range(IMGS)], axis=1
    )
    rows = lax.broadcasted_iota(jnp.int32, (length, IMGS * block_rows), 0)
    back = (rows == wanted).astype(BF16)
    for source, target in zip(sources, targets, strict=True):
        target[...] = nn(back, source[...]).astype(BF16)


def restore(info, image, block_rows, length, *blocked):
    rows, width = blocked[0].shape
    return pl.pallas_call(
        functools.partial(restore_body, image, block_rows),
        grid=(1,),
        in_specs=[smem()] + [full((rows, width))] * len(blocked),
        out_specs=[full((length, width))] * len(blocked),
        out_shape=[jax.ShapeDtypeStruct((length, width), BF16)] * len(blocked),
        compiler_params=params(),
        cost_estimate=cost(4),
        name="restore",
    )(info, *blocked)


def pack_body(bias_at, table_at, ratio, bias_ref, table_ref, *rest):
    *row_refs, out_ref, rows_s = rest
    own = out_ref.shape[0]
    rows_s[...] = jnp.zeros_like(rows_s)
    at_row = 0
    for ref in row_refs:
        rows_s[at_row : at_row + ref.shape[0], :] = ref[...].astype(F32)
        at_row += ref.shape[0]
    heads, slots = table_ref.shape
    rows_s[table_at : table_at + heads, :slots] = table_ref[...].astype(F32)
    eye = (
        lax.broadcasted_iota(jnp.int32, (own, own), 0)
        == lax.broadcasted_iota(jnp.int32, (own, own), 1)
    ).astype(BF16)
    small = nt(eye, rows_s[...].astype(BF16))
    biases = jnp.broadcast_to(bias_ref[...].astype(F32), (own, own * ratio))
    at = lax.broadcasted_iota(jnp.int32, (own, own * ratio), 1)
    row = lax.broadcasted_iota(jnp.int32, (own, own * ratio), 0)
    lane = lax.broadcasted_iota(jnp.int32, (own, SMALL), 1)
    for number in range(ratio):
        column = jnp.sum(
            jnp.where(at == row * ratio + number, biases, 0.0), axis=1, keepdims=True
        )
        small = small + jnp.where(lane == bias_at + number, column, 0.0)
    out_ref[...] = small.astype(BF16)


def pack(rows, bias, table, bias_at, table_at, ratio):
    own = rows[0].shape[1]
    operands = (bias, table, *rows)
    return pl.pallas_call(
        functools.partial(pack_body, bias_at, table_at, ratio),
        grid=(1,),
        in_specs=[full(value.shape) for value in operands],
        out_specs=full((own, SMALL)),
        out_shape=jax.ShapeDtypeStruct((own, SMALL), BF16),
        scratch_shapes=[pltpu.VMEM((SMALL, own), F32)],
        compiler_params=params(),
        name="pack",
    )(*operands)


def prepare_body(image, block_rows, info, x_ref, cot_ref, xb_ref, cb_ref, normed_ref, inv_ref):
    first = info[0]

    def one(number, carry):
        here = pl.ds(pl.multiple_of(number * block_rows, 16), block_rows)
        values = place_rows(first, x_ref[...], block_rows, image)(number)
        xb_ref[here, :] = values.astype(BF16)
        normed, inverse = normal(values)
        normed_ref[here, :] = normed
        inv_ref[here, :] = jnp.broadcast_to(inverse, (block_rows, 128))
        cb_ref[here, :] = place_rows(first, cot_ref[...], block_rows, image)(number).astype(BF16)
        return carry

    lax.fori_loop(0, IMGS, one, 0)


def prepare(info, x, cot, image, block_rows):
    length, width = x.shape
    rows = IMGS * block_rows
    return pl.pallas_call(
        functools.partial(prepare_body, image, block_rows),
        grid=(1,),
        in_specs=[smem(), full((length, width)), full((length, width))],
        out_specs=[full((rows, width))] * 3 + [full((rows, 128))],
        out_shape=[
            jax.ShapeDtypeStruct((rows, width), BF16),
            jax.ShapeDtypeStruct((rows, width), BF16),
            jax.ShapeDtypeStruct((rows, width), F32),
            jax.ShapeDtypeStruct((rows, 128), F32),
        ],
        compiler_params=params(),
        cost_estimate=cost(4),
        name="prepare",
    )(info, x, cot)


def expand_body(heads, small_ref, index_ref, vec_ref, fc1b_ref, table_ref, entries_s):
    eye = (
        lax.broadcasted_iota(jnp.int32, (SMALL, SMALL), 0)
        == lax.broadcasted_iota(jnp.int32, (SMALL, SMALL), 1)
    ).astype(BF16)
    width = small_ref.shape[0]
    hidden = fc1b_ref.shape[1]
    ratio = hidden // width
    rows = nt(eye, small_ref[...])
    vec_ref[...] = rows[: vec_ref.shape[0]]
    spread = (
        lax.broadcasted_iota(jnp.int32, (width, hidden), 0)
        == lax.broadcasted_iota(jnp.int32, (width, hidden), 1) // ratio
    ).astype(BF16)
    wide = nn(rows[FC1_B : FC1_B + 8].astype(BF16), spread)
    which = lax.broadcasted_iota(jnp.int32, (8, hidden), 1) % ratio
    mine = lax.broadcasted_iota(jnp.int32, (8, hidden), 0)
    total = jnp.sum(jnp.where(which == mine, wide, 0.0), axis=0, keepdims=True)
    fc1b_ref[...] = jnp.broadcast_to(total, fc1b_ref.shape)
    length, lanes = index_ref.shape
    parts = width // 128
    for head in range(heads):
        for part in range(parts):
            entries_s[head * parts + part] = jnp.broadcast_to(
                rows[TABLE + head : TABLE + head + 1, part * 128 : (part + 1) * 128], (8, 128)
            )

    def one(step, carry):
        at = pl.ds(pl.multiple_of(step * 8, 8), 8)
        for half in range(lanes // 128):
            columns = slice(half * 128, (half + 1) * 128)
            index = index_ref[at, columns]
            low = jnp.bitwise_and(index, 127)
            high = jnp.right_shift(index, 7)
            found = [jnp.full((8, 128), MASKED, F32)] * heads
            for part in range(parts):
                chosen = high == part
                for head in range(heads):
                    taken = jnp.take_along_axis(
                        entries_s[head * parts + part], low, axis=1, mode="promise_in_bounds"
                    )
                    found[head] = jnp.where(chosen, taken, found[head])
            for head in range(heads):
                table_ref[head, at, columns] = found[head]
        return carry

    lax.fori_loop(0, length // 8, one, 0)


def expand(small, index, heads, hidden):
    width = small.shape[0]
    length, lanes = index.shape
    return pl.pallas_call(
        functools.partial(expand_body, heads),
        grid=(1,),
        in_specs=[
            full((width, SMALL)),
            full((length, lanes)),
        ],
        out_specs=[full((64, width)), full((8, hidden)), full((heads, length, lanes))],
        out_shape=[
            jax.ShapeDtypeStruct((64, width), F32),
            jax.ShapeDtypeStruct((8, hidden), F32),
            jax.ShapeDtypeStruct((heads, length, lanes), F32),
        ],
        scratch_shapes=[pltpu.VMEM((heads * width // 128, 8, 128), F32)],
        compiler_params=params(),
        cost_estimate=cost(5),
        name="expand",
    )(small, index)


def project_body(
    scale,
    owners,
    normed_ref,
    vec_ref,
    mine_any,
    got_any,
    packed_ref,
    low_ref,
    weight_any,
    weight_s,
    sems,
    out_sem,
):
    step = pl.program_id(0)
    half = mine_any.shape[0]
    width = normed_ref.shape[1]
    keeping = pltpu.make_async_copy(weight_s, weight_any, out_sem)

    @pl.when(step == 0)
    def _():
        copies = []
        for spot in range(2 * half):
            source = mine_any.at[spot] if spot < half else got_any.at[spot - half]
            copy = pltpu.make_async_copy(source, weight_s.at[owners[spot]], sems.at[spot])
            copy.start()
            copies.append(copy)
        low_ref[...] = (
            normed_ref[...] * vec_ref[LN1_G : LN1_G + 1, :] + vec_ref[LN1_B : LN1_B + 1, :]
        ).astype(BF16)
        for copy in copies:
            copy.wait()
        keeping.start()

    bias = jnp.where(
        step == 0,
        vec_ref[Q_B : Q_B + 1, :],
        jnp.where(step == 2, vec_ref[V_B : V_B + 1, :], 0.0),
    )
    columns = pl.ds(pl.multiple_of(step * width, 128), width)
    weight = weight_s[:, :, columns].reshape(width, width)
    result = (nn(low_ref[...], weight) + bias).astype(BF16)
    packed_ref[...] = (result.astype(F32) * jnp.where(step == 0, scale, 1.0)).astype(BF16)

    @pl.when(step == 2)
    def _():
        keeping.wait()


def project(owners, normed, vec, mine, got, head_dim):
    rows, width = normed.shape
    count = owners.shape[0]
    wide = mine.shape[1]
    own = width // count
    anywhere = pl.BlockSpec(memory_space=pl.ANY)
    half = -(-count // 2)
    return pl.pallas_call(
        functools.partial(project_body, head_dim**-0.5),
        grid=(3,),
        in_specs=[smem(), full((rows, width)), full(vec.shape), anywhere, anywhere],
        out_specs=[
            pl.BlockSpec((rows, width), lambda i: (0, i)),
            full((rows, width)),
            anywhere,
        ],
        out_shape=[
            jax.ShapeDtypeStruct((rows, wide), BF16),
            jax.ShapeDtypeStruct((rows, width), BF16),
            jax.ShapeDtypeStruct((count, own, wide), BF16),
        ],
        scratch_shapes=[
            pltpu.VMEM((count, own, wide), BF16),
            pltpu.SemaphoreType.DMA((2 * half,)),
            pltpu.SemaphoreType.DMA,
        ],
        compiler_params=params(),
        cost_estimate=cost(4),
        name="project",
    )(owners, normed, vec, mine.reshape(half, own, wide), got.reshape(half, own, wide))


def turn_body(order_ref, qkv_order_ref, vec_ref, cb_ref, low_ref, up_ref, up_t_ref, low_t_ref):
    up_ref[...] = (vec_ref[GAM_M : GAM_M + 1, :] * cb_ref[...].astype(F32)).astype(BF16)
    width = low_ref.shape[1]

    def turned(here):
        up_t_ref[here, :] = nt(row_order(order_ref[here, :], width), up_ref[...]).astype(BF16)
        qkv_order = row_order(qkv_order_ref[here, :], width)
        low_t_ref[here, :] = nt(qkv_order, low_ref[...]).astype(BF16)

    in_chunks(width, width // 2, turned)


def turn(order, qkv_order, vec, cb, low):
    rows, width = cb.shape
    return pl.pallas_call(
        turn_body,
        grid=(1,),
        in_specs=[full((width, 1))] * 2
        + [full(vec.shape), full((rows, width)), full((rows, width))],
        out_specs=[full((rows, width)), full((width, rows)), full((width, rows))],
        out_shape=[
            jax.ShapeDtypeStruct((rows, width), BF16),
            jax.ShapeDtypeStruct((width, rows), BF16),
            jax.ShapeDtypeStruct((width, rows), BF16),
        ],
        compiler_params=params(),
        cost_estimate=cost(3),
        name="turn",
    )(order, qkv_order, vec, cb, low)


def halves(values):
    lanes = lax.broadcasted_iota(jnp.int32, values.shape, 1)
    zero = jnp.zeros((), values.dtype)
    side = values.shape[1] // 2
    return (jnp.where(lanes < side, values, zero), jnp.where(lanes >= side, values, zero))


def attend_body(block_rows, info, q_ref, k_ref, v_ref, table_ref, mixed_ref, weight_ref):
    rows = lax.broadcasted_iota(jnp.int32, (block_rows, block_rows), 0)
    columns = lax.broadcasted_iota(jnp.int32, (block_rows, block_rows), 1)
    alone = jnp.where(rows == columns, 0.0, MASKED)

    def one(number, carry):
        padded = jnp.logical_and(info[1] == 1, number == IMGS - 1)
        here = pl.ds(pl.multiple_of(number * block_rows, 16), block_rows)
        queries = halves(q_ref[here, :])
        values = halves(v_ref[here, :])
        keys = k_ref[here, :]
        mixed = None
        for side in range(2):
            bias = jnp.where(padded, alone, table_ref[side, :, :block_rows])
            scores = nt(queries[side], keys) + bias
            raised = jnp.exp(scores - jnp.max(scores, axis=1, keepdims=True))
            weights = raised * (1.0 / jnp.sum(raised, axis=1, keepdims=True))
            weight_ref[side, number] = weights
            part = nn(weights.astype(BF16), values[side])
            mixed = part if mixed is None else mixed + part
        mixed_ref[here, :] = mixed.astype(BF16)
        return carry

    lax.fori_loop(0, IMGS, one, 0, unroll=True)


def attend(info, packed, table, block_rows):
    rows, three = packed.shape
    pairs = three // (3 * 128)
    heads, length, lanes = table.shape
    return pl.pallas_call(
        functools.partial(attend_body, block_rows),
        grid=(pairs,),
        in_specs=[
            smem(),
            pl.BlockSpec((rows, 128), lambda p: (0, p)),
            pl.BlockSpec((rows, 128), lambda p: (0, pairs + p)),
            pl.BlockSpec((rows, 128), lambda p: (0, 2 * pairs + p)),
            pl.BlockSpec((2, length, lanes), lambda p: (p, 0, 0)),
        ],
        out_specs=[
            pl.BlockSpec((rows, 128), lambda p: (0, p)),
            pl.BlockSpec((2, IMGS, block_rows, block_rows), lambda p: (p, 0, 0, 0)),
        ],
        out_shape=[
            jax.ShapeDtypeStruct((rows, pairs * 128), BF16),
            jax.ShapeDtypeStruct((heads, IMGS, block_rows, block_rows), F32),
        ],
        compiler_params=params(),
        cost_estimate=cost(6),
        name="attend",
    )(info, packed, packed, packed, table)


def attend_back_body(block_rows, scale, q_ref, k_ref, v_ref, weight_ref, grad_ref, *rest):
    packed_ref, table_ref = rest[-2:]
    for side in range(2):
        table_ref[side] = jnp.zeros(table_ref.shape[1:], F32)

    def one(number, carry):
        here = pl.ds(pl.multiple_of(number * block_rows, 16), block_rows)
        queries = halves(q_ref[here, :])
        keys = halves(k_ref[here, :])
        grads = halves(grad_ref[here, :])
        values = v_ref[here, :]
        dq = dk = dv = 0.0
        for side in range(2):
            weights = weight_ref[side, number]
            up = nt(grads[side], values)
            inner = jnp.sum(weights * up, axis=1, keepdims=True)
            score = (weights * (up - inner)).astype(BF16)
            dv += tn(weights.astype(BF16), grads[side])
            dq += nn(score, keys[side])
            dk += tn(score, queries[side])
            table_ref[side, :, :block_rows] += score.astype(F32)
        packed_ref[0, here, :] = (dq * scale).astype(BF16)
        packed_ref[1, here, :] = dk.astype(BF16)
        packed_ref[2, here, :] = dv.astype(BF16)
        return carry

    lax.fori_loop(0, IMGS, one, 0, unroll=True)


def attend_back(packed, weights, mixed_grad, head_dim, lanes, first, last, earlier=()):
    rows, three = packed.shape
    pairs = three // (3 * 128)
    heads, _, block_rows, _ = weights.shape
    part = pl.BlockSpec((rows, 128), lambda p: (0, first + p))
    return pl.pallas_call(
        functools.partial(attend_back_body, block_rows, head_dim**-0.5),
        grid=(last - first,),
        in_specs=[
            part,
            pl.BlockSpec((rows, 128), lambda p: (0, pairs + first + p)),
            pl.BlockSpec((rows, 128), lambda p: (0, 2 * pairs + first + p)),
            pl.BlockSpec((2, IMGS, block_rows, block_rows), lambda p: (first + p, 0, 0, 0)),
            part,
        ]
        + [pl.BlockSpec(memory_space=pl.ANY)] * len(earlier),
        out_specs=[
            pl.BlockSpec((3, rows, 128), lambda p: (0, 0, first + p)),
            pl.BlockSpec((2, block_rows, lanes), lambda p: (first + p, 0, 0)),
        ],
        out_shape=[
            jax.ShapeDtypeStruct((3, rows, pairs * 128), BF16),
            jax.ShapeDtypeStruct((heads, block_rows, lanes), F32),
        ],
        input_output_aliases={5: 0, 6: 1} if earlier else {},
        compiler_params=params(),
        cost_estimate=cost(4),
        name="attend_back",
    )(packed, packed, packed, weights, mixed_grad, *earlier)


def cumulative(values):
    squared = jnp.exp(-0.5 * values * values)
    size = jnp.abs(values) * ROOT_HALF
    t = 1.0 / (1.0 + 0.3275911 * size)
    poly = t * (
        0.254829592 + t * (-0.284496736 + t * (1.421413741 + t * (-1.453152027 + t * 1.061405429)))
    )
    tail = 0.5 * poly * squared
    return jnp.where(values < 0, tail, 1.0 - tail), squared * INV_ROOT_TAU


def normal(values):
    average = jnp.mean(values, axis=-1, keepdims=True)
    centred = values - average
    inverse = lax.rsqrt(jnp.mean(centred * centred, axis=-1, keepdims=True) + EPS)
    return centred * inverse, inverse


def column_sum(ref, row, values):
    ref[row : row + 1, :] = jnp.sum(values, axis=0, keepdims=True)


def add_column_sum(ref, row, values):
    ref[row : row + 1, :] += jnp.sum(values, axis=0, keepdims=True)


class Late:
    def __init__(self, sources, targets, sems):
        self.copies = [
            pltpu.make_async_copy(source, target, sems.at[number])
            for number, (source, target) in enumerate(zip(sources, targets, strict=True))
        ]

    def start(self):
        for copy in self.copies:
            copy.start()

    def wait(self):
        for copy in self.copies:
            copy.wait()


def feed_body(
    image,
    block_rows,
    info,
    order_ref,
    mixed_ref,
    xb_ref,
    up_ref,
    up_t_ref,
    vec_ref,
    bias_ref,
    out_w_ref,
    fc1_ref,
    fc2_ref,
    cb_any,
    out_ref,
    keep_ref,
    send_ref,
    fc1_sum_ref,
    mixed_grad_ref,
    after_grad_ref,
    sums_ref,
    ff_s,
    second_s,
    cb_s,
    after_s,
    branch_s,
    low_s,
    turned_s,
    sems,
):
    step = pl.program_id(0)
    last = pl.num_programs(0) - 1
    rows, width = xb_ref.shape
    late = Late((cb_any,), (cb_s,), sems)

    half = keep_ref.shape[1]
    side = width // 2

    def put_out_grad(here):
        there = pl.ds(pl.multiple_of(half + here.start, 16), here.size)
        for ref, rows_here in ((keep_ref, here), (send_ref, there)):
            values = nn(turned_s[rows_here, :], mixed_ref[...]).astype(BF16)
            ref[0, here, :side] = values[:, :side]
            ref[1, here, :side] = values[:, side:]

    def turn_low():
        def turned(here):
            order = row_order(order_ref[here, :], width)
            turned_s[here, :] = nt(order, low_s[...]).astype(BF16)

        in_chunks(width, width // 2, turned)

    @pl.when(step == 0)
    def _():
        late.start()
        ff_s[...] = jnp.zeros_like(ff_s)
        second_s[...] = jnp.zeros_like(second_s)

        def one(here):
            branch = nt(mixed_ref[here, :], out_w_ref[...]) + vec_ref[OUT_B : OUT_B + 1, :]
            branch_s[here, :] = branch
            after_attn = xb_ref[here, :].astype(F32) + vec_ref[GAM_A : GAM_A + 1, :] * branch
            after_s[here, :] = after_attn
            normed, _ = normal(after_attn)
            low_s[here, :] = (
                normed * vec_ref[LN2_G : LN2_G + 1, :] + vec_ref[LN2_B : LN2_B + 1, :]
            ).astype(BF16)

        in_chunks(rows, rows // 2, one)
        turn_low()

    @pl.when(step < last)
    def _():
        pre = nn(low_s[...], fc1_ref[...]) + bias_ref[0:1, :]
        phi, density = cumulative(pre)
        hidden = (pre * phi).astype(BF16)
        slope = phi + pre * density
        grad = (nn(up_ref[...], fc2_ref[...]) * slope).astype(BF16)
        ff_s[...] += nt(hidden, fc2_ref[...])
        second_s[...] += nt(grad, fc1_ref[...])
        for plane, values in enumerate((nn(turned_s[...], grad), nn(up_t_ref[...], hidden))):
            keep_ref[plane] = values[:half].astype(BF16)
            send_ref[plane] = values[half:].astype(BF16)
        fc1_sum_ref[...] = jnp.broadcast_to(
            jnp.sum(grad.astype(F32), axis=0, keepdims=True), fc1_sum_ref.shape
        )

    @pl.when(step == last)
    def _():
        late.wait()
        sums_ref[...] = jnp.zeros_like(sums_ref)

        def finish(here):
            cot = cb_s[here, :].astype(F32)
            normed, inverse = normal(after_s[here, :])
            second = second_s[here, :]
            add_column_sum(sums_ref, G_LN2_G, second * normed)
            add_column_sum(sums_ref, G_LN2_B, second)
            scaled = second * vec_ref[LN2_G : LN2_G + 1, :]
            inner = jnp.mean(scaled, axis=-1, keepdims=True)
            along = jnp.mean(scaled * normed, axis=-1, keepdims=True)
            after_grad = cot + inverse * (scaled - inner - normed * along)
            after_grad_ref[here, :] = after_grad
            add_column_sum(sums_ref, G_GAM_A, after_grad * branch_s[here, :])
            low = (vec_ref[GAM_A : GAM_A + 1, :] * after_grad).astype(BF16)
            low_s[here, :] = low
            add_column_sum(sums_ref, G_OUT_B, low.astype(F32))
            mixed_grad_ref[here, :] = nn(low, out_w_ref[...]).astype(BF16)
            branch = ff_s[here, :] + vec_ref[FC2_B : FC2_B + 1, :]
            add_column_sum(sums_ref, G_GAM_M, cot * branch)
            add_column_sum(sums_ref, G_FC2_B, up_ref[here, :].astype(F32))
            out_ref[here, :] = (after_s[here, :] + vec_ref[GAM_M : GAM_M + 1, :] * branch).astype(BF16)

        in_chunks(rows, rows // 4, finish)
        turn_low()
        in_chunks(half, half // 2, put_out_grad)


def feed(
    info,
    order,
    mixed,
    xb,
    up,
    up_t,
    vec,
    fc1b,
    weights,
    cb,
    image,
    block_rows,
    length,
    tile,
):
    rows, width = xb.shape
    hidden = fc1b.shape[1]
    steps = hidden // tile
    anywhere = pl.BlockSpec(memory_space=pl.ANY)
    once = pl.Buffered(1)

    def at(i):
        return jnp.minimum(i, steps - 1)

    def fixed(shape):
        return pl.BlockSpec(shape, lambda i: (0, 0), pipeline_mode=once)

    return pl.pallas_call(
        functools.partial(feed_body, image, block_rows),
        grid=(steps + 1,),
        in_specs=[
            smem(),
            fixed((width, 1)),
            fixed((rows, width)),
            fixed((rows, width)),
            fixed((rows, width)),
            fixed((width, rows)),
            fixed(vec.shape),
            pl.BlockSpec((8, tile), lambda i: (0, at(i))),
            pl.BlockSpec((width, width), lambda i: (0, 2 * hidden // width), pipeline_mode=once),
            pl.BlockSpec((width, tile), lambda i: (0, at(i))),
            pl.BlockSpec((width, tile), lambda i: (0, steps + at(i))),
        ]
        + [anywhere],
        out_specs=[
            full((rows, width)),
            pl.BlockSpec((2, width // 2, tile), lambda i: (0, 0, i)),
            pl.BlockSpec((2, width // 2, tile), lambda i: (0, 0, i)),
            pl.BlockSpec((8, tile), lambda i: (0, at(i))),
            full((rows, width)),
            full((rows, width)),
            full((16, width)),
        ],
        out_shape=[
            jax.ShapeDtypeStruct((rows, width), BF16),
            jax.ShapeDtypeStruct((2, width // 2, hidden + width // 2), BF16),
            jax.ShapeDtypeStruct((2, width // 2, hidden + width // 2), BF16),
            jax.ShapeDtypeStruct((8, hidden), F32),
            jax.ShapeDtypeStruct((rows, width), BF16),
            jax.ShapeDtypeStruct((rows, width), F32),
            jax.ShapeDtypeStruct((16, width), F32),
        ],
        scratch_shapes=[
            pltpu.VMEM((rows, width), F32),
            pltpu.VMEM((rows, width), F32),
            pltpu.VMEM((rows, width), BF16),
            pltpu.VMEM((rows, width), F32),
            pltpu.VMEM((rows, width), F32),
            pltpu.VMEM((rows, width), BF16),
            pltpu.VMEM((width, rows), BF16),
            pltpu.SemaphoreType.DMA((1,)),
        ],
        compiler_params=params(),
        cost_estimate=cost(28),
        name="feed",
    )(
        info,
        order,
        mixed,
        xb,
        up,
        up_t,
        vec,
        fc1b,
        weights,
        weights,
        weights,
        cb,
    )


def weight_grad_body(low_t_ref, packed_ref, keep_ref, send_ref):
    half = keep_ref.shape[0]
    keep_ref[...] = nn(low_t_ref[:half], packed_ref[...]).astype(BF16)
    send_ref[...] = nn(low_t_ref[half:], packed_ref[...]).astype(BF16)


def weight_grad(low_t, packed_grad):
    width, rows = low_t.shape
    return pl.pallas_call(
        weight_grad_body,
        grid=(3,),
        in_specs=[full((width, rows)), pl.BlockSpec((None, rows, width), lambda i: (i, 0, 0))],
        out_specs=[pl.BlockSpec((width // 2, width), lambda i: (0, i))] * 2,
        out_shape=[jax.ShapeDtypeStruct((width // 2, 3 * width), BF16)] * 2,
        compiler_params=params(),
        cost_estimate=cost(5),
        name="weight_grad",
    )(low_t, packed_grad)


def input_grad_body(
    image,
    block_rows,
    info,
    packed_ref,
    weight_ref,
    vec_ref,
    normed_any,
    inv_any,
    after_grad_any,
    out_ref,
    sums_ref,
    first_s,
    normed_s,
    inv_s,
    after_grad_s,
    sems,
):
    step = pl.program_id(0)
    late = Late((normed_any, inv_any, after_grad_any), (normed_s, inv_s, after_grad_s), sems)

    @pl.when(step == 0)
    def _():
        late.start()
        first_s[...] = jnp.zeros_like(first_s)
        sums_ref[...] = jnp.zeros_like(sums_ref)
        column_sum(sums_ref, G_Q_B, packed_ref[...].astype(F32))

    def one(here):
        first_s[here, :] += nt(packed_ref[here, :], weight_ref[...])

    in_chunks(first_s.shape[0], first_s.shape[0] // 2, one)

    @pl.when(step == 2)
    def _():
        late.wait()
        column_sum(sums_ref, G_V_B, packed_ref[...].astype(F32))

        def finish(here):
            first = first_s[here, :]
            normed = normed_s[here, :]
            add_column_sum(sums_ref, G_LN1_G, first * normed)
            add_column_sum(sums_ref, G_LN1_B, first)
            scaled = first * vec_ref[LN1_G : LN1_G + 1, :]
            inner = jnp.mean(scaled, axis=-1, keepdims=True)
            along = jnp.mean(scaled * normed, axis=-1, keepdims=True)
            back = inv_s[here, :1] * (scaled - inner - normed * along)
            out_ref[here, :] = (after_grad_s[here, :] + back).astype(BF16)

        in_chunks(first_s.shape[0], first_s.shape[0] // 4, finish)


def input_grad(info, packed_grad, weights, vec, normed, inv, after_grad, image, block_rows, length):
    rows, width = normed.shape
    anywhere = pl.BlockSpec(memory_space=pl.ANY)
    return pl.pallas_call(
        functools.partial(input_grad_body, image, block_rows),
        grid=(3,),
        in_specs=[
            smem(),
            pl.BlockSpec((None, rows, width), lambda i: (i, 0, 0)),
            pl.BlockSpec((width, width), lambda i: (0, i)),
            full(vec.shape),
            anywhere,
            anywhere,
            anywhere,
        ],
        out_specs=[full((rows, width)), full((16, width))],
        out_shape=[
            jax.ShapeDtypeStruct((rows, width), BF16),
            jax.ShapeDtypeStruct((16, width), F32),
        ],
        scratch_shapes=[
            pltpu.VMEM((rows, width), F32),
            pltpu.VMEM((rows, width), F32),
            pltpu.VMEM((rows, 128), F32),
            pltpu.VMEM((rows, width), F32),
            pltpu.SemaphoreType.DMA((3,)),
        ],
        compiler_params=params(),
        cost_estimate=cost(8),
        name="input_grad",
    )(info, packed_grad, weights, vec, normed, inv, after_grad)


def table_grad_body(heads, groups, table_ref, index_ref, out_ref, acc):
    lanes = index_ref.shape[1]
    parts = out_ref.shape[1] // 128
    acc[...] = jnp.zeros_like(acc)
    slots = lax.broadcasted_iota(jnp.int32, (128, lanes), 0).astype(F32).astype(BF16)
    one_bf, zero_bf = jnp.ones((), BF16), jnp.zeros((), BF16)
    zero = jnp.zeros((), BF16)
    group = 8

    def one(step, carry):
        at = pl.ds(pl.multiple_of(step * group, group), group)
        indices = index_ref[at, :]
        lows = jnp.bitwise_and(indices, 127).astype(F32)
        highs = jnp.right_shift(indices, 7).astype(F32)
        values = table_ref[:, at, :]
        left, right = [], []
        for row in range(group):
            low = jnp.broadcast_to(lows[row : row + 1, :], (16, lanes)).astype(BF16)
            high = jnp.broadcast_to(highs[row : row + 1, :], (16, lanes)).astype(BF16)
            right.append(
                jnp.concatenate(
                    [
                        jnp.where(slots[start : start + 16] == low, one_bf, zero_bf)
                        for start in range(0, 128, 16)
                    ],
                    axis=0,
                )
            )
            here = jnp.concatenate(
                [values[:, row, :], jnp.zeros((16 - heads, lanes), F32)], axis=0
            )
            coarse = here.astype(BF16)
            fine = (here - coarse.astype(F32)).astype(BF16)
            masks = [high == jnp.asarray(part, BF16) for part in range(parts)]
            left.append(
                jnp.concatenate(
                    [jnp.where(mask, kind, zero) for kind in (coarse, fine) for mask in masks],
                    axis=0,
                )
            )
        acc[...] += nt(jnp.concatenate(left, axis=1), jnp.concatenate(right, axis=1))
        return carry

    lax.fori_loop(groups[0], groups[1], one, 0)
    half = parts * 16
    for part in range(parts):
        out_ref[:, part * 128 : (part + 1) * 128] = (
            acc[part * 16 : (part + 1) * 16, :] + acc[half + part * 16 : half + (part + 1) * 16, :]
        )


def table_grad(table, index, slots, groups):
    heads, length, lanes = table.shape
    return pl.pallas_call(
        functools.partial(table_grad_body, heads, groups),
        grid=(1,),
        in_specs=[full(table.shape), full(index.shape)],
        out_specs=full((16, slots)),
        out_shape=jax.ShapeDtypeStruct((16, slots), F32),
        scratch_shapes=[pltpu.VMEM((2 * 16 * slots // 128, 128), F32)],
        compiler_params=params(),
        cost_estimate=cost(8),
        name="table_grad",
    )(table, index)


def local(
    inputs,
    cotangent,
    segment_ids,
    keep_rows,
    index_map,
    ln1_gain,
    ln1_bias,
    qkv_weight,
    qv_bias,
    out_weight,
    out_bias,
    gamma_attn,
    rel_table,
    ln2_gain,
    ln2_bias,
    fc1_weight,
    fc1_bias,
    fc2_weight,
    fc2_bias,
    gamma_mlp,
):
    _, length, width = inputs.shape
    heads, per_device = rel_table.shape
    head_dim = width // heads
    own = ln1_gain.shape[0]
    count = width // own
    hidden = fc1_weight.shape[1]
    image = index_map.shape[0]
    block_rows = -(-image // 16) * 16

    keep = keep_rows[0] == 1
    ids = lax.iota(jnp.int32, length)
    info = jnp.stack([jnp.min(jnp.where(keep, ids, length)), jnp.max(jnp.where(keep, 0, 1))])
    moved = index_map // per_device * own + index_map % per_device
    moved = jnp.pad(moved, ((0, block_rows - image), (0, 256 - image)), constant_values=-1)

    small_rows = [
        ln1_gain[None],
        ln1_bias[None],
        qv_bias,
        out_bias[None],
        gamma_attn[None],
        ln2_gain[None],
        ln2_bias[None],
        fc2_bias[None],
        gamma_mlp[None],
    ]
    owners = exchange_owners(count, 0)

    def row_places(owning):
        return (owning[:, None] * own + jnp.arange(own, dtype=jnp.int32)).reshape(-1, 1)

    order, qkv_order = row_places(owners), row_places(exchange_owners(count, 1))
    later = lax.all_gather(
        jnp.concatenate([fc1_weight, fc2_weight.T, out_weight.T], axis=1), AX, axis=0, tiled=True
    )
    xb, cb, normed, inv = prepare(info, inputs[0], cotangent[0], image, block_rows)
    small = pack(small_rows, fc1_bias[None], rel_table, FC1_B, TABLE, hidden // width)
    small = jnp.broadcast_to(after(small, xb)[None], (count, own, SMALL))
    small = lax.all_to_all(small, AX, 0, 0, tiled=True).reshape(width, SMALL)
    vec, fc1b, table = expand(small, moved, heads, hidden)
    mine, got = gather_halves(qkv_weight, count, [(xb,), (small,), (table,)])
    packed, low, qkv_full = project(owners, normed, vec, mine, got, head_dim)
    qkv_full = qkv_full.reshape(width, -1)
    mixed, weights = attend(info, packed, table, block_rows)
    up, up_t, low_t = turn(order, qkv_order, vec, after(cb, mixed), low)
    tile = 1024
    out, feed_keep, feed_send, fc1_sum, mixed_grad, after_grad, sums2 = feed(
        info,
        order,
        mixed,
        xb,
        up,
        up_t,
        vec,
        fc1b,
        later,
        cb,
        image,
        block_rows,
        length,
        tile,
    )
    pairs = heads // 2
    some = attend_back(packed, weights, mixed_grad, head_dim, 256, 0, pairs // 2)
    a_pieces, a_send = scatter_step(0, [feed_keep], feed_send, 0, count, some[0])
    packed_grad, table_sum = attend_back(
        packed, weights, after(mixed_grad, a_send), head_dim, 256, pairs // 2, pairs, some
    )
    qkv_keep, qkv_send = weight_grad(low_t, packed_grad)
    biases = after(fc1_sum, qkv_keep)[0].reshape(count, -1, own)
    b_pieces, b_send = scatter_step(1, [qkv_keep], qkv_send, 0, count, biases)
    in_grad, sums1 = input_grad(
        info,
        packed_grad,
        qkv_full,
        vec,
        normed,
        after(inv, b_send),
        after_grad,
        image,
        block_rows,
        length,
    )
    groups = -(-image // 8)
    slots = own * count
    a_pieces, a_send = scatter_step(0, a_pieces, a_send, 1, count, in_grad)
    slot_sums = table_grad(after(table_sum, a_send), moved, slots, (0, groups // 2))
    b_pieces, b_send = scatter_step(1, b_pieces, b_send, 1, count, slot_sums)
    more_sums = table_grad(after(table_sum, b_send), moved, slots, (groups // 2, groups))
    a_pieces, a_send = scatter_step(0, a_pieces, a_send, 2, count, more_sums)
    b_pieces, b_send = scatter_step(1, b_pieces, b_send, 2, count, a_send)
    slot_sums = slot_sums + after(more_sums, b_send)

    rows = jnp.concatenate([sums1[:10] + sums2[:10], slot_sums[:heads]], axis=0)
    rows = jnp.transpose(rows.reshape(-1, count, own), (1, 0, 2))
    swapped = lax.all_to_all(jnp.concatenate([rows, biases], axis=1), AX, 0, 0, tiled=True)
    out, in_grad = restore(
        info, image, block_rows, length, after(out, b_send), in_grad
    )
    swapped = after(swapped, out)
    a_pieces, a_send = scatter_step(0, a_pieces, a_send, 3, count, swapped)
    b_pieces, b_send = scatter_step(1, b_pieces, b_send, 3, count, a_send)
    late_send = b_send
    for step in range(4, count.bit_length() - 1):
        a_pieces, a_send = scatter_step(0, a_pieces, a_send, step, count, b_send)
    for step in range(4, count.bit_length() - 1):
        b_pieces, b_send = scatter_step(1, b_pieces, b_send, step, count, a_pieces)
    feed_wide, qkv_shard = a_pieces, b_pieces
    small_shard = jnp.sum(after(swapped, late_send), axis=0)

    grad_fc1 = feed_wide[0, :, :hidden]
    grad_fc2 = feed_wide[1, :, :hidden].T
    grad_out = jnp.concatenate([feed_wide[0, :, hidden:], feed_wide[1, :, hidden:]], axis=1).T
    grad_table = small_shard[10 : 10 + heads, :per_device]
    grad_fc1_bias = small_shard[10 + heads :].reshape(-1)
    return (
        out[None],
        in_grad[None],
        small_shard[G_LN1_G],
        small_shard[G_LN1_B],
        qkv_shard,
        small_shard[G_Q_B : G_V_B + 1],
        grad_out,
        small_shard[G_OUT_B],
        small_shard[G_GAM_A],
        grad_table,
        small_shard[G_LN2_G],
        small_shard[G_LN2_B],
        grad_fc1,
        grad_fc1_bias,
        grad_fc2,
        small_shard[G_FC2_B],
        small_shard[G_GAM_M],
    )


def solution(mesh):
    rows = P(AX)
    columns = P(None, AX)
    return jax.shard_map(
        local,
        mesh=mesh,
        in_specs=(
            rows,
            rows,
            rows,
            rows,
            P(),
            rows,
            rows,
            rows,
            columns,
            columns,
            rows,
            rows,
            columns,
            rows,
            rows,
            rows,
            rows,
            columns,
            rows,
            rows,
        ),
        out_specs=(
            rows,
            rows,
            rows,
            rows,
            rows,
            columns,
            columns,
            rows,
            rows,
            columns,
            rows,
            rows,
            rows,
            rows,
            columns,
            rows,
            rows,
        ),
        check_vma=False,
    )
```
